32 devices in a mesh: curve: 8 (over z, y), band: 4 (over x, core).
Axes of the slice: x: 2, y: 2, z: 4, core: 2. Of those that a mesh axis runs over, the one named last changes fastest.
Arguments:
- state: float32 [16, 2048, 128], P('band', 'curve'), may hold values from -3 to 3
- blocks: bfloat16 [2048, 4, 128, 128], P('curve', 'band'), may hold values from -0.25 to 0.25
- diag_blocks: bfloat16 [2048, 128, 128], P(('curve', 'band')), may hold values from -1 to 1, as said below
- block_cols: int32 [2048, 4], P('curve', 'band'), may hold values from 0 to 2047, as said below
Outputs:
- updated: float32 [16, 2048, 128], P('band', 'curve')
The draws below stay inside these ranges and needn't reach their ends.
Inputs may be any that keep to these rules, and one draw needn't show every extreme that they name: `diag_blocks`: every diagonal block is symmetric. `block_cols`: A column is never the row's own patch, and no pair of patches is stored twice, in either order. The owner of patch p is index p // 256 of curve. Of the 256 rows of one index of curve, in each slot exactly 8 have their column on another index: 2 on each of 4 other indices; the columns of the others lie on the own index.
All inputs are finite; a program needn't handle non-finite values.
Results may differ from the reference program's by a relative error of at most 0.0003.
The reference program's roundings to bfloat16 on the way count: a program that leaves them out, or rounds other values in their place, can miss the bound.
Values may be sent and summed in bfloat16 or wider, within the bound.
No kernel may reach another device: no remote copies, remote signals or barrier semaphores. Data moves between devices by JAX's collectives and lax.ppermute only.
A program may use at most 64 MiB of HBM per device.

```python
import jax
import jax.numpy as jnp
from jax import lax

BS = 128
NV = 16
P_DEV = 256
CAP = 2
TAYLOR = 16
SLOTS = 4
PATCHES = 2048
REMOTE = 8


def draw_state(key, part):
    key_base, key_rows, key_cols = jax.random.split(key, 3)
    patch_index = jnp.arange(PATCHES, dtype=jnp.float32)
    ramp = (1.0 + 2.0 * patch_index / (PATCHES - 1.0)) / 3.0
    row_scale = 10.0 ** jax.random.uniform(key_rows, (PATCHES,), minval=-1.0, maxval=0.0)
    col_scale = 10.0 ** jax.random.uniform(key_cols, (NV,), minval=-0.92, maxval=0.08)
    base = jnp.clip(jax.random.normal(key_base, (NV, PATCHES, BS)), -2.5, 2.5)
    return base * col_scale[:, None, None] * (row_scale * ramp)[None, :, None]


def draw_diag_blocks(key, part):
    raw = jax.random.normal(key, (PATCHES, BS, BS))
    symmetric = (raw + jnp.swapaxes(raw, 1, 2)) * 0.5 ** 0.5 / (5.0 * BS) ** 0.5
    identity = jnp.eye(BS, dtype=jnp.float32)
    return (symmetric - 0.3 * identity[None, :, :]).astype(jnp.bfloat16)


def column_list(key, device, slot_id):
    devices = PATCHES // P_DEV
    mixed = jax.random.fold_in(jax.random.fold_in(jax.random.fold_in(key, 7331), device), slot_id)
    key_order, key_peer, key_gap = jax.random.split(mixed, 3)
    order = jax.random.permutation(key_order, P_DEV)
    place = jnp.zeros((P_DEV,), jnp.int32).at[order].set(jnp.arange(P_DEV, dtype=jnp.int32))
    offsets = 1 + jax.random.permutation(key_peer, devices - 1)
    group_index = jnp.minimum(place // CAP, devices // 2 - 1)
    device_shift = jnp.where(place < REMOTE, offsets[group_index], 0)
    range_width = P_DEV // (2 * SLOTS)
    gap = 1 + slot_id * range_width + jax.random.randint(key_gap, (P_DEV,), 0, range_width - 1)
    row_index = jnp.arange(P_DEV, dtype=jnp.int32)
    return (device + device_shift) % devices * P_DEV + (row_index + gap) % P_DEV


def draw_block_cols(key, part):
    devices = PATCHES // P_DEV
    device_ids = jnp.arange(devices, dtype=jnp.int32)
    slot_ids = jnp.arange(SLOTS, dtype=jnp.int32)
    table = jax.vmap(lambda device: jax.vmap(lambda slot_id: column_list(key, device, slot_id))(slot_ids))(device_ids)
    return jnp.transpose(table, (0, 2, 1)).reshape(PATCHES, SLOTS).astype(jnp.int32)


def levels(stream_key, dims, pieces, least, largest):
    def one(position, parts):
        heights = jax.random.uniform(jax.random.fold_in(jax.random.fold_in(stream_key, 6), position), (parts,), jnp.float32, least / len(pieces), largest / len(pieces))
        return jnp.repeat(jnp.exp(heights), dims[position] // parts).reshape((-1,) + (1,) * (len(dims) - position - 1))

    gain = one(*pieces[0])
    for cut in pieces[1:]:
        gain = gain * one(*cut)
    return gain


def bell_draw(own_key, extent, spread, most, pieces=(), kind=jnp.bfloat16):
    factor_of = levels(own_key, extent, pieces, -0.22, 0.18) if pieces else 1.0
    entries = jax.random.normal(own_key, extent, jnp.float32) * spread * factor_of
    return jnp.minimum(jnp.maximum(entries, -most), most).astype(kind)


def setup_inputs(seed: int = 0) -> dict:
    seeds = jax.random.split(jax.random.key(seed), 5)
    return {
        "state": draw_state(jax.random.fold_in(seeds[4], 71), 0),
        "blocks": bell_draw(seeds[1], (PATCHES, SLOTS, BS, BS), (5 * BS) ** -0.5, 0.25, ((0, 8), (1, 4))),
        "diag_blocks": draw_diag_blocks(jax.random.fold_in(seeds[4], 71), 0),
        "block_cols": draw_block_cols(jax.random.fold_in(seeds[4], 71), 0),
    }


epsilon = 1e-06
time_step = 0.5
quadratic = 1.0

def nonlinear(field):
    return quadratic * field * field - field * field * field

def phi_weights(alpha_first, beta_first, alpha_second):

    def advance(turn, carry):
        term_one, term_two, total_one, total_two = carry
        factor = time_step / (turn + 1.0)
        next_one = factor * (alpha_first * term_one + beta_first * term_two)
        next_two = factor * (beta_first * term_one + alpha_second * term_two)
        return (next_one, next_two, total_one + next_one, total_two + next_two)
    ones = jnp.ones_like(alpha_first)
    zeros = jnp.zeros_like(alpha_first)
    result = lax.fori_loop(1, TAYLOR, advance, (ones, zeros, ones, zeros))
    return (result[2], result[3])

def apply_operator(vector, blocks, diag_blocks, block_cols):
    vectors, patches, node_count = vector.shape
    slot_count = blocks.shape[1]
    group = P_DEV
    count = patches // group
    columns = block_cols.reshape(-1)
    column_field = vector[:, columns, :].reshape(vectors, count, group, slot_count, node_count)
    column_field = jnp.transpose(column_field, (1, 0, 2, 3, 4))
    row_field = jnp.transpose(vector.reshape(vectors, count, group, node_count), (1, 0, 2, 3))
    stored = blocks.reshape(count, group, slot_count, node_count, node_count)
    diagonal = diag_blocks.reshape(count, group, node_count, node_count)

    def piece(operands):
        stored_part, diagonal_part, row_part, column_part = operands
        stored_part = stored_part.astype(jnp.float32)
        diagonal_part = diagonal_part.astype(jnp.float32)
        row_part = row_part.astype(jnp.float32)
        column_part = column_part.astype(jnp.float32)
        forward = jnp.einsum('rbac,vrbc->vra', stored_part, column_part)
        forward = forward + jnp.einsum('rac,vrc->vra', diagonal_part, row_part)
        mirrored = jnp.einsum('rbac,vra->vrbc', stored_part, row_part)
        return (forward, mirrored)
    forward, mirrored = lax.map(piece, (stored, diagonal, row_field, column_field))
    forward = jnp.transpose(forward, (1, 0, 2, 3)).reshape(vectors, patches, node_count)
    mirrored = jnp.transpose(mirrored, (1, 0, 2, 3, 4)).reshape(vectors, patches * slot_count, node_count)
    return forward.at[:, columns, :].add(mirrored)

def reference(state, blocks, diag_blocks, block_cols):
    linear = apply_operator(state.astype(jnp.bfloat16), blocks, diag_blocks, block_cols)
    drive = linear + nonlinear(state)
    beta_zero = jnp.sqrt(lax.optimization_barrier(jnp.sum(drive * drive, axis=(1, 2))) + epsilon)
    first = drive / beta_zero[:, None, None]
    image = apply_operator(first.astype(jnp.bfloat16), blocks, diag_blocks, block_cols)
    alpha_first = lax.optimization_barrier(jnp.sum(first * image, axis=(1, 2)))
    rest = image - alpha_first[:, None, None] * first
    beta_first = jnp.sqrt(lax.optimization_barrier(jnp.sum(rest * rest, axis=(1, 2))) + epsilon)
    second = rest / beta_first[:, None, None]
    image_second = apply_operator(second.astype(jnp.bfloat16), blocks, diag_blocks, block_cols)
    image_second = image_second - beta_first[:, None, None] * first
    alpha_second = lax.optimization_barrier(jnp.sum(second * image_second, axis=(1, 2)))
    weight_one, weight_two = phi_weights(alpha_first, beta_first, alpha_second)
    combined = weight_one[:, None, None] * first + weight_two[:, None, None] * second
    return state + time_step * beta_zero[:, None, None] * combined
```

```python
import functools

import jax
import jax.numpy as jnp
from jax import lax
from jax.experimental import pallas as pl
from jax.experimental.pallas import tpu as pltpu
from jax.sharding import PartitionSpec as P

CAP = 2
TAYLOR = 16
UNROLL = 8
STEPS = 8

epsilon = 1e-06
time_step = 0.5
quadratic = 1.0
STEP = 256.0
FULL = 32767.0

f32 = jnp.float32
bf16 = jnp.bfloat16
i32 = jnp.int32


def nonlinear(field):
    return quadratic * field * field - field * field * field


def tile(index, rows):
    return pl.ds(pl.multiple_of(index * rows, rows), rows)


def smem():
    return pl.BlockSpec(memory_space=pltpu.SMEM)


def vmem():
    return pl.BlockSpec(memory_space=pltpu.VMEM)


def times(field, block):
    return lax.dot_general(field, block, (((1,), (0,)), ((), ())), preferred_element_type=f32)


def times_transposed(field, block):
    return lax.dot_general(field, block, (((1,), (1,)), ((), ())), preferred_element_type=f32)


def row_sum(part):
    return jnp.sum(part, axis=1, keepdims=True)


def plan_kernel(rows, groups, cols, where, pick, target, wanted, origin, count):
    here = where[0]

    def clear(peer, carry):
        count[peer] = 0
        return carry

    lax.fori_loop(0, groups, clear, 0)

    def empty(slot, carry):
        wanted[slot] = -1
        origin[slot] = 0
        return carry

    lax.fori_loop(0, groups * CAP, empty, 0)

    def visit(row, carry):
        column = cols[row]
        owner = column // rows
        inner = column - owner * rows
        pick[row] = inner
        target[row] = inner

        @pl.when(owner != here)
        def _():
            rank = count[owner]
            count[owner] = rank + 1
            slot = owner * CAP + rank
            wanted[slot] = inner
            origin[slot] = row
            pick[row] = rows + owner * (2 * CAP) + rank
            target[row] = rows

        return carry

    lax.fori_loop(0, rows, visit, 0)


def plan(cols, here):
    rows = cols.shape[0]
    groups = lax.axis_size("curve")
    slots = groups * CAP
    return pl.pallas_call(
        functools.partial(plan_kernel, rows, groups),
        out_shape=[jax.ShapeDtypeStruct((n,), i32) for n in (rows, rows, slots, slots)],
        in_specs=[smem(), smem()],
        out_specs=[smem()] * 4,
        scratch_shapes=[pltpu.SMEM((groups,), i32)],
        name="plan",
    )(cols, here)


def pick_blocks_kernel(slots, origin, blocks, out, sems):
    copies = [pltpu.make_async_copy(blocks.at[origin[k], 0], out.at[k], sems.at[k]) for k in range(slots)]
    for copy in copies:
        copy.start()
    for copy in copies:
        copy.wait()


def pick_blocks(origin, blocks):
    slots = origin.shape[0]
    node = blocks.shape[-1]
    return pl.pallas_call(
        functools.partial(pick_blocks_kernel, slots),
        out_shape=jax.ShapeDtypeStruct((slots, node, node), blocks.dtype),
        in_specs=[smem(), pl.BlockSpec(memory_space=pl.ANY)],
        out_specs=pl.BlockSpec(memory_space=pl.ANY),
        scratch_shapes=[pltpu.SemaphoreType.DMA((slots,))],
        name="pick_blocks",
    )(origin, blocks)


def spread_kernel(rows, vectors, groups, width, asked, origin, where, *refs):
    parts, (field, message, wide) = refs[: vectors // width], refs[vectors // width :]
    band = where[1]
    for k, part in enumerate(parts):
        start = jnp.bitwise_xor(band, k) * width
        for v in range(width):
            wide[pl.ds(start + v, rows, stride=vectors), :] = part[v].astype(f32)
    field[...] = wide[...].astype(bf16)

    def send(slot, carry):
        peer = slot // CAP
        rank = slot - peer * CAP
        place = peer * (2 * CAP) + rank
        message[tile(place, vectors), :] = field[tile(jnp.maximum(asked[slot], 0), vectors), :]
        message[tile(place + CAP, vectors), :] = field[tile(origin[slot], vectors), :]
        return carry

    lax.fori_loop(0, groups * CAP, send, 0)


def spread(parts, asked, origin, where):
    width, rows, node = parts[0].shape
    groups = lax.axis_size("curve")
    vectors = width * len(parts)
    return pl.pallas_call(
        functools.partial(spread_kernel, rows, vectors, groups, width),
        out_shape=[
            jax.ShapeDtypeStruct((rows * vectors, node), bf16),
            jax.ShapeDtypeStruct((groups * 2 * CAP * vectors, node), bf16),
        ],
        in_specs=[smem()] * 3 + [vmem()] * len(parts),
        out_specs=[vmem()] * 2,
        scratch_shapes=[pltpu.VMEM((rows * vectors, node), f32)],
        name="spread",
    )(asked, origin, where, *parts)


def block_products(rows, vectors, step, pick, target, band, field, blocks, diag, total):
    count = blocks.shape[0]
    base = step * count

    def some(chunk, carry):
        forward, mirrored, places = [], [], []
        for u in range(UNROLL):
            inner = chunk * UNROLL + u
            row = base + inner
            block = blocks[inner, 0]
            forward.append(times_transposed(field[tile(pick[row], vectors), :], block))
            mirrored.append(times(field[tile(row, vectors), :], block))
            places.append((row, target[row]))
        for (row, aim), one, two in zip(places, forward, mirrored):
            total[tile(row, vectors), :] += one
            total[tile(aim, vectors), :] += two
        return carry

    lax.fori_loop(0, count // UNROLL, some, 0)

    own = diag.shape[0]
    first = band * (own * pl.num_programs(0)) + step * own
    values = [times(field[tile(first + d, vectors), :], diag[d]) for d in range(own)]
    for d, value in enumerate(values):
        total[tile(first + d, vectors), :] += value


def received_products(rows, vectors, groups, asked, field, arrived, total):
    def some(peer, carry):
        values = []
        for k in range(CAP):
            slot = peer * CAP + k
            place = rows + peer * (2 * CAP) + CAP + k
            values.append((asked[slot], times(field[tile(place, vectors), :], arrived[slot])))
        for aim, value in values:
            total[tile(jnp.where(aim < 0, rows, aim), vectors), :] += value
        return carry

    lax.fori_loop(0, groups, some, 0)


def split_out(rows, vectors, band, total, keep, give):
    half = rows // 2
    core = jnp.bitwise_and(band, 1)
    size = half * vectors
    keep[...] = total[pl.ds(pl.multiple_of(core * size, size), size), :]
    give[...] = total[pl.ds(pl.multiple_of((1 - core) * size, size), size), :]


def first_kernel(rows, vectors, groups, pick, target, asked, where, gathered, halo, state, blocks, diag, arrived,
                 keep, give, field, total):
    step = pl.program_id(0)
    band = where[1]

    @pl.when(step == 0)
    def _():
        field[0 : rows * vectors, :] = gathered[...]
        field[rows * vectors :, :] = halo[...]
        total[...] = jnp.zeros_like(total)
        width = state.shape[0]
        for v in range(width):
            total[pl.ds(band * width + v, rows, stride=vectors), :] = nonlinear(state[v])

    block_products(rows, vectors, step, pick, target, band, field, blocks, diag, total)

    @pl.when(step == pl.num_programs(0) - 1)
    def _():
        received_products(rows, vectors, groups, asked, field, arrived, total)
        split_out(rows, vectors, band, total, keep, give)


def unpack(rows, vectors, groups, extra, band, mine, other, halo, convert):
    half = rows // 2
    core = jnp.bitwise_and(band, 1)
    size = half * vectors
    convert(pl.multiple_of(core * size, size), size, lambda ref: ref[0])
    convert(pl.multiple_of((1 - core) * size, size), size, lambda ref: ref[1])


def second_kernel(rows, vectors, groups, pick, target, asked, where, mine, other, halo, blocks, diag, arrived,
                  keep, give, scale, field, total):
    step = pl.program_id(0)
    band = where[1]
    half = rows // 2
    size = half * vectors
    stride = (2 * CAP + 1) * vectors

    @pl.when(step == 0)
    def _():
        energy = jnp.zeros((vectors, halo.shape[1]), f32)
        for g in range(groups):
            energy = energy + halo[g * stride + 2 * CAP * vectors : (g + 1) * stride, :]
        beta = jnp.sqrt(row_sum(energy) + epsilon)
        beta = jnp.broadcast_to(beta, energy.shape)
        scale[...] = beta
        inverse = 1.0 / beta
        core = jnp.bitwise_and(band, 1)

        def one(p, carry):
            field[tile(core * half + p, vectors), :] = (mine[tile(p, vectors), :] * inverse).astype(bf16)
            field[tile((1 - core) * half + p, vectors), :] = (other[tile(p, vectors), :] * inverse).astype(bf16)
            return carry

        lax.fori_loop(0, half, one, 0, unroll=8)

        def row(g, carry):
            for k in range(2 * CAP):
                value = halo[tile(g * (2 * CAP + 1) + k, vectors), :] * inverse
                field[tile(rows + g * (2 * CAP) + k, vectors), :] = value.astype(bf16)
            return carry

        lax.fori_loop(0, groups, row, 0)
        total[...] = jnp.zeros_like(total)

    block_products(rows, vectors, step, pick, target, band, field, blocks, diag, total)

    @pl.when(step == pl.num_programs(0) - 1)
    def _():
        received_products(rows, vectors, groups, asked, field, arrived, total)
        split_out(rows, vectors, band, total, keep, give)


def third_kernel(rows, vectors, groups, width, pick, where, scale, mine_d, other_d, halo_d, mine_i, other_i, halo_i,
                 blocks, diag, share, own_first, own_second, alpha_out, beta_out, field, wide, dots):
    step = pl.program_id(0)
    band = where[1]
    half = rows // 2
    node = scale.shape[1]
    shape = (vectors, node)
    stride = (2 * CAP + 2) * vectors

    @pl.when(step == 0)
    def _():
        alpha = jnp.zeros(shape, f32)
        energy = jnp.zeros(shape, f32)
        for g in range(groups):
            at = g * stride + 2 * CAP * vectors
            alpha = alpha + halo_i[at : at + vectors, :]
            energy = energy + halo_i[at + vectors : at + 2 * vectors, :]
        inverse = 1.0 / scale[...]
        alpha = jnp.broadcast_to(row_sum(alpha), shape) * inverse
        energy = jnp.broadcast_to(row_sum(energy), shape)
        beta = jnp.sqrt(jnp.maximum(energy - alpha * alpha, 0.0) + epsilon)
        alpha_out[...] = alpha
        beta_out[...] = beta
        over = 1.0 / beta
        core = jnp.bitwise_and(band, 1)

        def second_of(drive, image):
            return (image - alpha * (drive * inverse)) * over

        def one(p, carry):
            for place, drive, image in ((core * half + p, mine_d, mine_i), ((1 - core) * half + p, other_d, other_i)):
                value = second_of(drive[tile(p, vectors), :], image[tile(p, vectors), :])
                wide[tile(place, vectors), :] = value
                field[tile(place, vectors), :] = value.astype(bf16)
            return carry

        lax.fori_loop(0, half, one, 0, unroll=8)

        def row(g, carry):
            for k in range(2 * CAP):
                value = second_of(
                    halo_d[tile(g * (2 * CAP + 1) + k, vectors), :], halo_i[tile(g * (2 * CAP + 2) + k, vectors), :]
                )
                field[tile(rows + g * (2 * CAP) + k, vectors), :] = value.astype(bf16)
            return carry

        lax.fori_loop(0, groups, row, 0)
        dots[...] = jnp.zeros_like(dots)
        for v in range(width):
            at = band * width + v
            lift = inverse[0:1, :] * 0.0 + 1.0
            mine_row = mine_d[pl.ds(at, half, stride=vectors), :]
            other_row = other_d[pl.ds(at, half, stride=vectors), :]
            gain = jnp.broadcast_to(1.0 / scale[pl.ds(at, 1), :], mine_row.shape)
            own_first[v, pl.ds(pl.multiple_of(core * half, half), half), :] = mine_row * gain
            own_first[v, pl.ds(pl.multiple_of((1 - core) * half, half), half), :] = other_row * gain
            own_second[v] = wide[pl.ds(at, rows, stride=vectors), :]

    count = blocks.shape[0]
    base = step * count

    def some(chunk, carry):
        part = carry
        for u in range(UNROLL):
            inner = chunk * UNROLL + u
            row = base + inner
            value = times_transposed(field[tile(pick[row], vectors), :], blocks[inner, 0])
            part = part + value * field[tile(row, vectors), :].astype(f32)
        return part

    part = lax.fori_loop(0, count // UNROLL, some, jnp.zeros(shape, f32))
    own = diag.shape[0]
    first = band * (own * pl.num_programs(0)) + step * own
    core = jnp.bitwise_and(band, 1)
    gain = 1.0 / scale[...]
    beta = beta_out[...]
    acc = 2.0 * part
    for d in range(own):
        row = first + d
        value = times(field[tile(row, vectors), :], diag[d])
        acc = acc + value * field[tile(row, vectors), :].astype(f32)
        inside = row - (row // half) * half
        drive = jnp.where(
            row // half == core, mine_d[tile(inside, vectors), :], other_d[tile(inside, vectors), :]
        )
        acc = acc - (beta * wide[tile(row, vectors), :]) * (drive * gain)
    dots[...] += acc

    @pl.when(step == pl.num_programs(0) - 1)
    def _():
        across = lax.broadcasted_iota(i32, shape, 1)
        down = lax.broadcasted_iota(i32, shape, 0)
        column = jnp.broadcast_to(row_sum(dots[...]), shape)
        line = jnp.sum(jnp.where(across == down, column, 0.0), axis=0, keepdims=True)
        share[...] = jnp.broadcast_to(line, share.shape)


def block_specs(rows, node, diag_rows, steps):
    return [
        pl.BlockSpec((rows // steps, 1, node, node), lambda i: (i, 0, 0, 0)),
        pl.BlockSpec((diag_rows // steps, node, node), lambda i: (i, 0, 0)),
    ]


def apply_first(plans, gathered, halo, state, blocks, diag, arrived):
    pick, target, asked, where = plans
    rows, node = blocks.shape[0], blocks.shape[-1]
    vectors = gathered.shape[0] // rows
    groups = lax.axis_size("curve")
    half = jax.ShapeDtypeStruct((rows // 2 * vectors, node), f32)
    return pl.pallas_call(
        functools.partial(first_kernel, rows, vectors, groups),
        grid=(STEPS,),
        out_shape=[half, half],
        in_specs=[smem()] * 4 + [vmem()] * 3 + block_specs(rows, node, diag.shape[0], STEPS) + [vmem()],
        out_specs=[vmem()] * 2,
        scratch_shapes=[
            pltpu.VMEM(((rows + groups * 2 * CAP) * vectors, node), bf16),
            pltpu.VMEM(((rows + 1) * vectors, node), f32),
        ],
        name="operate_first",
    )(pick, target, asked, where, gathered, halo, state, blocks, diag, arrived)


def apply_second(plans, mine, other, halo, blocks, diag, arrived):
    pick, target, asked, where = plans
    rows, node = blocks.shape[0], blocks.shape[-1]
    groups = lax.axis_size("curve")
    vectors = halo.shape[0] // (groups * (2 * CAP + 1))
    half = jax.ShapeDtypeStruct((rows // 2 * vectors, node), f32)
    return pl.pallas_call(
        functools.partial(second_kernel, rows, vectors, groups),
        grid=(STEPS,),
        out_shape=[half, half, jax.ShapeDtypeStruct((vectors, node), f32)],
        in_specs=[smem()] * 4 + [vmem()] * 3 + block_specs(rows, node, diag.shape[0], STEPS) + [vmem()],
        out_specs=[vmem()] * 3,
        scratch_shapes=[
            pltpu.VMEM(((rows + groups * 2 * CAP) * vectors, node), bf16),
            pltpu.VMEM(((rows + 1) * vectors, node), f32),
        ],
        name="operate_second",
    )(pick, target, asked, where, mine, other, halo, blocks, diag, arrived)


def apply_third(plans, width, scale, drive, image, blocks, diag, devices):
    pick, target, asked, where = plans
    rows, node = blocks.shape[0], blocks.shape[-1]
    groups = lax.axis_size("curve")
    vectors = scale.shape[0]
    own = jax.ShapeDtypeStruct((width, rows, node), f32)
    one = jax.ShapeDtypeStruct((vectors, node), f32)
    return pl.pallas_call(
        functools.partial(third_kernel, rows, vectors, groups, width),
        grid=(STEPS,),
        out_shape=[jax.ShapeDtypeStruct((devices, node), f32), own, own, one, one],
        in_specs=[smem()] * 2 + [vmem()] * 7 + block_specs(rows, node, diag.shape[0], STEPS),
        out_specs=[vmem()] * 5,
        scratch_shapes=[
            pltpu.VMEM(((rows + groups * 2 * CAP) * vectors, node), bf16),
            pltpu.VMEM((rows * vectors, node), f32),
            pltpu.VMEM((vectors, node), f32),
        ],
        name="operate_third",
    )(pick, where, scale, *drive, *image, blocks, diag)


def encode_kernel(half, vectors, keep, came, code, wide):
    node = keep.shape[1]
    lanes = lax.broadcasted_iota(i32, (vectors, node), 1)
    for group in range(half // node):
        peak = jnp.zeros((vectors, node), f32)
        for p in range(node):
            at = (group * node + p) * vectors
            value = keep[at : at + vectors, :] + came[at : at + vectors, :]
            wide[at : at + vectors, :] = value
            peak = jnp.where(lanes == p, jnp.max(jnp.abs(value), axis=1, keepdims=True), peak)
        power = jnp.ceil(jnp.log2(jnp.maximum(peak, 1e-30)) * STEP) + 1.0
        start = half * vectors + group * vectors
        code[start : start + vectors, :] = power.astype(i32).astype(jnp.int16)
        gain = FULL * jnp.exp2(power * (-1.0 / STEP))
        for p in range(node):
            at = (group * node + p) * vectors
            scaled = wide[at : at + vectors, :] * gain[:, p : p + 1]
            code[at : at + vectors, :] = jnp.round(scaled).astype(i32).astype(jnp.int16)


def encode(keep, came, vectors):
    size, node = keep.shape
    half = size // vectors
    return pl.pallas_call(
        functools.partial(encode_kernel, half, vectors),
        out_shape=jax.ShapeDtypeStruct((size + half // node * vectors, node), jnp.int16),
        in_specs=[vmem()] * 2,
        out_specs=vmem(),
        scratch_shapes=[pltpu.VMEM((size, node), f32)],
        name="encode",
    )(keep, came)


def decode_kernel(half, vectors, weighted, *refs):
    if weighted:
        code, came, drive, out = refs
    else:
        code, came, out = refs
    node = code.shape[1]
    shape = (vectors, node)
    energy = jnp.zeros(shape, f32)
    cross = jnp.zeros(shape, f32)
    for group in range(half // node):
        start = half * vectors + group * vectors
        gains = [
            jnp.exp2(ref[start : start + vectors, :].astype(i32).astype(f32) * (1.0 / STEP)) * (1.0 / FULL)
            for ref in (code, came)
        ]
        for p in range(node):
            at = (group * node + p) * vectors
            one, two = [
                ref[at : at + vectors, :].astype(i32).astype(f32) * gain[:, p : p + 1]
                for ref, gain in zip((code, came), gains)
            ]
            value = one + two
            out[at : at + vectors, :] = value
            energy = energy + value * value
            if weighted:
                cross = cross + value * drive[at : at + vectors, :]
    at = half * vectors
    if weighted:
        out[at : at + vectors, :] = cross
        at = at + vectors
    out[at : at + vectors, :] = energy


def decode(code, came, vectors, drive=None):
    node = code.shape[1]
    extra = 1 if drive is None else 2
    half = code.shape[0] * node // (node + 1) // vectors
    inputs = (code, came) if drive is None else (code, came, drive)
    return pl.pallas_call(
        functools.partial(decode_kernel, half, vectors, drive is not None),
        out_shape=jax.ShapeDtypeStruct(((half + extra) * vectors, node), f32),
        in_specs=[vmem()] * len(inputs),
        out_specs=vmem(),
        name="decode",
    )(*inputs)


def pack_kernel(half, vectors, groups, extra, asked, origin, where, mine, other, message):
    core = jnp.bitwise_and(where[1], 1)
    each = 2 * CAP + extra

    def fetch(row):
        side = row // half
        inside = row - side * half
        return jnp.where(side == core, mine[tile(inside, vectors), :], other[tile(inside, vectors), :])

    sums = [
        mine[(half + e) * vectors : (half + e + 1) * vectors, :]
        + other[(half + e) * vectors : (half + e + 1) * vectors, :]
        for e in range(extra)
    ]

    def send(peer, carry):
        for k in range(CAP):
            slot = peer * CAP + k
            message[tile(peer * each + k, vectors), :] = fetch(jnp.maximum(asked[slot], 0))
            message[tile(peer * each + CAP + k, vectors), :] = fetch(origin[slot])
        for e in range(extra):
            message[tile(peer * each + 2 * CAP + e, vectors), :] = sums[e]
        return carry

    lax.fori_loop(0, groups, send, 0)


def pack(asked, origin, where, mine, other, vectors, extra):
    node = mine.shape[1]
    half = mine.shape[0] // vectors - extra
    groups = lax.axis_size("curve")
    return pl.pallas_call(
        functools.partial(pack_kernel, half, vectors, groups, extra),
        out_shape=jax.ShapeDtypeStruct((groups * (2 * CAP + extra) * vectors, node), f32),
        in_specs=[smem()] * 3 + [vmem()] * 2,
        out_specs=vmem(),
        name="pack",
    )(asked, origin, where, mine, other)


def finish_kernel(vectors, where, shares, scale, alpha, beta, state, first, second, out, one, two):
    shape = scale.shape
    across = lax.broadcasted_iota(i32, shape, 1)
    down = lax.broadcasted_iota(i32, shape, 0)
    line = jnp.broadcast_to(jnp.sum(shares[...], axis=0, keepdims=True), shape)
    alpha_second = jnp.broadcast_to(row_sum(jnp.where(across == down, line, 0.0)), shape)
    alpha_first, beta_first = alpha[...], beta[...]
    term_one = jnp.ones(shape, f32)
    term_two = jnp.zeros(shape, f32)
    total_one, total_two = term_one, term_two
    for turn in range(1, TAYLOR):
        factor = time_step / (turn + 1.0)
        next_one = factor * (alpha_first * term_one + beta_first * term_two)
        next_two = factor * (beta_first * term_one + alpha_second * term_two)
        term_one, term_two = next_one, next_two
        total_one, total_two = total_one + next_one, total_two + next_two
    one[...] = total_one
    two[...] = total_two
    width = state.shape[0]
    for v in range(width):
        at = where[1] * width + v
        spread_to = state.shape[1:]
        lift = jnp.broadcast_to(time_step * scale[pl.ds(at, 1), :], spread_to)
        weight_one = jnp.broadcast_to(one[pl.ds(at, 1), :], spread_to)
        weight_two = jnp.broadcast_to(two[pl.ds(at, 1), :], spread_to)
        out[v] = state[v] + lift * (weight_one * first[v] + weight_two * second[v])


def finish(where, shares, scale, alpha, beta, state, first, second):
    vectors, node = scale.shape
    return pl.pallas_call(
        functools.partial(finish_kernel, vectors),
        out_shape=jax.ShapeDtypeStruct(state.shape, f32),
        in_specs=[smem()] + [vmem()] * 7,
        out_specs=vmem(),
        scratch_shapes=[pltpu.VMEM((vectors, node), f32)] * 2,
        name="finish",
    )(where, shares, scale, alpha, beta, state, first, second)


def swap(array, bit):
    size = lax.axis_size("band")
    return lax.ppermute(array, "band", [(k, k ^ bit) for k in range(size)])


def exchange(array):
    return lax.all_to_all(array, "curve", split_axis=0, concat_axis=0, tiled=True)


def band_sum(keep, give, vectors, drive=None):
    code = encode(keep, swap(give, 1), vectors)
    mine = decode(code, swap(code, 2), vectors, drive)
    return mine, swap(mine, 1)


def body(state, blocks, diag_blocks, block_cols):
    groups = lax.axis_size("curve")
    devices = groups * lax.axis_size("band")
    width = state.shape[0]
    vectors = width * lax.axis_size("band")
    rounded = state.astype(bf16)
    across = swap(rounded, 2)
    parts = [rounded, swap(rounded, 1), across, swap(across, 1)]
    where = jnp.stack([lax.axis_index("curve"), lax.axis_index("band")]).astype(i32)
    pick, target, wanted, origin = plan(block_cols[:, 0], where)
    asked = exchange(wanted.reshape(groups, CAP)).reshape(-1)
    arrived = exchange(pick_blocks(origin, blocks))
    plans = (pick, target, asked, where)
    gathered, message = spread(parts, asked, origin, where)
    halo = exchange(message)
    keep, give = apply_first(plans, gathered, halo, state, blocks, diag_blocks, arrived)
    mine, other = band_sum(keep, give, vectors)
    halo = exchange(pack(asked, origin, where, mine, other, vectors, 1))
    drive = (mine, other, halo)
    keep, give, scale = apply_second(plans, mine, other, halo, blocks, diag_blocks, arrived)
    mine, other = band_sum(keep, give, vectors, mine)
    halo = exchange(pack(asked, origin, where, mine, other, vectors, 2))
    image = (mine, other, halo)
    share, first, second, alpha, beta = apply_third(plans, width, scale, drive, image, blocks, diag_blocks, devices)
    shares = lax.all_to_all(share, ("curve", "band"), split_axis=0, concat_axis=0, tiled=True)
    return finish(where, shares, scale, alpha, beta, state, first, second)


def solution(mesh):
    return jax.shard_map(
        body,
        mesh=mesh,
        in_specs=(
            P("band", "curve", None),
            P("curve", "band", None, None),
            P(("curve", "band"), None, None),
            P("curve", "band"),
        ),
        out_specs=P("band", "curve", None),
        check_vma=False,
    )
```

```python
import functools

import jax
import jax.numpy as jnp
from jax import lax
from jax.experimental import pallas as pl
from jax.experimental.pallas import tpu as pltpu
from jax.sharding import PartitionSpec as P

CAP = 2
TAYLOR = 16
UNROLL = 32
CHUNKS = 2

epsilon = 1e-06
time_step = 0.5
quadratic = 1.0
STEP = 256.0
FULL = 32767.0

f32 = jnp.float32
bf16 = jnp.bfloat16
i32 = jnp.int32


def nonlinear(field):
    return quadratic * field * field - field * field * field


def tile(index, rows):
    return pl.ds(pl.multiple_of(index * rows, rows), rows)


def smem():
    return pl.BlockSpec(memory_space=pltpu.SMEM)


def vmem():
    return pl.BlockSpec(memory_space=pltpu.VMEM)


def anywhere():
    return pl.BlockSpec(memory_space=pl.ANY)


def params(mebibytes):
    return pltpu.CompilerParams(vmem_limit_bytes=mebibytes * 1024 * 1024)


def shaped(shape, dtype):
    return jax.ShapeDtypeStruct(shape, dtype)


def times(field, block):
    return lax.dot_general(field, block, (((1,), (0,)), ((), ())), preferred_element_type=f32)


def times_transposed(field, block):
    return lax.dot_general(field, block, (((1,), (1,)), ((), ())), preferred_element_type=f32)


def row_sum(part):
    return jnp.sum(part, axis=1, keepdims=True)


def as_line(column, shape):
    across = lax.broadcasted_iota(i32, shape, 1)
    down = lax.broadcasted_iota(i32, shape, 0)
    return jnp.sum(jnp.where(across == down, jnp.broadcast_to(column, shape), 0.0), axis=0, keepdims=True)


def as_column(line, shape, offset=0):
    across = lax.broadcasted_iota(i32, shape, 1)
    down = lax.broadcasted_iota(i32, shape, 0)
    picked = jnp.where(across == down + offset, jnp.broadcast_to(line, shape), 0.0)
    return jnp.broadcast_to(row_sum(picked), shape)


def core_of(band):
    return jnp.bitwise_and(band, 1)


def plan_kernel(cols, pick, target, wanted, origin):
    groups, lanes = wanted.shape
    rows = cols.shape[1]
    here = lax.axis_index("curve")
    column = cols[...]
    owner = column // rows
    inner = column - owner * rows
    shape = (groups, rows)
    peer = lax.broadcasted_iota(i32, shape, 0)
    place = lax.broadcasted_iota(i32, shape, 1).astype(f32)
    inside = jnp.broadcast_to(inner.astype(f32), shape)
    left = (jnp.broadcast_to(owner, shape) == peer) & (peer != here)
    number = jnp.zeros((1, rows), f32)
    lane = lax.broadcasted_iota(i32, (groups, lanes), 1)
    want = jnp.full((groups, lanes), -1.0, f32)
    source = jnp.zeros((groups, lanes), f32)
    none = float(rows)
    for k in range(CAP):
        least = jnp.min(jnp.where(left, place, none), axis=1, keepdims=True)
        hit = left & (place == least)
        left = left & (place != least)
        aim = row_sum(jnp.where(hit, inside, 0.0))
        want = jnp.where((lane == k) & (least < none), aim, want)
        source = jnp.where((lane == k) & (least < none), least, source)
        slot = (peer * (2 * CAP) + k).astype(f32)
        number = number + jnp.sum(jnp.where(hit, slot, 0.0), axis=0, keepdims=True)
    wanted[...] = want.astype(i32)
    origin[...] = source.astype(i32)
    pick[...] = jnp.where(owner == here, inner, rows + number.astype(i32))
    target[...] = jnp.where(owner == here, inner, rows)


def plan(cols):
    rows = cols.shape[1]
    groups = lax.axis_size("curve")
    return pl.pallas_call(
        plan_kernel,
        out_shape=[shaped((1, rows), i32)] * 2 + [shaped((groups, 128), i32)] * 2,
        in_specs=[vmem()],
        out_specs=[vmem()] * 4,
        compiler_params=params(8),
        name="plan",
    )(cols)


def spread_kernel(rows, vectors, groups, width, origin, blocks, *refs):
    count = vectors // width
    parts, (field, own, split, wide, sems) = refs[:count], refs[count:]
    slots = groups * CAP

    def fetch(slot):
        peer = slot // CAP
        row = origin[peer, slot - peer * CAP]
        return pltpu.make_async_copy(blocks.at[row, 0], own.at[slot], sems.at[slot])

    def begin(slot, carry):
        fetch(slot).start()
        return carry

    lax.fori_loop(0, slots, begin, 0)
    band = lax.axis_index("band")
    for k, part in enumerate(parts):
        start = jnp.bitwise_xor(band, k) * width
        for v in range(width):
            wide[pl.ds(start + v, rows, stride=vectors), :] = part[v].astype(f32)
    field[0 : rows * vectors, :] = wide[...].astype(bf16)
    field[rows * vectors :, :] = jnp.zeros((vectors, field.shape[1]), bf16)

    def end(slot, carry):
        fetch(slot).wait()
        return carry

    lax.fori_loop(0, slots, end, 0)

    def product(peer, carry):
        for k in range(CAP):
            value = times(field[tile(origin[peer, k], vectors), :], own[peer * CAP + k])
            high = value.astype(bf16)
            split[tile(peer * (2 * CAP) + k, vectors), :] = high
            split[tile(peer * (2 * CAP) + CAP + k, vectors), :] = (value - high.astype(f32)).astype(bf16)
        return carry

    lax.fori_loop(0, groups, product, 0)


def spread(parts, origin, blocks):
    width, rows, node = parts[0].shape
    groups = lax.axis_size("curve")
    slots = groups * CAP
    vectors = width * len(parts)
    return pl.pallas_call(
        functools.partial(spread_kernel, rows, vectors, groups, width),
        out_shape=[
            shaped(((rows + 1) * vectors, node), bf16),
            shaped((slots, node, node), bf16),
            shaped((slots * 2 * vectors, node), bf16),
        ],
        in_specs=[smem(), anywhere()] + [vmem()] * len(parts),
        out_specs=[vmem()] * 3,
        scratch_shapes=[pltpu.VMEM((rows * vectors, node), f32), pltpu.SemaphoreType.DMA((slots,))],
        compiler_params=params(16),
        name="spread",
    )(origin, blocks, *parts)


def reply_kernel(vectors, groups, asked, field, split, message):
    def send(peer, carry):
        at = peer * (3 * CAP)
        for k in range(CAP):
            message[tile(at + k, vectors), :] = field[tile(jnp.maximum(asked[peer, k], 0), vectors), :]
        for k in range(2 * CAP):
            message[tile(at + CAP + k, vectors), :] = split[tile(peer * (2 * CAP) + k, vectors), :]
        return carry

    lax.fori_loop(0, groups, send, 0)


def reply(asked, field, split, vectors):
    groups = lax.axis_size("curve")
    return pl.pallas_call(
        functools.partial(reply_kernel, vectors, groups),
        out_shape=shaped((groups * 3 * CAP * vectors, field.shape[1]), bf16),
        in_specs=[smem()] + [vmem()] * 2,
        out_specs=vmem(),
        compiler_params=params(16),
        name="reply",
    )(asked, field, split)


class Stream:
    def __init__(self, blocks, diag, held, held_diag, sems):
        self.blocks, self.diag, self.held, self.held_diag, self.sems = blocks, diag, held, held_diag, sems
        self.pieces = blocks.shape[0] // UNROLL
        self.own = diag.shape[0] // self.pieces

    def copies(self, piece):
        rows = pl.ds(piece * UNROLL, UNROLL)
        own = pl.ds(piece * self.own, self.own)
        return (
            pltpu.make_async_copy(self.blocks.at[rows, 0], self.held.at[rows], self.sems.at[0, piece]),
            pltpu.make_async_copy(self.diag.at[own], self.held_diag.at[own], self.sems.at[1, piece]),
        )

    def start(self):
        for piece in range(self.pieces):
            for copy in self.copies(piece):
                copy.start()

    def wait(self, piece):
        for copy in self.copies(piece):
            copy.wait()


def stream_scratch(blocks, diag):
    rows, node = blocks.shape[0], blocks.shape[-1]
    return [
        pltpu.VMEM((rows, node, node), bf16),
        pltpu.VMEM(diag.shape, bf16),
        pltpu.SemaphoreType.DMA((2, rows // UNROLL)),
    ]


def products(vectors, limit, pick, target, field, stream, total):
    band = lax.axis_index("band")

    def some(piece, carry):
        stream.wait(piece)
        forward, mirrored = [], []
        base = piece * UNROLL
        for u in range(UNROLL):
            row = base + u
            block = stream.held[row]
            source = pick[0, row]
            if limit is not None:
                source = jnp.minimum(source, limit)
            forward.append(times_transposed(field[tile(source, vectors), :], block))
            mirrored.append(times(field[tile(row, vectors), :], block))
        for u in range(UNROLL):
            total[tile(base + u, vectors), :] += forward[u]
            total[tile(target[0, base + u], vectors), :] += mirrored[u]
        own = stream.own
        first = band * (own * stream.pieces) + piece * own
        values = [times(field[tile(first + d, vectors), :], stream.held_diag[piece * own + d]) for d in range(own)]
        for d, value in enumerate(values):
            total[tile(first + d, vectors), :] += value
        return carry

    lax.fori_loop(0, stream.pieces, some, 0)


def give_out(rows, vectors, total, outs):
    core = core_of(lax.axis_index("band"))
    half = rows // 2
    size = half // CHUNKS * vectors
    for side in range(2):
        start = jnp.where(core == side, 0, half) * vectors
        for c in range(CHUNKS):
            outs[side * CHUNKS + c][...] = total[pl.ds(pl.multiple_of(start + c * size, size), size), :]


def local_kernel(rows, vectors, pick, target, field, state, blocks, diag, total, *scratch):
    stream = Stream(blocks, diag, *scratch)
    stream.start()
    total[...] = jnp.zeros_like(total)
    width = state.shape[0]
    band = lax.axis_index("band")
    for v in range(width):
        total[pl.ds(band * width + v, rows, stride=vectors), :] = nonlinear(state[v])
    products(vectors, rows, pick, target, field, stream, total)


def operate_local(pick, target, field, state, blocks, diag):
    rows, node = blocks.shape[0], blocks.shape[-1]
    vectors = field.shape[0] // (rows + 1)
    return pl.pallas_call(
        functools.partial(local_kernel, rows, vectors),
        out_shape=shaped(((rows + 1) * vectors, node), f32),
        in_specs=[smem()] * 2 + [vmem()] * 2 + [anywhere()] * 2,
        out_specs=vmem(),
        scratch_shapes=stream_scratch(blocks, diag),
        compiler_params=params(24),
        name="operate_local",
    )(pick, target, field, state, blocks, diag)


def settle_kernel(rows, vectors, groups, wanted, origin, asked, local, halo, own, *refs):
    outs, total = refs[:-1], refs[-1]
    total[...] = local[...]

    def some(peer, carry):
        at = peer * (3 * CAP)
        values = []
        for k in range(CAP):
            value = times_transposed(halo[tile(at + k, vectors), :], own[peer * CAP + k])
            values.append((jnp.where(wanted[peer, k] < 0, rows, origin[peer, k]), value))
        for k in range(CAP):
            value = halo[tile(at + CAP + k, vectors), :].astype(f32)
            value = value + halo[tile(at + 2 * CAP + k, vectors), :].astype(f32)
            values.append((jnp.where(asked[peer, k] < 0, rows, asked[peer, k]), value))
        for aim, value in values:
            total[tile(aim, vectors), :] += value
        return carry

    lax.fori_loop(0, groups, some, 0)
    give_out(rows, vectors, total, outs)


def chunk_shapes(rows, vectors, node):
    return [shaped((rows // 2 // CHUNKS * vectors, node), f32)] * (2 * CHUNKS)


def settle(wanted, origin, asked, local, halo, own, rows):
    node = local.shape[1]
    vectors = local.shape[0] // (rows + 1)
    groups = lax.axis_size("curve")
    outs = pl.pallas_call(
        functools.partial(settle_kernel, rows, vectors, groups),
        out_shape=chunk_shapes(rows, vectors, node),
        in_specs=[smem()] * 3 + [vmem()] * 3,
        out_specs=[vmem()] * (2 * CHUNKS),
        scratch_shapes=[pltpu.VMEM(local.shape, f32)],
        compiler_params=params(24),
        name="settle",
    )(wanted, origin, asked, local, halo, own)
    return outs[:CHUNKS], outs[CHUNKS:]


def second_kernel(rows, vectors, groups, pick, target, asked, *refs):
    arrays, (halo, arrived, blocks, diag), refs = refs[: 2 * CHUNKS], refs[2 * CHUNKS : 2 * CHUNKS + 4], refs[2 * CHUNKS + 4 :]
    outs, (scale, field, total), scratch = refs[: 2 * CHUNKS], refs[2 * CHUNKS : 2 * CHUNKS + 3], refs[2 * CHUNKS + 3 :]
    stream = Stream(blocks, diag, *scratch)
    stream.start()
    half = rows // 2
    each = half // CHUNKS
    message = halo.shape[0] // groups
    shape = scale.shape
    line = jnp.zeros((1, shape[1]), f32)
    for g in range(groups):
        at = g * message + 2 * CAP * vectors
        line = line + halo[at : at + 1, :]
    energy = as_column(line, shape)
    beta = jnp.sqrt(energy + epsilon)
    scale[...] = beta
    inverse = 1.0 / beta
    core = core_of(lax.axis_index("band"))
    for side in range(2):
        start = jnp.where(core == side, 0, half)
        for c in range(CHUNKS):
            array = arrays[side * CHUNKS + c]

            def one(p, carry, start=start, c=c, array=array):
                field[tile(start + c * each + p, vectors), :] = (array[tile(p, vectors), :] * inverse).astype(bf16)
                return carry

            lax.fori_loop(0, each, one, 0, unroll=16)

    def row(g, carry):
        for k in range(2 * CAP):
            at = pl.multiple_of(g * message + k * vectors, 8)
            value = halo[pl.ds(at, vectors), :] * inverse
            field[tile(rows + g * (2 * CAP) + k, vectors), :] = value.astype(bf16)
        return carry

    lax.fori_loop(0, groups, row, 0)
    total[...] = jnp.zeros_like(total)
    products(vectors, None, pick, target, field, stream, total)

    def some(peer, carry):
        values = []
        for k in range(CAP):
            place = rows + peer * (2 * CAP) + CAP + k
            aim = asked[peer, k]
            value = times(field[tile(place, vectors), :], arrived[peer * CAP + k])
            values.append((jnp.where(aim < 0, rows, aim), value))
        for aim, value in values:
            total[tile(aim, vectors), :] += value
        return carry

    lax.fori_loop(0, groups, some, 0)
    give_out(rows, vectors, total, outs)


def operate_second(pick, target, asked, arrays, halo, arrived, blocks, diag):
    rows, node = blocks.shape[0], blocks.shape[-1]
    groups = lax.axis_size("curve")
    message = halo.shape[0] // groups
    vectors = (message - 8) // (2 * CAP)
    outs = pl.pallas_call(
        functools.partial(second_kernel, rows, vectors, groups),
        out_shape=chunk_shapes(rows, vectors, node) + [shaped((vectors, node), f32)],
        in_specs=[smem()] * 3 + [vmem()] * (2 * CHUNKS + 2) + [anywhere()] * 2,
        out_specs=[vmem()] * (2 * CHUNKS + 1),
        scratch_shapes=[
            pltpu.VMEM(((rows + groups * 2 * CAP) * vectors, node), bf16),
            pltpu.VMEM(((rows + 1) * vectors, node), f32),
        ]
        + stream_scratch(blocks, diag),
        compiler_params=params(32),
        name="operate_second",
    )(pick, target, asked, *arrays, halo, arrived, blocks, diag)
    return outs[:CHUNKS], outs[CHUNKS : 2 * CHUNKS], outs[-1]


def third_kernel(rows, vectors, groups, width, pick, wanted, origin, *refs):
    count = 2 * CHUNKS
    drive, image, (own, blocks, diag), refs = refs[:count], refs[count : 2 * count], refs[2 * count : 2 * count + 3], refs[2 * count + 3 :]
    form, left, drive_own, image_own, field = refs[:5]
    stream = Stream(blocks, diag, *refs[5:])
    stream.start()
    half = rows // 2
    each = half // CHUNKS
    shape = form.shape
    band = lax.axis_index("band")
    core = core_of(band)
    for side in range(2):
        start = jnp.where(core == side, 0, half)
        for c in range(CHUNKS):
            array = image[side * CHUNKS + c]

            def one(p, carry, start=start, c=c, array=array):
                field[tile(start + c * each + p, vectors), :] = array[tile(p, vectors), :].astype(bf16)
                return carry

            lax.fori_loop(0, each, one, 0, unroll=16)
            for v in range(width):
                inside = pl.ds(pl.multiple_of(start + c * each, each), each)
                source = pl.ds(band * width + v, each, stride=vectors)
                drive_own[v, inside, :] = drive[side * CHUNKS + c][source, :]
                image_own[v, inside, :] = array[source, :]
    field[rows * vectors :, :] = jnp.zeros((vectors, shape[1]), bf16)

    def some(piece, parts):
        stream.wait(piece)
        twice, once = parts
        base = piece * UNROLL
        for u in range(UNROLL):
            row = base + u
            value = times(field[tile(row, vectors), :], stream.held[row])
            source = jnp.minimum(pick[0, row], rows)
            twice = twice + value * field[tile(source, vectors), :].astype(f32)
        for d in range(stream.own):
            row = (band * stream.pieces + piece) * stream.own + d
            here = field[tile(row, vectors), :]
            once = once + times(here, stream.held_diag[piece * stream.own + d]) * here.astype(f32)
        return twice, once

    nothing = jnp.zeros(shape, f32)
    twice, once = lax.fori_loop(0, stream.pieces, some, (nothing, nothing))
    form[...] = 2.0 * twice + once

    def remote(peer, carry):
        for k in range(CAP):
            value = times(field[tile(origin[peer, k], vectors), :], own[peer * CAP + k])
            left[tile(peer * CAP + k, vectors), :] = jnp.where(wanted[peer, k] < 0, 0.0, 2.0) * value
        return carry

    lax.fori_loop(0, groups, remote, 0)


def operate_third(pick, wanted, origin, drive, image, own, blocks, diag, width, vectors):
    rows, node = blocks.shape[0], blocks.shape[-1]
    groups = lax.axis_size("curve")
    mine = shaped((width, rows, node), f32)
    return pl.pallas_call(
        functools.partial(third_kernel, rows, vectors, groups, width),
        out_shape=[shaped((vectors, node), f32), shaped((groups * CAP * vectors, node), f32), mine, mine],
        in_specs=[smem()] * 3 + [vmem()] * (4 * CHUNKS + 1) + [anywhere()] * 2,
        out_specs=[vmem()] * 4,
        scratch_shapes=[pltpu.VMEM(((rows + 1) * vectors, node), bf16)] + stream_scratch(blocks, diag),
        compiler_params=params(32),
        name="operate_third",
    )(pick, wanted, origin, *drive, *image, own, blocks, diag)


def tail_kernel(each, vectors, form, left, halo, *refs):
    image, share = refs[:-1], refs[-1]
    shape = form.shape
    total = form[...]
    for slot in range(left.shape[0] // vectors):
        at = slot * vectors
        total = total + left[at : at + vectors, :] * halo[at : at + vectors, :].astype(f32)
    values = [total]
    for e in range(2):
        at = (each + e) * vectors
        value = image[0][at : at + vectors, :]
        for other in image[1:]:
            value = value + other[at : at + vectors, :]
        values.append(0.5 * value)
    line = jnp.zeros((1, shape[1]), f32)
    across = lax.broadcasted_iota(i32, shape, 1)
    down = lax.broadcasted_iota(i32, shape, 0)
    for e, value in enumerate(values):
        column = jnp.broadcast_to(row_sum(value), shape)
        line = line + jnp.sum(jnp.where(across == down + e * vectors, column, 0.0), axis=0, keepdims=True)
    share[...] = jnp.broadcast_to(line, share.shape)


def tail(form, left, halo, image, devices):
    vectors, node = form.shape
    each = image[0].shape[0] // vectors - 2
    return pl.pallas_call(
        functools.partial(tail_kernel, each, vectors),
        out_shape=shaped((devices, node), f32),
        in_specs=[vmem()] * (3 + len(image)),
        out_specs=vmem(),
        compiler_params=params(16),
        name="tail",
    )(form, left, halo, *image)


def code_tiles(each, node):
    return -(-each // node)


def encode_kernel(each, vectors, keep, came, code, wide):
    node = keep.shape[1]
    lanes = lax.broadcasted_iota(i32, (vectors, node), 1)
    for group in range(code_tiles(each, node)):
        inside = range(group * node, min(each, (group + 1) * node))
        peak = jnp.zeros((vectors, node), f32)
        for p in inside:
            at = p * vectors
            value = keep[at : at + vectors, :] + came[at : at + vectors, :]
            wide[at : at + vectors, :] = value
            peak = jnp.where(lanes == p - group * node, jnp.max(jnp.abs(value), axis=1, keepdims=True), peak)
        power = jnp.ceil(jnp.log2(jnp.maximum(peak, 1e-30)) * STEP) + 1.0
        start = (each + group) * vectors
        code[start : start + vectors, :] = power.astype(i32).astype(jnp.int16)
        gain = FULL * jnp.exp2(power * (-1.0 / STEP))
        for p in inside:
            at = p * vectors
            lane = p - group * node
            scaled = wide[at : at + vectors, :] * gain[:, lane : lane + 1]
            code[at : at + vectors, :] = jnp.round(scaled).astype(i32).astype(jnp.int16)


def encode(keep, came, vectors):
    size, node = keep.shape
    each = size // vectors
    return pl.pallas_call(
        functools.partial(encode_kernel, each, vectors),
        out_shape=shaped(((each + code_tiles(each, node)) * vectors, node), jnp.int16),
        in_specs=[vmem()] * 2,
        out_specs=vmem(),
        scratch_shapes=[pltpu.VMEM((size, node), f32)],
        compiler_params=params(12),
        name="encode",
    )(keep, came)


def decode_kernel(each, vectors, weighted, *refs):
    if weighted:
        code, came, drive, out = refs
    else:
        code, came, out = refs
    node = code.shape[1]
    shape = (vectors, node)
    energy = jnp.zeros(shape, f32)
    cross = jnp.zeros(shape, f32)
    for group in range(code_tiles(each, node)):
        start = (each + group) * vectors
        gains = [
            jnp.exp2(ref[start : start + vectors, :].astype(i32).astype(f32) * (1.0 / STEP)) * (1.0 / FULL)
            for ref in (code, came)
        ]
        for p in range(group * node, min(each, (group + 1) * node)):
            at = p * vectors
            lane = p - group * node
            one, two = [
                ref[at : at + vectors, :].astype(i32).astype(f32) * gain[:, lane : lane + 1]
                for ref, gain in zip((code, came), gains)
            ]
            value = one + two
            out[at : at + vectors, :] = value
            energy = energy + value * value
            if weighted:
                cross = cross + value * drive[at : at + vectors, :]
    at = each * vectors
    if weighted:
        out[at : at + vectors, :] = cross
        at = at + vectors
    out[at : at + vectors, :] = energy


def decode(code, came, vectors, each, drive=None):
    node = code.shape[1]
    extra = 1 if drive is None else 2
    inputs = (code, came) if drive is None else (code, came, drive)
    return pl.pallas_call(
        functools.partial(decode_kernel, each, vectors, drive is not None),
        out_shape=shaped(((each + extra) * vectors, node), f32),
        in_specs=[vmem()] * len(inputs),
        out_specs=vmem(),
        compiler_params=params(12),
        name="decode",
    )(*inputs)


def fetch_row(arrays, each, vectors, row):
    core = core_of(lax.axis_index("band"))
    half = each * CHUNKS
    side = row // half
    inside = row - side * half
    chunk = inside // each
    place = tile(inside - chunk * each, vectors)
    value = arrays[0][place, :]
    number = jnp.where(side == core, chunk, CHUNKS + chunk)
    for k in range(1, 2 * CHUNKS):
        value = jnp.where(number == k, arrays[k][place, :], value)
    return value


def pack_kernel(each, vectors, groups, asked, origin, *refs):
    arrays, message = refs[:-1], refs[-1]
    shape = (vectors, message.shape[1])
    sums = arrays[0][each * vectors :, :]
    for array in arrays[1:]:
        sums = sums + array[each * vectors :, :]
    line = jnp.broadcast_to(as_line(row_sum(sums), shape), shape)[0:8, :]
    size = 2 * CAP * vectors + 8

    def send(peer, carry):
        for k in range(2 * CAP):
            row = jnp.maximum(asked[peer, k], 0) if k < CAP else origin[peer, k - CAP]
            at = pl.multiple_of(peer * size + k * vectors, 8)
            message[pl.ds(at, vectors), :] = fetch_row(arrays, each, vectors, row)
        message[pl.ds(pl.multiple_of(peer * size + 2 * CAP * vectors, 8), 8), :] = line
        return carry

    lax.fori_loop(0, groups, send, 0)


def pack(asked, origin, arrays, vectors):
    node = arrays[0].shape[1]
    each = arrays[0].shape[0] // vectors - 1
    groups = lax.axis_size("curve")
    return pl.pallas_call(
        functools.partial(pack_kernel, each, vectors, groups),
        out_shape=shaped((groups * (2 * CAP * vectors + 8), node), f32),
        in_specs=[smem()] * 2 + [vmem()] * (2 * CHUNKS),
        out_specs=vmem(),
        compiler_params=params(16),
        name="pack",
    )(asked, origin, *arrays)


def pack_rounded_kernel(each, vectors, groups, asked, *refs):
    arrays, message = refs[:-1], refs[-1]

    def send(peer, carry):
        for k in range(CAP):
            value = fetch_row(arrays, each, vectors, jnp.maximum(asked[peer, k], 0))
            message[tile(peer * CAP + k, vectors), :] = value.astype(bf16)
        return carry

    lax.fori_loop(0, groups, send, 0)


def pack_rounded(asked, arrays, vectors):
    node = arrays[0].shape[1]
    each = arrays[0].shape[0] // vectors - 2
    groups = lax.axis_size("curve")
    return pl.pallas_call(
        functools.partial(pack_rounded_kernel, each, vectors, groups),
        out_shape=shaped((groups * CAP * vectors, node), bf16),
        in_specs=[smem()] + [vmem()] * (2 * CHUNKS),
        out_specs=vmem(),
        compiler_params=params(16),
        name="pack_rounded",
    )(asked, *arrays)


def finish_kernel(shares, scale, state, drive, image, out, one, two, lift, mix):
    shape = scale.shape
    vectors = shape[0]
    line = jnp.sum(shares[...], axis=0, keepdims=True)
    form, cross, energy = [as_column(line, shape, e * vectors) for e in range(3)]
    beta_zero = scale[...]
    unit = 1.0 - epsilon / (beta_zero * beta_zero)
    alpha_first = cross / beta_zero
    square = alpha_first * alpha_first
    beta_first = jnp.sqrt(jnp.maximum(energy - square * (2.0 - unit), 0.0) + epsilon)
    alpha_second = (form - 2.0 * alpha_first * energy + square * alpha_first) / (beta_first * beta_first)
    alpha_second = alpha_second - alpha_first * (1.0 - unit)
    term_one = jnp.ones(shape, f32)
    term_two = jnp.zeros(shape, f32)
    total_one, total_two = term_one, term_two
    for turn in range(1, TAYLOR):
        factor = time_step / (turn + 1.0)
        next_one = factor * (alpha_first * term_one + beta_first * term_two)
        next_two = factor * (beta_first * term_one + alpha_second * term_two)
        term_one, term_two = next_one, next_two
        total_one, total_two = total_one + next_one, total_two + next_two
    one[...] = time_step * total_one
    two[...] = time_step * beta_zero * total_two / beta_first
    mix[...] = alpha_first / beta_zero
    width = state.shape[0]
    for v in range(width):
        at = pl.ds(lax.axis_index("band") * width + v, 1)
        size = state.shape[1:]
        weight_one, weight_two, share = [jnp.broadcast_to(ref[at, :], size) for ref in (one, two, mix)]
        out[v] = state[v] + (weight_one * drive[v] + weight_two * (image[v] - share * drive[v]))


def finish(shares, scale, state, drive, image):
    return pl.pallas_call(
        finish_kernel,
        out_shape=shaped(state.shape, f32),
        in_specs=[vmem()] * 5,
        out_specs=vmem(),
        scratch_shapes=[pltpu.VMEM(scale.shape, f32)] * 4,
        compiler_params=params(16),
        name="finish",
    )(shares, scale, state, drive, image)


def swap(array, bit):
    size = lax.axis_size("band")
    return lax.ppermute(array, "band", [(k, k ^ bit) for k in range(size)])


def exchange(array):
    return lax.all_to_all(array, "curve", split_axis=0, concat_axis=0, tiled=True)


def band_sum(keep, give, vectors, drive=None):
    each = keep[0].shape[0] // vectors
    came = [swap(array, 1) for array in give]
    codes = [encode(one, two, vectors) for one, two in zip(keep, came)]
    across = [swap(code, 2) for code in codes]
    mine = [
        decode(code, other, vectors, each, None if drive is None else drive[c])
        for c, (code, other) in enumerate(zip(codes, across))
    ]
    return mine + [swap(array, 1) for array in mine]


def body(state, blocks, diag_blocks, block_cols):
    groups = lax.axis_size("curve")
    devices = groups * lax.axis_size("band")
    width, rows = state.shape[:2]
    vectors = width * lax.axis_size("band")
    rounded = state.astype(bf16)
    across = swap(rounded, 2)
    parts = [rounded, swap(rounded, 1), across, swap(across, 1)]
    pick, target, wanted, origin = plan(block_cols.reshape(1, rows))
    asked = exchange(wanted)
    field, own, split = spread(parts, origin, blocks)
    message = reply(asked, field, split, vectors)
    halo = exchange(message)
    local = operate_local(pick, target, field, state, blocks, diag_blocks)
    keep, give = settle(wanted, origin, asked, local, halo, own, rows)
    drive = band_sum(keep, give, vectors)
    arrived = exchange(own)
    halo = exchange(pack(asked, origin, drive, vectors))
    keep, give, scale = operate_second(pick, target, asked, drive, halo, arrived, blocks, diag_blocks)
    image = band_sum(keep, give, vectors, drive)
    halo = exchange(pack_rounded(asked, image, vectors))
    form, left, drive_own, image_own = operate_third(
        pick, wanted, origin, drive, image, own, blocks, diag_blocks, width, vectors
    )
    share = tail(form, left, halo, image[:CHUNKS], devices)
    shares = lax.all_to_all(share, ("curve", "band"), split_axis=0, concat_axis=0, tiled=True)
    return finish(shares, scale, state, drive_own, image_own)


def solution(mesh):
    return jax.shard_map(
        body,
        mesh=mesh,
        in_specs=(
            P("band", "curve", None),
            P("curve", "band", None, None),
            P(("curve", "band"), None, None),
            P("curve", "band"),
        ),
        out_specs=P("band", "curve", None),
        check_vma=False,
    )
```

```python
import functools

import jax
import jax.numpy as jnp
from jax import lax
from jax.experimental import pallas as pl
from jax.experimental.pallas import tpu as pltpu
from jax.sharding import PartitionSpec as P

CAP = 2
TAYLOR = 16
UNROLL = 32
CHUNKS = 2

epsilon = 1e-06
time_step = 0.5
quadratic = 1.0
STEP = 256.0
FULL = 32767.0

f32 = jnp.float32
bf16 = jnp.bfloat16
i32 = jnp.int32


def nonlinear(field):
    return quadratic * field * field - field * field * field


def tile(index, rows):
    return pl.ds(pl.multiple_of(index * rows, rows), rows)


def smem():
    return pl.BlockSpec(memory_space=pltpu.SMEM)


def vmem():
    return pl.BlockSpec(memory_space=pltpu.VMEM)


def anywhere():
    return pl.BlockSpec(memory_space=pltpu.HBM)


def params(mebibytes):
    return pltpu.CompilerParams(vmem_limit_bytes=mebibytes * 1024 * 1024)


def in_hbm(array):
    return pltpu.with_memory_space_constraint(array, pltpu.HBM)


def shaped(shape, dtype):
    return jax.ShapeDtypeStruct(shape, dtype)


def times(field, block):
    return lax.dot_general(field, block, (((1,), (0,)), ((), ())), preferred_element_type=f32)


def times_transposed(field, block):
    return lax.dot_general(field, block, (((1,), (1,)), ((), ())), preferred_element_type=f32)


def row_sum(part):
    return jnp.sum(part, axis=1, keepdims=True)


def as_line(column, shape):
    across = lax.broadcasted_iota(i32, shape, 1)
    down = lax.broadcasted_iota(i32, shape, 0)
    return jnp.sum(jnp.where(across == down, jnp.broadcast_to(column, shape), 0.0), axis=0, keepdims=True)


def as_column(line, shape, offset=0):
    across = lax.broadcasted_iota(i32, shape, 1)
    down = lax.broadcasted_iota(i32, shape, 0)
    picked = jnp.where(across == down + offset, jnp.broadcast_to(line, shape), 0.0)
    return jnp.broadcast_to(row_sum(picked), shape)


def core_of(band):
    return jnp.bitwise_and(band, 1)


def plan_kernel(cols, pick, target, wanted, origin):
    groups, lanes = wanted.shape
    rows = cols.shape[1]
    here = lax.axis_index("curve")
    column = cols[...]
    owner = column // rows
    inner = column - owner * rows
    shape = (groups, rows)
    peer = lax.broadcasted_iota(i32, shape, 0)
    place = lax.broadcasted_iota(i32, shape, 1).astype(f32)
    inside = jnp.broadcast_to(inner.astype(f32), shape)
    left = (jnp.broadcast_to(owner, shape) == peer) & (peer != here)
    number = jnp.zeros((1, rows), f32)
    lane = lax.broadcasted_iota(i32, (groups, lanes), 1)
    want = jnp.full((groups, lanes), -1.0, f32)
    source = jnp.zeros((groups, lanes), f32)
    none = float(rows)
    for k in range(CAP):
        least = jnp.min(jnp.where(left, place, none), axis=1, keepdims=True)
        hit = left & (place == least)
        left = left & (place != least)
        aim = row_sum(jnp.where(hit, inside, 0.0))
        want = jnp.where((lane == k) & (least < none), aim, want)
        source = jnp.where((lane == k) & (least < none), least, source)
        slot = (peer * (2 * CAP) + k).astype(f32)
        number = number + jnp.sum(jnp.where(hit, slot, 0.0), axis=0, keepdims=True)
    wanted[...] = want.astype(i32)
    origin[...] = source.astype(i32)
    pick[...] = jnp.where(owner == here, inner, rows + number.astype(i32))
    target[...] = jnp.where(owner == here, inner, rows)


def plan(cols):
    rows = cols.shape[1]
    groups = lax.axis_size("curve")
    return pl.pallas_call(
        plan_kernel,
        out_shape=[shaped((1, rows), i32)] * 2 + [shaped((groups, 128), i32)] * 2,
        in_specs=[vmem()],
        out_specs=[vmem()] * 4,
        compiler_params=params(8),
        name="plan",
    )(cols)


def spread_kernel(rows, vectors, groups, width, origin, blocks, *refs):
    count = vectors // width
    parts, (field, own, split, wide, sems) = refs[:count], refs[count:]
    slots = groups * CAP

    def fetch(slot):
        peer = slot // CAP
        row = origin[peer, slot - peer * CAP]
        return pltpu.make_async_copy(blocks.at[row, 0], own.at[slot], sems.at[slot])

    def begin(slot, carry):
        fetch(slot).start()
        return carry

    lax.fori_loop(0, slots, begin, 0)
    band = lax.axis_index("band")
    for k, part in enumerate(parts):
        start = jnp.bitwise_xor(band, k) * width
        for v in range(width):
            wide[pl.ds(start + v, rows, stride=vectors), :] = part[v].astype(f32)
    field[0 : rows * vectors, :] = wide[...].astype(bf16)
    field[rows * vectors :, :] = jnp.zeros((vectors, field.shape[1]), bf16)

    def end(slot, carry):
        fetch(slot).wait()
        return carry

    lax.fori_loop(0, slots, end, 0)

    def product(peer, carry):
        for k in range(CAP):
            value = times(field[tile(origin[peer, k], vectors), :], own[peer * CAP + k])
            high = value.astype(bf16)
            split[tile(peer * (2 * CAP) + k, vectors), :] = high
            split[tile(peer * (2 * CAP) + CAP + k, vectors), :] = (value - high.astype(f32)).astype(bf16)
        return carry

    lax.fori_loop(0, groups, product, 0)


def spread(parts, origin, blocks):
    width, rows, node = parts[0].shape
    groups = lax.axis_size("curve")
    slots = groups * CAP
    vectors = width * len(parts)
    return pl.pallas_call(
        functools.partial(spread_kernel, rows, vectors, groups, width),
        out_shape=[
            pltpu.HBM(((rows + 1) * vectors, node), bf16),
            shaped((slots, node, node), bf16),
            shaped((slots * 2 * vectors, node), bf16),
        ],
        in_specs=[smem(), anywhere()] + [vmem()] * len(parts),
        out_specs=[vmem()] * 3,
        scratch_shapes=[pltpu.VMEM((rows * vectors, node), f32), pltpu.SemaphoreType.DMA((slots,))],
        compiler_params=params(16),
        name="spread",
    )(origin, blocks, *parts)


def reply_kernel(vectors, groups, asked, field, split, message):
    def send(peer, carry):
        at = peer * (3 * CAP)
        for k in range(CAP):
            message[tile(at + k, vectors), :] = field[tile(jnp.maximum(asked[peer, k], 0), vectors), :]
        for k in range(2 * CAP):
            message[tile(at + CAP + k, vectors), :] = split[tile(peer * (2 * CAP) + k, vectors), :]
        return carry

    lax.fori_loop(0, groups, send, 0)


def reply(asked, field, split, vectors):
    groups = lax.axis_size("curve")
    return pl.pallas_call(
        functools.partial(reply_kernel, vectors, groups),
        out_shape=shaped((groups * 3 * CAP * vectors, field.shape[1]), bf16),
        in_specs=[smem()] + [vmem()] * 2,
        out_specs=vmem(),
        compiler_params=params(16),
        name="reply",
    )(asked, in_hbm(field), split)


class Stream:
    def __init__(self, blocks, diag, held, held_diag, sems):
        self.blocks, self.diag, self.held, self.held_diag, self.sems = blocks, diag, held, held_diag, sems
        self.pieces = blocks.shape[0] // UNROLL
        self.own = diag.shape[0] // self.pieces

    def copies(self, piece):
        rows = pl.ds(piece * UNROLL, UNROLL)
        own = pl.ds(piece * self.own, self.own)
        return (
            pltpu.make_async_copy(self.blocks.at[rows, 0], self.held.at[rows], self.sems.at[0, piece]),
            pltpu.make_async_copy(self.diag.at[own], self.held_diag.at[own], self.sems.at[1, piece]),
        )

    def start(self):
        for piece in range(self.pieces):
            for copy in self.copies(piece):
                copy.start()

    def wait(self, piece):
        for copy in self.copies(piece):
            copy.wait()


def stream_scratch(blocks, diag):
    rows, node = blocks.shape[0], blocks.shape[-1]
    return [
        pltpu.VMEM((rows, node, node), bf16),
        pltpu.VMEM(diag.shape, bf16),
        pltpu.SemaphoreType.DMA((2, rows // UNROLL)),
    ]


def products(vectors, limit, pick, target, field, stream, total):
    band = lax.axis_index("band")

    def some(piece, carry):
        stream.wait(piece)
        forward, mirrored = [], []
        base = piece * UNROLL
        for u in range(UNROLL):
            row = base + u
            block = stream.held[row]
            source = pick[0, row]
            if limit is not None:
                source = jnp.minimum(source, limit)
            forward.append(times_transposed(field[tile(source, vectors), :], block))
            mirrored.append(times(field[tile(row, vectors), :], block))
        for u in range(UNROLL):
            total[tile(base + u, vectors), :] += forward[u]
            total[tile(target[0, base + u], vectors), :] += mirrored[u]
        own = stream.own
        first = band * (own * stream.pieces) + piece * own
        values = [times(field[tile(first + d, vectors), :], stream.held_diag[piece * own + d]) for d in range(own)]
        for d, value in enumerate(values):
            total[tile(first + d, vectors), :] += value
        return carry

    lax.fori_loop(0, stream.pieces, some, 0)


def give_out(rows, vectors, total, outs):
    core = core_of(lax.axis_index("band"))
    half = rows // 2
    size = half // CHUNKS * vectors
    for side in range(2):
        start = jnp.where(core == side, 0, half) * vectors
        for c in range(CHUNKS):
            outs[side * CHUNKS + c][...] = total[pl.ds(pl.multiple_of(start + c * size, size), size), :]


def local_kernel(rows, vectors, pick, target, field, state, blocks, diag, total, *scratch):
    stream = Stream(blocks, diag, *scratch)
    stream.start()
    total[...] = jnp.zeros_like(total)
    width = state.shape[0]
    band = lax.axis_index("band")
    for v in range(width):
        total[pl.ds(band * width + v, rows, stride=vectors), :] = nonlinear(state[v])
    products(vectors, rows, pick, target, field, stream, total)


def operate_local(pick, target, field, state, blocks, diag):
    rows, node = blocks.shape[0], blocks.shape[-1]
    vectors = field.shape[0] // (rows + 1)
    return pl.pallas_call(
        functools.partial(local_kernel, rows, vectors),
        out_shape=shaped(((rows + 1) * vectors, node), f32),
        in_specs=[smem()] * 2 + [vmem()] * 2 + [anywhere()] * 2,
        out_specs=vmem(),
        scratch_shapes=stream_scratch(blocks, diag),
        compiler_params=params(20),
        name="operate_local",
    )(pick, target, in_hbm(field), state, blocks, diag)


def settle_kernel(rows, vectors, groups, wanted, origin, asked, local, halo, own, *refs):
    outs, total = refs[:-1], refs[-1]
    total[...] = local[...]

    def some(peer, carry):
        at = peer * (3 * CAP)
        values = []
        for k in range(CAP):
            value = times_transposed(halo[tile(at + k, vectors), :], own[peer * CAP + k])
            values.append((jnp.where(wanted[peer, k] < 0, rows, origin[peer, k]), value))
        for k in range(CAP):
            value = halo[tile(at + CAP + k, vectors), :].astype(f32)
            value = value + halo[tile(at + 2 * CAP + k, vectors), :].astype(f32)
            values.append((jnp.where(asked[peer, k] < 0, rows, asked[peer, k]), value))
        for aim, value in values:
            total[tile(aim, vectors), :] += value
        return carry

    lax.fori_loop(0, groups, some, 0)
    give_out(rows, vectors, total, outs)


def chunk_shapes(rows, vectors, node):
    return [shaped((rows // 2 // CHUNKS * vectors, node), f32)] * (2 * CHUNKS)


def settle(wanted, origin, asked, local, halo, own, rows):
    node = local.shape[1]
    vectors = local.shape[0] // (rows + 1)
    groups = lax.axis_size("curve")
    outs = pl.pallas_call(
        functools.partial(settle_kernel, rows, vectors, groups),
        out_shape=chunk_shapes(rows, vectors, node),
        in_specs=[smem()] * 3 + [vmem()] * 3,
        out_specs=[vmem()] * (2 * CHUNKS),
        scratch_shapes=[pltpu.VMEM(local.shape, f32)],
        compiler_params=params(20),
        name="settle",
    )(wanted, origin, asked, local, halo, own)
    return outs[:CHUNKS], outs[CHUNKS:]


def second_kernel(rows, vectors, groups, pick, target, asked, *refs):
    arrays, (halo, arrived, blocks, diag), refs = refs[: 2 * CHUNKS], refs[2 * CHUNKS : 2 * CHUNKS + 4], refs[2 * CHUNKS + 4 :]
    outs, (scale, field, total), scratch = refs[: 2 * CHUNKS], refs[2 * CHUNKS : 2 * CHUNKS + 3], refs[2 * CHUNKS + 3 :]
    stream = Stream(blocks, diag, *scratch)
    stream.start()
    half = rows // 2
    each = half // CHUNKS
    message = halo.shape[0] // groups
    shape = scale.shape
    line = jnp.zeros((1, shape[1]), f32)
    for g in range(groups):
        at = g * message + 2 * CAP * vectors
        line = line + halo[at : at + 1, :]
    energy = as_column(line, shape)
    beta = jnp.sqrt(energy + epsilon)
    scale[...] = beta
    inverse = 1.0 / beta
    core = core_of(lax.axis_index("band"))
    for side in range(2):
        start = jnp.where(core == side, 0, half)
        for c in range(CHUNKS):
            array = arrays[side * CHUNKS + c]

            def one(p, carry, start=start, c=c, array=array):
                field[tile(start + c * each + p, vectors), :] = (array[tile(p, vectors), :] * inverse).astype(bf16)
                return carry

            lax.fori_loop(0, each, one, 0, unroll=16)

    def row(g, carry):
        for k in range(2 * CAP):
            at = pl.multiple_of(g * message + k * vectors, 8)
            value = halo[pl.ds(at, vectors), :] * inverse
            field[tile(rows + g * (2 * CAP) + k, vectors), :] = value.astype(bf16)
        return carry

    lax.fori_loop(0, groups, row, 0)
    total[...] = jnp.zeros_like(total)
    products(vectors, None, pick, target, field, stream, total)

    def some(peer, carry):
        values = []
        for k in range(CAP):
            place = rows + peer * (2 * CAP) + CAP + k
            aim = asked[peer, k]
            value = times(field[tile(place, vectors), :], arrived[peer * CAP + k])
            values.append((jnp.where(aim < 0, rows, aim), value))
        for aim, value in values:
            total[tile(aim, vectors), :] += value
        return carry

    lax.fori_loop(0, groups, some, 0)
    give_out(rows, vectors, total, outs)


def operate_second(pick, target, asked, arrays, halo, arrived, blocks, diag):
    rows, node = blocks.shape[0], blocks.shape[-1]
    groups = lax.axis_size("curve")
    message = halo.shape[0] // groups
    vectors = (message - 8) // (2 * CAP)
    outs = pl.pallas_call(
        functools.partial(second_kernel, rows, vectors, groups),
        out_shape=chunk_shapes(rows, vectors, node) + [shaped((vectors, node), f32)],
        in_specs=[smem()] * 3 + [vmem()] * (2 * CHUNKS + 2) + [anywhere()] * 2,
        out_specs=[vmem()] * (2 * CHUNKS + 1),
        scratch_shapes=[
            pltpu.VMEM(((rows + groups * 2 * CAP) * vectors, node), bf16),
            pltpu.VMEM(((rows + 1) * vectors, node), f32),
        ]
        + stream_scratch(blocks, diag),
        compiler_params=params(22),
        name="operate_second",
    )(pick, target, asked, *arrays, halo, arrived, blocks, diag)
    return outs[:CHUNKS], outs[CHUNKS : 2 * CHUNKS], outs[-1]


def third_kernel(rows, vectors, groups, width, pick, wanted, origin, *refs):
    count = 2 * CHUNKS
    drive, image, (own, blocks, diag), refs = refs[:count], refs[count : 2 * count], refs[2 * count : 2 * count + 3], refs[2 * count + 3 :]
    form, left, drive_own, image_own, field = refs[:5]
    stream = Stream(blocks, diag, *refs[5:])
    stream.start()
    half = rows // 2
    each = half // CHUNKS
    shape = form.shape
    band = lax.axis_index("band")
    core = core_of(band)
    for side in range(2):
        start = jnp.where(core == side, 0, half)
        for c in range(CHUNKS):
            array = image[side * CHUNKS + c]

            def one(p, carry, start=start, c=c, array=array):
                field[tile(start + c * each + p, vectors), :] = array[tile(p, vectors), :].astype(bf16)
                return carry

            lax.fori_loop(0, each, one, 0, unroll=16)
            for v in range(width):
                inside = pl.ds(pl.multiple_of(start + c * each, each), each)
                source = pl.ds(band * width + v, each, stride=vectors)
                drive_own[v, inside, :] = drive[side * CHUNKS + c][source, :]
                image_own[v, inside, :] = array[source, :]
    field[rows * vectors :, :] = jnp.zeros((vectors, shape[1]), bf16)

    def some(piece, parts):
        stream.wait(piece)
        twice, once = parts
        base = piece * UNROLL
        for u in range(UNROLL):
            row = base + u
            value = times(field[tile(row, vectors), :], stream.held[row])
            source = jnp.minimum(pick[0, row], rows)
            twice = twice + value * field[tile(source, vectors), :].astype(f32)
        for d in range(stream.own):
            row = (band * stream.pieces + piece) * stream.own + d
            here = field[tile(row, vectors), :]
            once = once + times(here, stream.held_diag[piece * stream.own + d]) * here.astype(f32)
        return twice, once

    nothing = jnp.zeros(shape, f32)
    twice, once = lax.fori_loop(0, stream.pieces, some, (nothing, nothing))
    form[...] = 2.0 * twice + once

    def remote(peer, carry):
        for k in range(CAP):
            value = times(field[tile(origin[peer, k], vectors), :], own[peer * CAP + k])
            left[tile(peer * CAP + k, vectors), :] = jnp.where(wanted[peer, k] < 0, 0.0, 2.0) * value
        return carry

    lax.fori_loop(0, groups, remote, 0)


def operate_third(pick, wanted, origin, drive, image, own, blocks, diag, width, vectors):
    rows, node = blocks.shape[0], blocks.shape[-1]
    groups = lax.axis_size("curve")
    mine = pltpu.HBM((width, rows, node), f32)
    return pl.pallas_call(
        functools.partial(third_kernel, rows, vectors, groups, width),
        out_shape=[shaped((vectors, node), f32), shaped((groups * CAP * vectors, node), f32), mine, mine],
        in_specs=[smem()] * 3 + [vmem()] * (4 * CHUNKS + 1) + [anywhere()] * 2,
        out_specs=[vmem()] * 4,
        scratch_shapes=[pltpu.VMEM(((rows + 1) * vectors, node), bf16)] + stream_scratch(blocks, diag),
        compiler_params=params(22),
        name="operate_third",
    )(pick, wanted, origin, *drive, *image[:CHUNKS], *map(in_hbm, image[CHUNKS:]), own, blocks, diag)


def tail_kernel(each, vectors, form, left, halo, *refs):
    image, share = refs[:-1], refs[-1]
    shape = form.shape
    total = form[...]
    for slot in range(left.shape[0] // vectors):
        at = slot * vectors
        total = total + left[at : at + vectors, :] * halo[at : at + vectors, :].astype(f32)
    values = [total]
    for e in range(2):
        at = (each + e) * vectors
        value = image[0][at : at + vectors, :]
        for other in image[1:]:
            value = value + other[at : at + vectors, :]
        values.append(0.5 * value)
    line = jnp.zeros((1, shape[1]), f32)
    across = lax.broadcasted_iota(i32, shape, 1)
    down = lax.broadcasted_iota(i32, shape, 0)
    for e, value in enumerate(values):
        column = jnp.broadcast_to(row_sum(value), shape)
        line = line + jnp.sum(jnp.where(across == down + e * vectors, column, 0.0), axis=0, keepdims=True)
    share[...] = jnp.broadcast_to(line, share.shape)


def tail(form, left, halo, image, devices):
    vectors, node = form.shape
    each = image[0].shape[0] // vectors - 2
    return pl.pallas_call(
        functools.partial(tail_kernel, each, vectors),
        out_shape=shaped((devices, node), f32),
        in_specs=[vmem()] * (3 + len(image)),
        out_specs=vmem(),
        compiler_params=params(16),
        name="tail",
    )(form, left, halo, *image)


def code_tiles(each, node):
    return -(-each // node)


def encode_kernel(each, vectors, keep, came, code, wide):
    node = keep.shape[1]
    lanes = lax.broadcasted_iota(i32, (vectors, node), 1)
    for group in range(code_tiles(each, node)):
        inside = range(group * node, min(each, (group + 1) * node))
        peak = jnp.zeros((vectors, node), f32)
        for p in inside:
            at = p * vectors
            value = keep[at : at + vectors, :] + came[at : at + vectors, :]
            wide[at : at + vectors, :] = value
            peak = jnp.where(lanes == p - group * node, jnp.max(jnp.abs(value), axis=1, keepdims=True), peak)
        power = jnp.ceil(jnp.log2(jnp.maximum(peak, 1e-30)) * STEP) + 1.0
        start = (each + group) * vectors
        code[start : start + vectors, :] = power.astype(i32).astype(jnp.int16)
        gain = FULL * jnp.exp2(power * (-1.0 / STEP))
        for p in inside:
            at = p * vectors
            lane = p - group * node
            scaled = wide[at : at + vectors, :] * gain[:, lane : lane + 1]
            code[at : at + vectors, :] = jnp.round(scaled).astype(i32).astype(jnp.int16)


def encode(keep, came, vectors):
    size, node = keep.shape
    each = size // vectors
    return pl.pallas_call(
        functools.partial(encode_kernel, each, vectors),
        out_shape=shaped(((each + code_tiles(each, node)) * vectors, node), jnp.int16),
        in_specs=[vmem()] * 2,
        out_specs=vmem(),
        scratch_shapes=[pltpu.VMEM((size, node), f32)],
        compiler_params=params(12),
        name="encode",
    )(keep, came)


def decode_kernel(each, vectors, weighted, *refs):
    if weighted:
        code, came, drive, out = refs
    else:
        code, came, out = refs
    node = code.shape[1]
    shape = (vectors, node)
    energy = jnp.zeros(shape, f32)
    cross = jnp.zeros(shape, f32)
    for group in range(code_tiles(each, node)):
        start = (each + group) * vectors
        gains = [
            jnp.exp2(ref[start : start + vectors, :].astype(i32).astype(f32) * (1.0 / STEP)) * (1.0 / FULL)
            for ref in (code, came)
        ]
        for p in range(group * node, min(each, (group + 1) * node)):
            at = p * vectors
            lane = p - group * node
            one, two = [
                ref[at : at + vectors, :].astype(i32).astype(f32) * gain[:, lane : lane + 1]
                for ref, gain in zip((code, came), gains)
            ]
            value = one + two
            out[at : at + vectors, :] = value
            energy = energy + value * value
            if weighted:
                cross = cross + value * drive[at : at + vectors, :]
    at = each * vectors
    if weighted:
        out[at : at + vectors, :] = cross
        at = at + vectors
    out[at : at + vectors, :] = energy


def decode(code, came, vectors, each, drive=None):
    node = code.shape[1]
    extra = 1 if drive is None else 2
    inputs = (code, came) if drive is None else (code, came, drive)
    return pl.pallas_call(
        functools.partial(decode_kernel, each, vectors, drive is not None),
        out_shape=shaped(((each + extra) * vectors, node), f32),
        in_specs=[vmem()] * len(inputs),
        out_specs=vmem(),
        compiler_params=params(12),
        name="decode",
    )(*inputs)


def fetch_row(arrays, each, vectors, row):
    core = core_of(lax.axis_index("band"))
    half = each * CHUNKS
    side = row // half
    inside = row - side * half
    chunk = inside // each
    place = tile(inside - chunk * each, vectors)
    value = arrays[0][place, :]
    number = jnp.where(side == core, chunk, CHUNKS + chunk)
    for k in range(1, 2 * CHUNKS):
        value = jnp.where(number == k, arrays[k][place, :], value)
    return value


def pack_kernel(each, vectors, groups, asked, origin, *refs):
    arrays, message = refs[:-1], refs[-1]
    shape = (vectors, message.shape[1])
    sums = arrays[0][each * vectors :, :]
    for array in arrays[1:]:
        sums = sums + array[each * vectors :, :]
    line = jnp.broadcast_to(as_line(row_sum(sums), shape), shape)[0:8, :]
    size = 2 * CAP * vectors + 8

    def send(peer, carry):
        for k in range(2 * CAP):
            row = jnp.maximum(asked[peer, k], 0) if k < CAP else origin[peer, k - CAP]
            at = pl.multiple_of(peer * size + k * vectors, 8)
            message[pl.ds(at, vectors), :] = fetch_row(arrays, each, vectors, row)
        message[pl.ds(pl.multiple_of(peer * size + 2 * CAP * vectors, 8), 8), :] = line
        return carry

    lax.fori_loop(0, groups, send, 0)


def pack(asked, origin, arrays, vectors):
    node = arrays[0].shape[1]
    each = arrays[0].shape[0] // vectors - 1
    groups = lax.axis_size("curve")
    return pl.pallas_call(
        functools.partial(pack_kernel, each, vectors, groups),
        out_shape=shaped((groups * (2 * CAP * vectors + 8), node), f32),
        in_specs=[smem()] * 2 + [vmem()] * (2 * CHUNKS),
        out_specs=vmem(),
        compiler_params=params(16),
        name="pack",
    )(asked, origin, *arrays)


def pack_rounded_kernel(each, vectors, groups, asked, *refs):
    arrays, message = refs[:-1], refs[-1]

    def send(peer, carry):
        for k in range(CAP):
            value = fetch_row(arrays, each, vectors, jnp.maximum(asked[peer, k], 0))
            message[tile(peer * CAP + k, vectors), :] = value.astype(bf16)
        return carry

    lax.fori_loop(0, groups, send, 0)


def pack_rounded(asked, arrays, vectors):
    node = arrays[0].shape[1]
    each = arrays[0].shape[0] // vectors - 2
    groups = lax.axis_size("curve")
    return pl.pallas_call(
        functools.partial(pack_rounded_kernel, each, vectors, groups),
        out_shape=shaped((groups * CAP * vectors, node), bf16),
        in_specs=[smem()] + [vmem()] * (2 * CHUNKS),
        out_specs=vmem(),
        compiler_params=params(16),
        name="pack_rounded",
    )(asked, *arrays)


def finish_kernel(shares, scale, state, drive, image, out, one, two, lift, mix):
    shape = scale.shape
    vectors = shape[0]
    line = jnp.sum(shares[...], axis=0, keepdims=True)
    form, cross, energy = [as_column(line, shape, e * vectors) for e in range(3)]
    beta_zero = scale[...]
    unit = 1.0 - epsilon / (beta_zero * beta_zero)
    alpha_first = cross / beta_zero
    square = alpha_first * alpha_first
    beta_first = jnp.sqrt(jnp.maximum(energy - square * (2.0 - unit), 0.0) + epsilon)
    alpha_second = (form - 2.0 * alpha_first * energy + square * alpha_first) / (beta_first * beta_first)
    alpha_second = alpha_second - alpha_first * (1.0 - unit)
    term_one = jnp.ones(shape, f32)
    term_two = jnp.zeros(shape, f32)
    total_one, total_two = term_one, term_two
    for turn in range(1, TAYLOR):
        factor = time_step / (turn + 1.0)
        next_one = factor * (alpha_first * term_one + beta_first * term_two)
        next_two = factor * (beta_first * term_one + alpha_second * term_two)
        term_one, term_two = next_one, next_two
        total_one, total_two = total_one + next_one, total_two + next_two
    one[...] = time_step * total_one
    two[...] = time_step * beta_zero * total_two / beta_first
    mix[...] = alpha_first / beta_zero
    width = state.shape[0]
    for v in range(width):
        at = pl.ds(lax.axis_index("band") * width + v, 1)
        size = state.shape[1:]
        weight_one, weight_two, share = [jnp.broadcast_to(ref[at, :], size) for ref in (one, two, mix)]
        out[v] = state[v] + (weight_one * drive[v] + weight_two * (image[v] - share * drive[v]))


def finish(shares, scale, state, drive, image):
    return pl.pallas_call(
        finish_kernel,
        out_shape=shaped(state.shape, f32),
        in_specs=[vmem()] * 5,
        out_specs=vmem(),
        scratch_shapes=[pltpu.VMEM(scale.shape, f32)] * 4,
        compiler_params=params(16),
        name="finish",
    )(shares, scale, state, in_hbm(drive), in_hbm(image))


def swap(array, bit):
    size = lax.axis_size("band")
    return lax.ppermute(array, "band", [(k, k ^ bit) for k in range(size)])


def exchange(array):
    return lax.all_to_all(array, "curve", split_axis=0, concat_axis=0, tiled=True)


def band_sum(keep, give, vectors, drive=None):
    each = keep[0].shape[0] // vectors
    came = [swap(array, 1) for array in give]
    codes = [encode(one, two, vectors) for one, two in zip(keep, came)]
    across = [swap(code, 2) for code in codes]
    mine = [
        decode(code, other, vectors, each, None if drive is None else drive[c])
        for c, (code, other) in enumerate(zip(codes, across))
    ]
    return mine + [swap(array, 1) for array in mine]


def body(state, blocks, diag_blocks, block_cols):
    groups = lax.axis_size("curve")
    devices = groups * lax.axis_size("band")
    width, rows = state.shape[:2]
    vectors = width * lax.axis_size("band")
    blocks = in_hbm(blocks)
    diag_blocks = in_hbm(diag_blocks)
    rounded = state.astype(bf16)
    state = in_hbm(state)
    across = swap(rounded, 2)
    parts = [rounded, swap(rounded, 1), across, swap(across, 1)]
    pick, target, wanted, origin = plan(block_cols.reshape(1, rows))
    asked = exchange(wanted)
    field, own, split = spread(parts, origin, blocks)
    message = reply(asked, field, split, vectors)
    halo = exchange(message)
    local = operate_local(pick, target, field, state, blocks, diag_blocks)
    keep, give = settle(wanted, origin, asked, local, halo, own, rows)
    drive = band_sum(keep, give, vectors)
    arrived = exchange(own)
    halo = exchange(pack(asked, origin, drive, vectors))
    keep, give, scale = operate_second(pick, target, asked, drive, halo, arrived, blocks, diag_blocks)
    image = band_sum(keep, give, vectors, drive)
    halo = exchange(pack_rounded(asked, image, vectors))
    form, left, drive_own, image_own = operate_third(
        pick, wanted, origin, drive, image, own, blocks, diag_blocks, width, vectors
    )
    share = tail(form, left, halo, image[:CHUNKS], devices)
    shares = lax.all_to_all(share, ("curve", "band"), split_axis=0, concat_axis=0, tiled=True)
    return finish(shares, scale, state, drive_own, image_own)


def solution(mesh):
    return jax.shard_map(
        body,
        mesh=mesh,
        in_specs=(
            P("band", "curve", None),
            P("curve", "band", None, None),
            P(("curve", "band"), None, None),
            P("curve", "band"),
        ),
        out_specs=P("band", "curve", None),
        check_vma=False,
    )
```

```python
import functools

import jax
import jax.numpy as jnp
from jax import lax
from jax.experimental import pallas as pl
from jax.experimental.pallas import tpu as pltpu
from jax.sharding import PartitionSpec as P


CAP = 2
TAYLOR = 16
UNROLL = 32
CHUNKS = 2

epsilon = 1e-06
time_step = 0.5
quadratic = 1.0
STEP = 256.0
FULL = 32767.0

f32 = jnp.float32
bf16 = jnp.bfloat16
i32 = jnp.int32


def nonlinear(field):
    return quadratic * field * field - field * field * field


def tile(index, rows):
    return pl.ds(pl.multiple_of(index * rows, rows), rows)


def smem():
    return pl.BlockSpec(memory_space=pltpu.SMEM)


def vmem():
    return pl.BlockSpec(memory_space=pltpu.VMEM)


def anywhere():
    return pl.BlockSpec(memory_space=pltpu.HBM)


def params(mebibytes):
    return pltpu.CompilerParams(vmem_limit_bytes=mebibytes * 1024 * 1024)


def in_hbm(array):
    return pltpu.with_memory_space_constraint(array, pltpu.HBM)


def shaped(shape, dtype):
    return jax.ShapeDtypeStruct(shape, dtype)


def times(field, block):
    return lax.dot_general(field, block, (((1,), (0,)), ((), ())), preferred_element_type=f32)


def times_transposed(field, block):
    return lax.dot_general(field, block, (((1,), (1,)), ((), ())), preferred_element_type=f32)


def two(one, other):
    nothing = jnp.zeros_like(one)
    upper = jnp.concatenate([one, nothing], axis=1)
    return jnp.concatenate([upper, jnp.concatenate([nothing, other], axis=1)], axis=0)


def times_two(one, other, blocks):
    value = times(two(one, other), blocks.reshape(-1, blocks.shape[-1]))
    return value[: one.shape[0]], value[one.shape[0] :]


def times_two_transposed(one, other, first, second):
    value = times(two(one, other), jnp.concatenate([first.T, second.T], axis=0))
    return value[: one.shape[0]], value[one.shape[0] :]


def row_sum(part):
    return jnp.sum(part, axis=1, keepdims=True)


def as_line(column, shape):
    across = lax.broadcasted_iota(i32, shape, 1)
    down = lax.broadcasted_iota(i32, shape, 0)
    return jnp.sum(jnp.where(across == down, jnp.broadcast_to(column, shape), 0.0), axis=0, keepdims=True)


def as_column(line, shape, offset=0):
    across = lax.broadcasted_iota(i32, shape, 1)
    down = lax.broadcasted_iota(i32, shape, 0)
    picked = jnp.where(across == down + offset, jnp.broadcast_to(line, shape), 0.0)
    return jnp.broadcast_to(row_sum(picked), shape)


def core_of(band):
    return jnp.bitwise_and(band, 1)


def plan_kernel(cols, pick, target, wanted, origin):
    groups, lanes = wanted.shape
    rows = cols.shape[1]
    here = lax.axis_index("curve")
    column = cols[...]
    owner = column // rows
    inner = column - owner * rows
    shape = (groups, rows)
    peer = lax.broadcasted_iota(i32, shape, 0)
    place = lax.broadcasted_iota(i32, shape, 1).astype(f32)
    inside = jnp.broadcast_to(inner.astype(f32), shape)
    left = (jnp.broadcast_to(owner, shape) == peer) & (peer != here)
    number = jnp.zeros((1, rows), f32)
    lane = lax.broadcasted_iota(i32, (groups, lanes), 1)
    want = jnp.full((groups, lanes), -1.0, f32)
    source = jnp.zeros((groups, lanes), f32)
    none = float(rows)
    for k in range(CAP):
        least = jnp.min(jnp.where(left, place, none), axis=1, keepdims=True)
        hit = left & (place == least)
        left = left & (place != least)
        aim = row_sum(jnp.where(hit, inside, 0.0))
        want = jnp.where((lane == k) & (least < none), aim, want)
        source = jnp.where((lane == k) & (least < none), least, source)
        slot = (peer * (2 * CAP) + k).astype(f32)
        number = number + jnp.sum(jnp.where(hit, slot, 0.0), axis=0, keepdims=True)
    wanted[...] = want.astype(i32)
    origin[...] = source.astype(i32)
    pick[...] = jnp.where(owner == here, inner, rows + number.astype(i32))
    target[...] = jnp.where(owner == here, inner, rows)


def plan(cols):
    rows = cols.shape[1]
    groups = lax.axis_size("curve")
    return pl.pallas_call(
        plan_kernel,
        out_shape=[shaped((1, rows), i32)] * 2 + [shaped((groups, 128), i32)] * 2,
        in_specs=[vmem()],
        out_specs=[vmem()] * 4,
        compiler_params=params(8),
        name="plan",
    )(cols)


def spread_kernel(rows, vectors, groups, width, origin, blocks, *refs):
    count = vectors // width
    parts, (field, own, split, wide, sems) = refs[:count], refs[count:]
    slots = groups * CAP

    def fetch(slot):
        peer = slot // CAP
        row = origin[peer, slot - peer * CAP]
        return pltpu.make_async_copy(blocks.at[row, 0], own.at[slot], sems.at[slot])

    def begin(slot, carry):
        fetch(slot).start()
        return carry

    lax.fori_loop(0, slots, begin, 0)
    band = lax.axis_index("band")
    for k, part in enumerate(parts):
        start = jnp.bitwise_xor(band, k) * width
        for v in range(width):
            wide[pl.ds(start + v, rows, stride=vectors), :] = part[v].astype(f32)
    field[0 : rows * vectors, :] = wide[...].astype(bf16)
    field[rows * vectors :, :] = jnp.zeros((vectors, field.shape[1]), bf16)

    def end(slot, carry):
        fetch(slot).wait()
        return carry

    lax.fori_loop(0, slots, end, 0)

    def product(peer, carry):
        for k in range(CAP):
            value = times(field[tile(origin[peer, k], vectors), :], own[peer * CAP + k])
            high = value.astype(bf16)
            split[tile(peer * (2 * CAP) + k, vectors), :] = high
            split[tile(peer * (2 * CAP) + CAP + k, vectors), :] = (value - high.astype(f32)).astype(bf16)
        return carry

    lax.fori_loop(0, groups, product, 0)


def spread(parts, origin, blocks):
    width, rows, node = parts[0].shape
    groups = lax.axis_size("curve")
    slots = groups * CAP
    vectors = width * len(parts)
    return pl.pallas_call(
        functools.partial(spread_kernel, rows, vectors, groups, width),
        out_shape=[
            pltpu.HBM(((rows + 1) * vectors, node), bf16),
            shaped((slots, node, node), bf16),
            shaped((slots * 2 * vectors, node), bf16),
        ],
        in_specs=[smem(), anywhere()] + [vmem()] * len(parts),
        out_specs=[vmem()] * 3,
        scratch_shapes=[pltpu.VMEM((rows * vectors, node), f32), pltpu.SemaphoreType.DMA((slots,))],
        compiler_params=params(16),
        name="spread",
    )(origin, blocks, *parts)


def reply_kernel(vectors, groups, asked, field, split, message):
    def send(peer, carry):
        at = peer * (3 * CAP)
        for k in range(CAP):
            message[tile(at + k, vectors), :] = field[tile(jnp.maximum(asked[peer, k], 0), vectors), :]
        for k in range(2 * CAP):
            message[tile(at + CAP + k, vectors), :] = split[tile(peer * (2 * CAP) + k, vectors), :]
        return carry

    lax.fori_loop(0, groups, send, 0)


def reply(asked, field, split, vectors):
    groups = lax.axis_size("curve")
    return pl.pallas_call(
        functools.partial(reply_kernel, vectors, groups),
        out_shape=shaped((groups * 3 * CAP * vectors, field.shape[1]), bf16),
        in_specs=[smem()] + [vmem()] * 2,
        out_specs=vmem(),
        compiler_params=params(16),
        name="reply",
    )(asked, in_hbm(field), split)


class Stream:
    def __init__(self, blocks, diag, held, held_diag, sems):
        self.blocks, self.diag, self.held, self.held_diag, self.sems = blocks, diag, held, held_diag, sems
        self.pieces = blocks.shape[0] // UNROLL
        self.own = diag.shape[0] // self.pieces

    def copies(self, piece):
        rows = pl.ds(piece * UNROLL, UNROLL)
        own = pl.ds(piece * self.own, self.own)
        return (
            pltpu.make_async_copy(self.blocks.at[rows, 0], self.held.at[rows], self.sems.at[0, piece]),
            pltpu.make_async_copy(self.diag.at[own], self.held_diag.at[own], self.sems.at[1, piece]),
        )

    def start(self):
        for piece in range(self.pieces):
            for copy in self.copies(piece):
                copy.start()

    def wait(self, piece):
        for copy in self.copies(piece):
            copy.wait()


def stream_scratch(blocks, diag):
    rows, node = blocks.shape[0], blocks.shape[-1]
    return [
        pltpu.VMEM((rows, node, node), bf16),
        pltpu.VMEM(diag.shape, bf16),
        pltpu.SemaphoreType.DMA((2, rows // UNROLL)),
    ]


def products(vectors, limit, pick, target, field, stream, total):
    band = lax.axis_index("band")

    def at(row):
        return field[tile(row, vectors), :]

    def source(row):
        place = pick[0, row]
        return at(place if limit is None else jnp.minimum(place, limit))

    def some(piece, carry):
        stream.wait(piece)
        forward, mirrored = [], []
        base = piece * UNROLL
        for u in range(0, UNROLL, 2):
            row = base + u
            forward += times_two_transposed(source(row), source(row + 1), stream.held[row], stream.held[row + 1])
            mirrored += times_two(at(row), at(row + 1), stream.held[pl.ds(row, 2)])
        own = stream.own
        first = band * (own * stream.pieces) + piece * own
        values = []
        for d in range(0, own, 2):
            values += times_two(at(first + d), at(first + d + 1), stream.held_diag[pl.ds(piece * own + d, 2)])
        for u in range(UNROLL):
            total[tile(base + u, vectors), :] += forward[u]
            total[tile(target[0, base + u], vectors), :] += mirrored[u]
        for d, value in enumerate(values):
            total[tile(first + d, vectors), :] += value
        return carry

    lax.fori_loop(0, stream.pieces, some, 0)


def give_out(rows, vectors, total, outs):
    core = core_of(lax.axis_index("band"))
    half = rows // 2
    size = half // CHUNKS * vectors
    for side in range(2):
        start = jnp.where(core == side, 0, half) * vectors
        for c in range(CHUNKS):
            outs[side * CHUNKS + c][...] = total[pl.ds(pl.multiple_of(start + c * size, size), size), :]


def local_kernel(rows, vectors, pick, target, field, state, blocks, diag, total, *scratch):
    stream = Stream(blocks, diag, *scratch)
    stream.start()
    total[...] = jnp.zeros_like(total)
    width = state.shape[0]
    band = lax.axis_index("band")
    for v in range(width):
        total[pl.ds(band * width + v, rows, stride=vectors), :] = nonlinear(state[v])
    products(vectors, rows, pick, target, field, stream, total)


def operate_local(pick, target, field, state, blocks, diag):
    rows, node = blocks.shape[0], blocks.shape[-1]
    vectors = field.shape[0] // (rows + 1)
    return pl.pallas_call(
        functools.partial(local_kernel, rows, vectors),
        out_shape=shaped(((rows + 1) * vectors, node), f32),
        in_specs=[smem()] * 2 + [vmem()] * 2 + [anywhere()] * 2,
        out_specs=vmem(),
        scratch_shapes=stream_scratch(blocks, diag),
        compiler_params=params(20),
        name="operate_local",
    )(pick, target, in_hbm(field), state, blocks, diag)


def settle_kernel(rows, vectors, groups, wanted, origin, asked, local, halo, own, *refs):
    outs, total = refs[:-1], refs[-1]
    total[...] = local[...]

    def some(peer, carry):
        at = peer * (3 * CAP)
        values = []
        for k in range(CAP):
            value = times_transposed(halo[tile(at + k, vectors), :], own[peer * CAP + k])
            values.append((jnp.where(wanted[peer, k] < 0, rows, origin[peer, k]), value))
        for k in range(CAP):
            value = halo[tile(at + CAP + k, vectors), :].astype(f32)
            value = value + halo[tile(at + 2 * CAP + k, vectors), :].astype(f32)
            values.append((jnp.where(asked[peer, k] < 0, rows, asked[peer, k]), value))
        for aim, value in values:
            total[tile(aim, vectors), :] += value
        return carry

    lax.fori_loop(0, groups, some, 0)
    give_out(rows, vectors, total, outs)


def chunk_shapes(rows, vectors, node):
    return [shaped((rows // 2 // CHUNKS * vectors, node), f32)] * (2 * CHUNKS)


def settle(wanted, origin, asked, local, halo, own, rows):
    node = local.shape[1]
    vectors = local.shape[0] // (rows + 1)
    groups = lax.axis_size("curve")
    outs = pl.pallas_call(
        functools.partial(settle_kernel, rows, vectors, groups),
        out_shape=chunk_shapes(rows, vectors, node),
        in_specs=[smem()] * 3 + [vmem()] * 3,
        out_specs=[vmem()] * (2 * CHUNKS),
        scratch_shapes=[pltpu.VMEM(local.shape, f32)],
        compiler_params=params(20),
        name="settle",
    )(wanted, origin, asked, local, halo, own)
    return outs[:CHUNKS], outs[CHUNKS:]


def second_kernel(rows, vectors, groups, pick, target, asked, *refs):
    arrays, (halo, arrived, blocks, diag), refs = refs[: 2 * CHUNKS], refs[2 * CHUNKS : 2 * CHUNKS + 4], refs[2 * CHUNKS + 4 :]
    outs, (scale, field, total), scratch = refs[: 2 * CHUNKS], refs[2 * CHUNKS : 2 * CHUNKS + 3], refs[2 * CHUNKS + 3 :]
    stream = Stream(blocks, diag, *scratch)
    stream.start()
    half = rows // 2
    each = half // CHUNKS
    message = halo.shape[0] // groups
    shape = scale.shape
    line = jnp.zeros((1, shape[1]), f32)
    for g in range(groups):
        at = g * message + 2 * CAP * vectors
        line = line + halo[at : at + 1, :]
    energy = as_column(line, shape)
    beta = jnp.sqrt(energy + epsilon)
    scale[...] = beta
    inverse = 1.0 / beta
    core = core_of(lax.axis_index("band"))
    for side in range(2):
        start = jnp.where(core == side, 0, half)
        for c in range(CHUNKS):
            array = arrays[side * CHUNKS + c]

            def one(p, carry, start=start, c=c, array=array):
                field[tile(start + c * each + p, vectors), :] = (array[tile(p, vectors), :] * inverse).astype(bf16)
                return carry

            lax.fori_loop(0, each, one, 0, unroll=16)

    def row(g, carry):
        for k in range(2 * CAP):
            at = pl.multiple_of(g * message + k * vectors, 8)
            value = halo[pl.ds(at, vectors), :] * inverse
            field[tile(rows + g * (2 * CAP) + k, vectors), :] = value.astype(bf16)
        return carry

    lax.fori_loop(0, groups, row, 0)
    total[...] = jnp.zeros_like(total)
    products(vectors, None, pick, target, field, stream, total)

    def some(peer, carry):
        values = []
        for k in range(CAP):
            place = rows + peer * (2 * CAP) + CAP + k
            aim = asked[peer, k]
            value = times(field[tile(place, vectors), :], arrived[peer * CAP + k])
            values.append((jnp.where(aim < 0, rows, aim), value))
        for aim, value in values:
            total[tile(aim, vectors), :] += value
        return carry

    lax.fori_loop(0, groups, some, 0)
    give_out(rows, vectors, total, outs)


def operate_second(pick, target, asked, arrays, halo, arrived, blocks, diag):
    rows, node = blocks.shape[0], blocks.shape[-1]
    groups = lax.axis_size("curve")
    message = halo.shape[0] // groups
    vectors = (message - 8) // (2 * CAP)
    outs = pl.pallas_call(
        functools.partial(second_kernel, rows, vectors, groups),
        out_shape=chunk_shapes(rows, vectors, node) + [shaped((vectors, node), f32)],
        in_specs=[smem()] * 3 + [vmem()] * (2 * CHUNKS + 2) + [anywhere()] * 2,
        out_specs=[vmem()] * (2 * CHUNKS + 1),
        scratch_shapes=[
            pltpu.VMEM(((rows + groups * 2 * CAP) * vectors, node), bf16),
            pltpu.VMEM(((rows + 1) * vectors, node), f32),
        ]
        + stream_scratch(blocks, diag),
        compiler_params=params(22),
        name="operate_second",
    )(pick, target, asked, *arrays, halo, arrived, blocks, diag)
    return outs[:CHUNKS], outs[CHUNKS : 2 * CHUNKS], outs[-1]


def third_kernel(rows, vectors, groups, width, pick, wanted, origin, *refs):
    count = 2 * CHUNKS
    drive, image, (own, blocks, diag), refs = refs[:count], refs[count : 2 * count], refs[2 * count : 2 * count + 3], refs[2 * count + 3 :]
    form, left, drive_own, image_own, field = refs[:5]
    stream = Stream(blocks, diag, *refs[5:])
    stream.start()
    half = rows // 2
    each = half // CHUNKS
    shape = form.shape
    band = lax.axis_index("band")
    core = core_of(band)
    for side in range(2):
        start = jnp.where(core == side, 0, half)
        for c in range(CHUNKS):
            array = image[side * CHUNKS + c]

            def one(p, carry, start=start, c=c, array=array):
                field[tile(start + c * each + p, vectors), :] = array[tile(p, vectors), :].astype(bf16)
                return carry

            lax.fori_loop(0, each, one, 0, unroll=16)
            for v in range(width):
                inside = pl.ds(pl.multiple_of(start + c * each, each), each)
                source = pl.ds(band * width + v, each, stride=vectors)
                drive_own[v, inside, :] = drive[side * CHUNKS + c][source, :]
                image_own[v, inside, :] = array[source, :]
    field[rows * vectors :, :] = jnp.zeros((vectors, shape[1]), bf16)

    def at(row):
        return field[tile(row, vectors), :]

    def some(piece, parts):
        stream.wait(piece)
        twice, once = parts
        base = piece * UNROLL
        for u in range(0, UNROLL, 2):
            row = base + u
            values = times_two(at(row), at(row + 1), stream.held[pl.ds(row, 2)])
            for k, value in enumerate(values):
                source = jnp.minimum(pick[0, row + k], rows)
                twice = twice + value * at(source).astype(f32)
        for d in range(0, stream.own, 2):
            row = (band * stream.pieces + piece) * stream.own + d
            here, there = at(row), at(row + 1)
            one, other = times_two(here, there, stream.held_diag[pl.ds(piece * stream.own + d, 2)])
            once = once + one * here.astype(f32) + other * there.astype(f32)
        return twice, once

    nothing = jnp.zeros(shape, f32)
    twice, once = lax.fori_loop(0, stream.pieces, some, (nothing, nothing))
    form[...] = 2.0 * twice + once

    def remote(peer, carry):
        for k in range(CAP):
            value = times(field[tile(origin[peer, k], vectors), :], own[peer * CAP + k])
            left[tile(peer * CAP + k, vectors), :] = jnp.where(wanted[peer, k] < 0, 0.0, 2.0) * value
        return carry

    lax.fori_loop(0, groups, remote, 0)


def operate_third(pick, wanted, origin, drive, image, own, blocks, diag, width, vectors):
    rows, node = blocks.shape[0], blocks.shape[-1]
    groups = lax.axis_size("curve")
    mine = pltpu.HBM((width, rows, node), f32)
    return pl.pallas_call(
        functools.partial(third_kernel, rows, vectors, groups, width),
        out_shape=[shaped((vectors, node), f32), shaped((groups * CAP * vectors, node), f32), mine, mine],
        in_specs=[smem()] * 3 + [vmem()] * (4 * CHUNKS + 1) + [anywhere()] * 2,
        out_specs=[vmem()] * 4,
        scratch_shapes=[pltpu.VMEM(((rows + 1) * vectors, node), bf16)] + stream_scratch(blocks, diag),
        compiler_params=params(22),
        name="operate_third",
    )(pick, wanted, origin, *drive, *image[:CHUNKS], *map(in_hbm, image[CHUNKS:]), own, blocks, diag)


def tail_kernel(each, vectors, form, left, halo, *refs):
    image, share = refs[:-1], refs[-1]
    shape = form.shape
    total = form[...]
    for slot in range(left.shape[0] // vectors):
        at = slot * vectors
        total = total + left[at : at + vectors, :] * halo[at : at + vectors, :].astype(f32)
    values = [total]
    for e in range(2):
        at = (each + e) * vectors
        value = image[0][at : at + vectors, :]
        for other in image[1:]:
            value = value + other[at : at + vectors, :]
        values.append(0.5 * value)
    line = jnp.zeros((1, shape[1]), f32)
    across = lax.broadcasted_iota(i32, shape, 1)
    down = lax.broadcasted_iota(i32, shape, 0)
    for e, value in enumerate(values):
        column = jnp.broadcast_to(row_sum(value), shape)
        line = line + jnp.sum(jnp.where(across == down + e * vectors, column, 0.0), axis=0, keepdims=True)
    share[...] = jnp.broadcast_to(line, share.shape)


def tail(form, left, halo, image, devices):
    vectors, node = form.shape
    each = image[0].shape[0] // vectors - 2
    return pl.pallas_call(
        functools.partial(tail_kernel, each, vectors),
        out_shape=shaped((devices, node), f32),
        in_specs=[vmem()] * (3 + len(image)),
        out_specs=vmem(),
        compiler_params=params(16),
        name="tail",
    )(form, left, halo, *image)


def code_tiles(each, node):
    return -(-each // node)


def encode_kernel(each, vectors, keep, came, code, wide):
    node = keep.shape[1]
    lanes = lax.broadcasted_iota(i32, (vectors, node), 1)
    for group in range(code_tiles(each, node)):
        inside = range(group * node, min(each, (group + 1) * node))
        peak = jnp.zeros((vectors, node), f32)
        for p in inside:
            at = p * vectors
            value = keep[at : at + vectors, :] + came[at : at + vectors, :]
            wide[at : at + vectors, :] = value
            peak = jnp.where(lanes == p - group * node, jnp.max(jnp.abs(value), axis=1, keepdims=True), peak)
        power = jnp.ceil(jnp.log2(jnp.maximum(peak, 1e-30)) * STEP) + 1.0
        start = (each + group) * vectors
        code[start : start + vectors, :] = power.astype(i32).astype(jnp.int16)
        gain = FULL * jnp.exp2(power * (-1.0 / STEP))
        for p in inside:
            at = p * vectors
            lane = p - group * node
            scaled = wide[at : at + vectors, :] * gain[:, lane : lane + 1]
            code[at : at + vectors, :] = jnp.round(scaled).astype(i32).astype(jnp.int16)


def encode(keep, came, vectors):
    size, node = keep.shape
    each = size // vectors
    return pl.pallas_call(
        functools.partial(encode_kernel, each, vectors),
        out_shape=shaped(((each + code_tiles(each, node)) * vectors, node), jnp.int16),
        in_specs=[vmem()] * 2,
        out_specs=vmem(),
        scratch_shapes=[pltpu.VMEM((size, node), f32)],
        compiler_params=params(12),
        name="encode",
    )(keep, came)


def decode_kernel(each, vectors, weighted, *refs):
    if weighted:
        code, came, drive, out = refs
    else:
        code, came, out = refs
    node = code.shape[1]
    shape = (vectors, node)
    energy = jnp.zeros(shape, f32)
    cross = jnp.zeros(shape, f32)
    for group in range(code_tiles(each, node)):
        start = (each + group) * vectors
        gains = [
            jnp.exp2(ref[start : start + vectors, :].astype(i32).astype(f32) * (1.0 / STEP)) * (1.0 / FULL)
            for ref in (code, came)
        ]
        for p in range(group * node, min(each, (group + 1) * node)):
            at = p * vectors
            lane = p - group * node
            one, two = [
                ref[at : at + vectors, :].astype(i32).astype(f32) * gain[:, lane : lane + 1]
                for ref, gain in zip((code, came), gains)
            ]
            value = one + two
            out[at : at + vectors, :] = value
            energy = energy + value * value
            if weighted:
                cross = cross + value * drive[at : at + vectors, :]
    at = each * vectors
    if weighted:
        out[at : at + vectors, :] = cross
        at = at + vectors
    out[at : at + vectors, :] = energy


def decode(code, came, vectors, each, drive=None):
    node = code.shape[1]
    extra = 1 if drive is None else 2
    inputs = (code, came) if drive is None else (code, came, drive)
    return pl.pallas_call(
        functools.partial(decode_kernel, each, vectors, drive is not None),
        out_shape=shaped(((each + extra) * vectors, node), f32),
        in_specs=[vmem()] * len(inputs),
        out_specs=vmem(),
        compiler_params=params(12),
        name="decode",
    )(*inputs)


def fetch_row(arrays, each, vectors, row):
    core = core_of(lax.axis_index("band"))
    half = each * CHUNKS
    side = row // half
    inside = row - side * half
    chunk = inside // each
    place = tile(inside - chunk * each, vectors)
    value = arrays[0][place, :]
    number = jnp.where(side == core, chunk, CHUNKS + chunk)
    for k in range(1, 2 * CHUNKS):
        value = jnp.where(number == k, arrays[k][place, :], value)
    return value


def pack_kernel(each, vectors, groups, asked, origin, *refs):
    arrays, message = refs[:-1], refs[-1]
    shape = (vectors, message.shape[1])
    sums = arrays[0][each * vectors :, :]
    for array in arrays[1:]:
        sums = sums + array[each * vectors :, :]
    line = jnp.broadcast_to(as_line(row_sum(sums), shape), shape)[0:8, :]
    size = 2 * CAP * vectors + 8

    def send(peer, carry):
        for k in range(2 * CAP):
            row = jnp.maximum(asked[peer, k], 0) if k < CAP else origin[peer, k - CAP]
            at = pl.multiple_of(peer * size + k * vectors, 8)
            message[pl.ds(at, vectors), :] = fetch_row(arrays, each, vectors, row)
        message[pl.ds(pl.multiple_of(peer * size + 2 * CAP * vectors, 8), 8), :] = line
        return carry

    lax.fori_loop(0, groups, send, 0)


def pack(asked, origin, arrays, vectors):
    node = arrays[0].shape[1]
    each = arrays[0].shape[0] // vectors - 1
    groups = lax.axis_size("curve")
    return pl.pallas_call(
        functools.partial(pack_kernel, each, vectors, groups),
        out_shape=shaped((groups * (2 * CAP * vectors + 8), node), f32),
        in_specs=[smem()] * 2 + [vmem()] * (2 * CHUNKS),
        out_specs=vmem(),
        compiler_params=params(16),
        name="pack",
    )(asked, origin, *arrays)


def pack_rounded_kernel(each, vectors, groups, asked, *refs):
    arrays, message = refs[:-1], refs[-1]

    def send(peer, carry):
        for k in range(CAP):
            value = fetch_row(arrays, each, vectors, jnp.maximum(asked[peer, k], 0))
            message[tile(peer * CAP + k, vectors), :] = value.astype(bf16)
        return carry

    lax.fori_loop(0, groups, send, 0)


def pack_rounded(asked, arrays, vectors):
    node = arrays[0].shape[1]
    each = arrays[0].shape[0] // vectors - 2
    groups = lax.axis_size("curve")
    return pl.pallas_call(
        functools.partial(pack_rounded_kernel, each, vectors, groups),
        out_shape=shaped((groups * CAP * vectors, node), bf16),
        in_specs=[smem()] + [vmem()] * (2 * CHUNKS),
        out_specs=vmem(),
        compiler_params=params(16),
        name="pack_rounded",
    )(asked, *arrays)


def finish_kernel(shares, scale, state, drive, image, out, one, two, lift, mix):
    shape = scale.shape
    vectors = shape[0]
    line = jnp.sum(shares[...], axis=0, keepdims=True)
    form, cross, energy = [as_column(line, shape, e * vectors) for e in range(3)]
    beta_zero = scale[...]
    unit = 1.0 - epsilon / (beta_zero * beta_zero)
    alpha_first = cross / beta_zero
    square = alpha_first * alpha_first
    beta_first = jnp.sqrt(jnp.maximum(energy - square * (2.0 - unit), 0.0) + epsilon)
    alpha_second = (form - 2.0 * alpha_first * energy + square * alpha_first) / (beta_first * beta_first)
    alpha_second = alpha_second - alpha_first * (1.0 - unit)
    term_one = jnp.ones(shape, f32)
    term_two = jnp.zeros(shape, f32)
    total_one, total_two = term_one, term_two
    for turn in range(1, TAYLOR):
        factor = time_step / (turn + 1.0)
        next_one = factor * (alpha_first * term_one + beta_first * term_two)
        next_two = factor * (beta_first * term_one + alpha_second * term_two)
        term_one, term_two = next_one, next_two
        total_one, total_two = total_one + next_one, total_two + next_two
    one[...] = time_step * total_one
    two[...] = time_step * beta_zero * total_two / beta_first
    mix[...] = alpha_first / beta_zero
    width = state.shape[0]
    for v in range(width):
        at = pl.ds(lax.axis_index("band") * width + v, 1)
        size = state.shape[1:]
        weight_one, weight_two, share = [jnp.broadcast_to(ref[at, :], size) for ref in (one, two, mix)]
        out[v] = state[v] + (weight_one * drive[v] + weight_two * (image[v] - share * drive[v]))


def finish(shares, scale, state, drive, image):
    return pl.pallas_call(
        finish_kernel,
        out_shape=shaped(state.shape, f32),
        in_specs=[vmem()] * 5,
        out_specs=vmem(),
        scratch_shapes=[pltpu.VMEM(scale.shape, f32)] * 4,
        compiler_params=params(16),
        name="finish",
    )(shares, scale, state, in_hbm(drive), in_hbm(image))


def swap(array, bit):
    size = lax.axis_size("band")
    return lax.ppermute(array, "band", [(k, k ^ bit) for k in range(size)])


def exchange(array):
    return lax.all_to_all(array, "curve", split_axis=0, concat_axis=0, tiled=True)


def band_sum(keep, give, vectors, drive=None):
    each = keep[0].shape[0] // vectors
    came = [swap(array, 1) for array in give]
    codes = [encode(one, two, vectors) for one, two in zip(keep, came)]
    across = []
    for code in codes:
        across.append(swap(code, 2))
    mine = [
        decode(code, other, vectors, each, None if drive is None else drive[c])
        for c, (code, other) in enumerate(zip(codes, across))
    ]
    return mine + [swap(array, 1) for array in mine]


def body(state, blocks, diag_blocks, block_cols):
    groups = lax.axis_size("curve")
    devices = groups * lax.axis_size("band")
    width, rows = state.shape[:2]
    vectors = width * lax.axis_size("band")
    blocks = in_hbm(blocks)
    diag_blocks = in_hbm(diag_blocks)
    rounded = state.astype(bf16)
    state = in_hbm(state)
    across = swap(rounded, 2)
    beside = swap(rounded, 1)
    pick, target, wanted, origin = plan(block_cols.reshape(1, rows))
    asked = exchange(wanted)
    corner = swap(across, 1)
    parts = [rounded, beside, across, corner]
    field, own, split = spread(parts, origin, blocks)
    message = reply(asked, field, split, vectors)
    halo = exchange(message)
    local = operate_local(pick, target, field, state, blocks, diag_blocks)
    keep, give = settle(wanted, origin, asked, local, halo, own, rows)
    drive = band_sum(keep, give, vectors)
    arrived = exchange(own)
    halo = exchange(pack(asked, origin, drive, vectors))
    keep, give, scale = operate_second(pick, target, asked, drive, halo, arrived, blocks, diag_blocks)
    image = band_sum(keep, give, vectors, drive)
    halo = exchange(pack_rounded(asked, image, vectors))
    form, left, drive_own, image_own = operate_third(
        pick, wanted, origin, drive, image, own, blocks, diag_blocks, width, vectors
    )
    share = tail(form, left, halo, image[:CHUNKS], devices)
    shares = lax.all_to_all(share, ("curve", "band"), split_axis=0, concat_axis=0, tiled=True)
    return finish(shares, scale, state, drive_own, image_own)


def solution(mesh):
    return jax.shard_map(
        body,
        mesh=mesh,
        in_specs=(
            P("band", "curve", None),
            P("curve", "band", None, None),
            P(("curve", "band"), None, None),
            P("curve", "band"),
        ),
        out_specs=P("band", "curve", None),
        check_vma=False,
    )
```

```python
import functools

import jax
import jax.numpy as jnp
from jax import lax
from jax.experimental import pallas as pl
from jax.experimental.pallas import tpu as pltpu
from jax.sharding import PartitionSpec as P


CAP = 2
TAYLOR = 16
UNROLL = 32
CHUNKS = 2

epsilon = 1e-06
time_step = 0.5
quadratic = 1.0
STEP = 256.0
FULL = 32767.0

f32 = jnp.float32
bf16 = jnp.bfloat16
i32 = jnp.int32


def nonlinear(field):
    return quadratic * field * field - field * field * field


def tile(index, rows):
    return pl.ds(pl.multiple_of(index * rows, rows), rows)


def smem():
    return pl.BlockSpec(memory_space=pltpu.SMEM)


def vmem():
    return pl.BlockSpec(memory_space=pltpu.VMEM)


def anywhere():
    return pl.BlockSpec(memory_space=pltpu.HBM)


def params(mebibytes):
    return pltpu.CompilerParams(vmem_limit_bytes=mebibytes * 1024 * 1024)


def in_hbm(array):
    return pltpu.with_memory_space_constraint(array, pltpu.HBM)


def shaped(shape, dtype):
    return jax.ShapeDtypeStruct(shape, dtype)


def times(field, block):
    return lax.dot_general(field, block, (((1,), (0,)), ((), ())), preferred_element_type=f32)


def two(one, other):
    nothing = jnp.zeros_like(one)
    upper = jnp.concatenate([one, nothing], axis=1)
    return jnp.concatenate([upper, jnp.concatenate([nothing, other], axis=1)], axis=0)


def times_two(one, other, blocks):
    value = times(two(one, other), blocks.reshape(-1, blocks.shape[-1]))
    return value[: one.shape[0]], value[one.shape[0] :]


def times_two_transposed(one, other, first, second):
    value = times(two(one, other), jnp.concatenate([first.T, second.T], axis=0))
    return value[: one.shape[0]], value[one.shape[0] :]


def row_sum(part):
    return jnp.sum(part, axis=1, keepdims=True)


def as_column(line, shape, offset=0):
    across = lax.broadcasted_iota(i32, shape, 1)
    down = lax.broadcasted_iota(i32, shape, 0)
    picked = jnp.where(across == down + offset, jnp.broadcast_to(line, shape), 0.0)
    return jnp.broadcast_to(row_sum(picked), shape)


def core_of(band):
    return jnp.bitwise_and(band, 1)


def plan_kernel(cols, pick, target, wanted, origin):
    groups, lanes = wanted.shape
    rows = cols.shape[1]
    here = lax.axis_index("curve")
    column = cols[...]
    owner = column // rows
    inner = column - owner * rows
    shape = (groups, rows)
    peer = lax.broadcasted_iota(i32, shape, 0)
    place = lax.broadcasted_iota(i32, shape, 1).astype(f32)
    inside = jnp.broadcast_to(inner.astype(f32), shape)
    left = (jnp.broadcast_to(owner, shape) == peer) & (peer != here)
    number = jnp.zeros((1, rows), f32)
    lane = lax.broadcasted_iota(i32, (groups, lanes), 1)
    want = jnp.full((groups, lanes), -1.0, f32)
    source = jnp.zeros((groups, lanes), f32)
    none = float(rows)
    for k in range(CAP):
        least = jnp.min(jnp.where(left, place, none), axis=1, keepdims=True)
        hit = left & (place == least)
        left = left & (place != least)
        aim = row_sum(jnp.where(hit, inside, 0.0))
        want = jnp.where((lane == k) & (least < none), aim, want)
        source = jnp.where((lane == k) & (least < none), least, source)
        slot = (peer * (2 * CAP) + k).astype(f32)
        number = number + jnp.sum(jnp.where(hit, slot, 0.0), axis=0, keepdims=True)
    wanted[...] = want.astype(i32)
    origin[...] = source.astype(i32)
    pick[...] = jnp.where(owner == here, inner, rows + number.astype(i32))
    target[...] = jnp.where(owner == here, inner, rows)


def plan(cols):
    rows = cols.shape[1]
    groups = lax.axis_size("curve")
    return pl.pallas_call(
        plan_kernel,
        out_shape=[shaped((1, rows), i32)] * 2 + [shaped((groups, 128), i32)] * 2,
        in_specs=[vmem()],
        out_specs=[vmem()] * 4,
        compiler_params=params(8),
        name="plan",
    )(cols)


def spread_kernel(rows, vectors, groups, width, origin, blocks, *refs):
    count = vectors // width
    parts, (field, own, split, wide, sems) = refs[:count], refs[count:]
    slots = groups * CAP

    def fetch(slot):
        peer = slot // CAP
        row = origin[peer, slot - peer * CAP]
        return pltpu.make_async_copy(blocks.at[row, 0], own.at[slot], sems.at[slot])

    def begin(slot, carry):
        fetch(slot).start()
        return carry

    lax.fori_loop(0, slots, begin, 0)
    band = lax.axis_index("band")
    for k, part in enumerate(parts):
        start = jnp.bitwise_xor(band, k) * width
        for v in range(width):
            wide[pl.ds(start + v, rows, stride=vectors), :] = part[v].astype(f32)
    field[0 : rows * vectors, :] = wide[...].astype(bf16)
    field[rows * vectors :, :] = jnp.zeros((vectors, field.shape[1]), bf16)

    def end(slot, carry):
        fetch(slot).wait()
        return carry

    lax.fori_loop(0, slots, end, 0)

    def product(peer, carry):
        fields = [field[tile(origin[peer, k], vectors), :] for k in range(CAP)]
        for k, value in enumerate(times_two(*fields, own[pl.ds(peer * CAP, CAP)])):
            high = value.astype(bf16)
            split[tile(peer * (2 * CAP) + k, vectors), :] = high
            split[tile(peer * (2 * CAP) + CAP + k, vectors), :] = (value - high.astype(f32)).astype(bf16)
        return carry

    lax.fori_loop(0, groups, product, 0, unroll=8)


def spread(parts, origin, blocks):
    width, rows, node = parts[0].shape
    groups = lax.axis_size("curve")
    slots = groups * CAP
    vectors = width * len(parts)
    return pl.pallas_call(
        functools.partial(spread_kernel, rows, vectors, groups, width),
        out_shape=[
            pltpu.HBM(((rows + 1) * vectors, node), bf16),
            shaped((slots, node, node), bf16),
            shaped((slots * 2 * vectors, node), bf16),
        ],
        in_specs=[smem(), anywhere()] + [vmem()] * len(parts),
        out_specs=[vmem()] * 3,
        scratch_shapes=[pltpu.VMEM((rows * vectors, node), f32), pltpu.SemaphoreType.DMA((slots,))],
        compiler_params=params(16),
        name="spread",
    )(origin, blocks, *parts)


def reply_kernel(vectors, groups, asked, field, split, message):
    def send(peer, carry):
        at = peer * (3 * CAP)
        for k in range(CAP):
            message[tile(at + k, vectors), :] = field[tile(jnp.maximum(asked[peer, k], 0), vectors), :]
        for k in range(2 * CAP):
            message[tile(at + CAP + k, vectors), :] = split[tile(peer * (2 * CAP) + k, vectors), :]
        return carry

    lax.fori_loop(0, groups, send, 0)


def reply(asked, field, split, vectors):
    groups = lax.axis_size("curve")
    return pl.pallas_call(
        functools.partial(reply_kernel, vectors, groups),
        out_shape=shaped((groups * 3 * CAP * vectors, field.shape[1]), bf16),
        in_specs=[smem()] + [vmem()] * 2,
        out_specs=vmem(),
        compiler_params=params(16),
        name="reply",
    )(asked, in_hbm(field), split)


class Stream:
    def __init__(self, blocks, diag, held, held_diag, sems):
        self.blocks, self.diag, self.held, self.held_diag, self.sems = blocks, diag, held, held_diag, sems
        self.pieces = blocks.shape[0] // UNROLL
        self.own = diag.shape[0] // self.pieces

    def copies(self, piece):
        rows = pl.ds(piece * UNROLL, UNROLL)
        own = pl.ds(piece * self.own, self.own)
        return (
            pltpu.make_async_copy(self.blocks.at[rows, 0], self.held.at[rows], self.sems.at[0, piece]),
            pltpu.make_async_copy(self.diag.at[own], self.held_diag.at[own], self.sems.at[1, piece]),
        )

    def start(self):
        for piece in range(self.pieces):
            for copy in self.copies(piece):
                copy.start()

    def wait(self, piece):
        for copy in self.copies(piece):
            copy.wait()


def stream_scratch(blocks, diag):
    rows, node = blocks.shape[0], blocks.shape[-1]
    return [
        pltpu.VMEM((rows, node, node), bf16),
        pltpu.VMEM(diag.shape, bf16),
        pltpu.SemaphoreType.DMA((2, rows // UNROLL)),
    ]


def products(vectors, limit, pick, target, field, stream, total):
    band = lax.axis_index("band")

    def at(row):
        return field[tile(row, vectors), :]

    def source(row):
        place = pick[0, row]
        return at(place if limit is None else jnp.minimum(place, limit))

    def some(piece, carry):
        stream.wait(piece)
        forward, mirrored = [], []
        base = piece * UNROLL
        for u in range(0, UNROLL, 2):
            row = base + u
            forward += times_two_transposed(source(row), source(row + 1), stream.held[row], stream.held[row + 1])
            mirrored += times_two(at(row), at(row + 1), stream.held[pl.ds(row, 2)])
        own = stream.own
        first = band * (own * stream.pieces) + piece * own
        values = []
        for d in range(0, own, 2):
            values += times_two(at(first + d), at(first + d + 1), stream.held_diag[pl.ds(piece * own + d, 2)])
        for u in range(UNROLL):
            total[tile(base + u, vectors), :] += forward[u]
            total[tile(target[0, base + u], vectors), :] += mirrored[u]
        for d, value in enumerate(values):
            total[tile(first + d, vectors), :] += value
        return carry

    lax.fori_loop(0, stream.pieces, some, 0)


def give_out(rows, vectors, total, outs):
    core = core_of(lax.axis_index("band"))
    half = rows // 2
    size = half // CHUNKS * vectors
    for side in range(2):
        start = jnp.where(core == side, 0, half) * vectors
        for c in range(CHUNKS):
            outs[side * CHUNKS + c][...] = total[pl.ds(pl.multiple_of(start + c * size, size), size), :]


def local_kernel(rows, vectors, pick, target, field, state, blocks, diag, total, *scratch):
    stream = Stream(blocks, diag, *scratch)
    stream.start()
    total[...] = jnp.zeros_like(total)
    width = state.shape[0]
    band = lax.axis_index("band")
    for v in range(width):
        total[pl.ds(band * width + v, rows, stride=vectors), :] = nonlinear(state[v])
    products(vectors, rows, pick, target, field, stream, total)


def operate_local(pick, target, field, state, blocks, diag):
    rows, node = blocks.shape[0], blocks.shape[-1]
    vectors = field.shape[0] // (rows + 1)
    return pl.pallas_call(
        functools.partial(local_kernel, rows, vectors),
        out_shape=shaped(((rows + 1) * vectors, node), f32),
        in_specs=[smem()] * 2 + [vmem()] * 2 + [anywhere()] * 2,
        out_specs=vmem(),
        scratch_shapes=stream_scratch(blocks, diag),
        compiler_params=params(20),
        name="operate_local",
    )(pick, target, in_hbm(field), state, blocks, diag)


def settle_kernel(rows, vectors, groups, wanted, origin, asked, local, halo, own, *refs):
    outs, total = refs[:-1], refs[-1]
    total[...] = local[...]

    def some(peer, carry):
        at = peer * (3 * CAP)
        values = []
        fields = [halo[tile(at + k, vectors), :] for k in range(CAP)]
        for k, value in enumerate(times_two_transposed(*fields, own[peer * CAP], own[peer * CAP + 1])):
            values.append((jnp.where(wanted[peer, k] < 0, rows, origin[peer, k]), value))
        for k in range(CAP):
            value = halo[tile(at + CAP + k, vectors), :].astype(f32)
            value = value + halo[tile(at + 2 * CAP + k, vectors), :].astype(f32)
            values.append((jnp.where(asked[peer, k] < 0, rows, asked[peer, k]), value))
        for aim, value in values:
            total[tile(aim, vectors), :] += value
        return carry

    lax.fori_loop(0, groups, some, 0, unroll=8)
    give_out(rows, vectors, total, outs)


def chunk_shapes(rows, vectors, node):
    return [shaped((rows // 2 // CHUNKS * vectors, node), f32)] * (2 * CHUNKS)


def settle(wanted, origin, asked, local, halo, own, rows):
    node = local.shape[1]
    vectors = local.shape[0] // (rows + 1)
    groups = lax.axis_size("curve")
    outs = pl.pallas_call(
        functools.partial(settle_kernel, rows, vectors, groups),
        out_shape=chunk_shapes(rows, vectors, node),
        in_specs=[smem()] * 3 + [vmem()] * 3,
        out_specs=[vmem()] * (2 * CHUNKS),
        scratch_shapes=[pltpu.VMEM(local.shape, f32)],
        compiler_params=params(20),
        name="settle",
    )(wanted, origin, asked, local, halo, own)
    return outs[:CHUNKS], outs[CHUNKS:]


def second_kernel(rows, vectors, groups, pick, target, asked, *refs):
    arrays, (halo, arrived, blocks, diag), refs = refs[: 2 * CHUNKS], refs[2 * CHUNKS : 2 * CHUNKS + 4], refs[2 * CHUNKS + 4 :]
    outs, (scale, field, total), scratch = refs[: 2 * CHUNKS], refs[2 * CHUNKS : 2 * CHUNKS + 3], refs[2 * CHUNKS + 3 :]
    stream = Stream(blocks, diag, *scratch)
    stream.start()
    half = rows // 2
    each = half // CHUNKS
    size = 2 * CAP + 1
    shape = scale.shape

    def gather(g, energy):
        last = from_code(halo[tile(g * size + 2 * CAP, vectors), :])
        digits = last[:, 2 * CAP + 1 : 2 * CAP + 2] + last[:, 2 * CAP + 2 : 2 * CAP + 3] * (1.0 / FULL)
        return energy + digits * scale_of(last)[:, 2 * CAP : 2 * CAP + 1]

    energy = lax.fori_loop(0, groups, gather, jnp.zeros((vectors, 1), f32), unroll=8)
    energy = jnp.broadcast_to(energy * (1.0 / FULL), shape)
    beta = jnp.sqrt(energy + epsilon)
    scale[...] = beta
    inverse = 1.0 / beta
    core = core_of(lax.axis_index("band"))
    for side in range(2):
        start = jnp.where(core == side, 0, half)
        for c in range(CHUNKS):
            array = arrays[side * CHUNKS + c]

            def one(p, carry, start=start, c=c, array=array):
                field[tile(start + c * each + p, vectors), :] = (array[tile(p, vectors), :] * inverse).astype(bf16)
                return carry

            lax.fori_loop(0, each, one, 0, unroll=16)

    def row(g, carry):
        gains = scale_of(from_code(halo[tile(g * size + 2 * CAP, vectors), :])) * (1.0 / FULL)
        for k in range(2 * CAP):
            value = from_code(halo[tile(g * size + k, vectors), :]) * gains[:, k : k + 1] * inverse
            field[tile(rows + g * (2 * CAP) + k, vectors), :] = value.astype(bf16)
        return carry

    lax.fori_loop(0, groups, row, 0, unroll=4)
    total[...] = jnp.zeros_like(total)
    products(vectors, None, pick, target, field, stream, total)

    def some(peer, carry):
        place = rows + peer * (2 * CAP) + CAP
        fields = [field[tile(place + k, vectors), :] for k in range(CAP)]
        for k, value in enumerate(times_two(*fields, arrived[pl.ds(peer * CAP, CAP)])):
            aim = asked[peer, k]
            total[tile(jnp.where(aim < 0, rows, aim), vectors), :] += value
        return carry

    lax.fori_loop(0, groups, some, 0, unroll=8)
    give_out(rows, vectors, total, outs)


def operate_second(pick, target, asked, arrays, halo, arrived, blocks, diag):
    rows, node = blocks.shape[0], blocks.shape[-1]
    groups = lax.axis_size("curve")
    vectors = halo.shape[0] // (groups * (2 * CAP + 1))
    outs = pl.pallas_call(
        functools.partial(second_kernel, rows, vectors, groups),
        out_shape=chunk_shapes(rows, vectors, node) + [shaped((vectors, node), f32)],
        in_specs=[smem()] * 3 + [vmem()] * (2 * CHUNKS + 2) + [anywhere()] * 2,
        out_specs=[vmem()] * (2 * CHUNKS + 1),
        scratch_shapes=[
            pltpu.VMEM(((rows + groups * 2 * CAP) * vectors, node), bf16),
            pltpu.VMEM(((rows + 1) * vectors, node), f32),
        ]
        + stream_scratch(blocks, diag),
        compiler_params=params(22),
        name="operate_second",
    )(pick, target, asked, *arrays, halo, arrived, blocks, diag)
    return outs[:CHUNKS], outs[CHUNKS : 2 * CHUNKS], outs[-1]


def third_kernel(rows, vectors, groups, width, pick, wanted, origin, *refs):
    count = 2 * CHUNKS
    drive, image, (own, blocks, diag), refs = refs[:count], refs[count : 2 * count], refs[2 * count : 2 * count + 3], refs[2 * count + 3 :]
    form, left, drive_own, image_own, field = refs[:5]
    stream = Stream(blocks, diag, *refs[5:])
    stream.start()
    half = rows // 2
    each = half // CHUNKS
    shape = form.shape
    band = lax.axis_index("band")
    core = core_of(band)
    for side in range(2):
        start = jnp.where(core == side, 0, half)
        for c in range(CHUNKS):
            array = image[side * CHUNKS + c]

            def one(p, carry, start=start, c=c, array=array):
                field[tile(start + c * each + p, vectors), :] = array[tile(p, vectors), :].astype(bf16)
                return carry

            lax.fori_loop(0, each, one, 0, unroll=16)
            for v in range(width):
                inside = pl.ds(pl.multiple_of(start + c * each, each), each)
                source = pl.ds(band * width + v, each, stride=vectors)
                drive_own[v, inside, :] = drive[side * CHUNKS + c][source, :]
                image_own[v, inside, :] = array[source, :]
    field[rows * vectors :, :] = jnp.zeros((vectors, shape[1]), bf16)

    def at(row):
        return field[tile(row, vectors), :]

    def some(piece, parts):
        stream.wait(piece)
        twice, once = parts
        base = piece * UNROLL
        for u in range(0, UNROLL, 2):
            row = base + u
            values = times_two(at(row), at(row + 1), stream.held[pl.ds(row, 2)])
            for k, value in enumerate(values):
                source = jnp.minimum(pick[0, row + k], rows)
                twice = twice + value * at(source).astype(f32)
        for d in range(0, stream.own, 2):
            row = (band * stream.pieces + piece) * stream.own + d
            here, there = at(row), at(row + 1)
            one, other = times_two(here, there, stream.held_diag[pl.ds(piece * stream.own + d, 2)])
            once = once + one * here.astype(f32) + other * there.astype(f32)
        return twice, once

    nothing = jnp.zeros(shape, f32)
    twice, once = lax.fori_loop(0, stream.pieces, some, (nothing, nothing))
    form[...] = 2.0 * twice + once

    def remote(peer, carry):
        fields = [at(origin[peer, k]) for k in range(CAP)]
        for k, value in enumerate(times_two(*fields, own[pl.ds(peer * CAP, CAP)])):
            left[tile(peer * CAP + k, vectors), :] = jnp.where(wanted[peer, k] < 0, 0.0, 2.0) * value
        return carry

    lax.fori_loop(0, groups, remote, 0, unroll=8)


def operate_third(pick, wanted, origin, drive, image, own, blocks, diag, width, vectors):
    rows, node = blocks.shape[0], blocks.shape[-1]
    groups = lax.axis_size("curve")
    mine = pltpu.HBM((width, rows, node), f32)
    return pl.pallas_call(
        functools.partial(third_kernel, rows, vectors, groups, width),
        out_shape=[shaped((vectors, node), f32), shaped((groups * CAP * vectors, node), f32), mine, mine],
        in_specs=[smem()] * 3 + [vmem()] * (4 * CHUNKS + 1) + [anywhere()] * 2,
        out_specs=[vmem()] * 4,
        scratch_shapes=[pltpu.VMEM(((rows + 1) * vectors, node), bf16)] + stream_scratch(blocks, diag),
        compiler_params=params(22),
        name="operate_third",
    )(pick, wanted, origin, *drive, *image[:CHUNKS], *map(in_hbm, image[CHUNKS:]), own, blocks, diag)


def tail_kernel(each, vectors, form, left, halo, *refs):
    image, share = refs[:-1], refs[-1]
    shape = form.shape
    total = form[...]
    for slot in range(left.shape[0] // vectors):
        at = slot * vectors
        total = total + left[at : at + vectors, :] * halo[at : at + vectors, :].astype(f32)
    values = [total]
    for e in range(2):
        at = (each + e) * vectors
        value = image[0][at : at + vectors, :]
        for other in image[1:]:
            value = value + other[at : at + vectors, :]
        values.append(0.5 * value)
    line = jnp.zeros((1, shape[1]), f32)
    across = lax.broadcasted_iota(i32, shape, 1)
    down = lax.broadcasted_iota(i32, shape, 0)
    for e, value in enumerate(values):
        column = jnp.broadcast_to(row_sum(value), shape)
        line = line + jnp.sum(jnp.where(across == down + e * vectors, column, 0.0), axis=0, keepdims=True)
    share[...] = jnp.broadcast_to(line, share.shape)


def tail(form, left, halo, image, devices):
    vectors, node = form.shape
    each = image[0].shape[0] // vectors - 2
    return pl.pallas_call(
        functools.partial(tail_kernel, each, vectors),
        out_shape=shaped((devices, node), f32),
        in_specs=[vmem()] * (3 + len(image)),
        out_specs=vmem(),
        compiler_params=params(16),
        name="tail",
    )(form, left, halo, *image)


def code_tiles(each, node):
    return -(-each // node)


def encode_kernel(each, vectors, keep, came, code, wide):
    node = keep.shape[1]
    lanes = lax.broadcasted_iota(i32, (vectors, node), 1)
    for group in range(code_tiles(each, node)):
        inside = range(group * node, min(each, (group + 1) * node))
        peak = jnp.zeros((vectors, node), f32)
        for p in inside:
            at = p * vectors
            value = keep[at : at + vectors, :] + came[at : at + vectors, :]
            wide[at : at + vectors, :] = value
            peak = jnp.where(lanes == p - group * node, jnp.max(jnp.abs(value), axis=1, keepdims=True), peak)
        power = scale_power(peak)
        start = (each + group) * vectors
        code[start : start + vectors, :] = as_code(power)
        gain = FULL * scale_of(-power)
        for p in inside:
            at = p * vectors
            lane = p - group * node
            scaled = wide[at : at + vectors, :] * gain[:, lane : lane + 1]
            code[at : at + vectors, :] = as_code(jnp.round(scaled))


def encode(keep, came, vectors):
    size, node = keep.shape
    each = size // vectors
    return pl.pallas_call(
        functools.partial(encode_kernel, each, vectors),
        out_shape=shaped(((each + code_tiles(each, node)) * vectors, node), jnp.int16),
        in_specs=[vmem()] * 2,
        out_specs=vmem(),
        scratch_shapes=[pltpu.VMEM((size, node), f32)],
        compiler_params=params(12),
        name="encode",
    )(keep, came)


def decode_kernel(each, vectors, weighted, *refs):
    if weighted:
        code, came, drive, out = refs
    else:
        code, came, out = refs
    node = code.shape[1]
    shape = (vectors, node)
    energy = jnp.zeros(shape, f32)
    cross = jnp.zeros(shape, f32)
    for group in range(code_tiles(each, node)):
        start = (each + group) * vectors
        gains = [
            scale_of(from_code(ref[start : start + vectors, :])) * (1.0 / FULL)
            for ref in (code, came)
        ]
        for p in range(group * node, min(each, (group + 1) * node)):
            at = p * vectors
            lane = p - group * node
            one, two = [
                from_code(ref[at : at + vectors, :]) * gain[:, lane : lane + 1]
                for ref, gain in zip((code, came), gains)
            ]
            value = one + two
            out[at : at + vectors, :] = value
            energy = energy + value * value
            if weighted:
                cross = cross + value * drive[at : at + vectors, :]
    at = each * vectors
    if weighted:
        out[at : at + vectors, :] = cross
        at = at + vectors
    out[at : at + vectors, :] = energy


def decode(code, came, vectors, each, drive=None):
    node = code.shape[1]
    extra = 1 if drive is None else 2
    inputs = (code, came) if drive is None else (code, came, drive)
    return pl.pallas_call(
        functools.partial(decode_kernel, each, vectors, drive is not None),
        out_shape=shaped(((each + extra) * vectors, node), f32),
        in_specs=[vmem()] * len(inputs),
        out_specs=vmem(),
        compiler_params=params(12),
        name="decode",
    )(*inputs)


def fetch_row(arrays, each, vectors, row):
    core = core_of(lax.axis_index("band"))
    half = each * CHUNKS
    side = row // half
    inside = row - side * half
    chunk = inside // each
    place = tile(inside - chunk * each, vectors)
    value = arrays[0][place, :]
    number = jnp.where(side == core, chunk, CHUNKS + chunk)
    for k in range(1, 2 * CHUNKS):
        value = jnp.where(number == k, arrays[k][place, :], value)
    return value


def scale_power(peak):
    return jnp.ceil(jnp.log2(jnp.maximum(peak, 1e-30)) * STEP) + 1.0


def scale_of(power):
    return jnp.exp2(power * (1.0 / STEP))


def as_code(value):
    return value.astype(i32).astype(jnp.int16)


def from_code(code):
    return code.astype(i32).astype(f32)


def pack_kernel(each, vectors, groups, asked, origin, *refs):
    arrays, message = refs[:-1], refs[-1]
    shape = (vectors, message.shape[1])
    lanes = lax.broadcasted_iota(i32, shape, 1)
    sums = arrays[0][each * vectors :, :]
    for array in arrays[1:]:
        sums = sums + array[each * vectors :, :]
    energy = jnp.broadcast_to(row_sum(sums), shape)
    power = scale_power(energy)
    digits = energy * (FULL * scale_of(-power))
    high = jnp.floor(digits)
    low = jnp.round((digits - high) * FULL)
    extra = jnp.where(lanes == 2 * CAP, power, jnp.where(lanes == 2 * CAP + 1, high, low))
    size = 2 * CAP + 1

    def send(peer, carry):
        last = extra
        for k in range(2 * CAP):
            row = jnp.maximum(asked[peer, k], 0) if k < CAP else origin[peer, k - CAP]
            value = fetch_row(arrays, each, vectors, row)
            power = scale_power(jnp.broadcast_to(jnp.max(jnp.abs(value), axis=1, keepdims=True), shape))
            message[tile(peer * size + k, vectors), :] = as_code(jnp.round(value * (FULL * scale_of(-power))))
            last = jnp.where(lanes == k, power, last)
        message[tile(peer * size + 2 * CAP, vectors), :] = as_code(last)
        return carry

    lax.fori_loop(0, groups, send, 0, unroll=4)


def pack(asked, origin, arrays, vectors):
    node = arrays[0].shape[1]
    each = arrays[0].shape[0] // vectors - 1
    groups = lax.axis_size("curve")
    return pl.pallas_call(
        functools.partial(pack_kernel, each, vectors, groups),
        out_shape=shaped((groups * (2 * CAP + 1) * vectors, node), jnp.int16),
        in_specs=[smem()] * 2 + [vmem()] * (2 * CHUNKS),
        out_specs=vmem(),
        compiler_params=params(16),
        name="pack",
    )(asked, origin, *arrays)


def pack_rounded_kernel(each, vectors, groups, asked, *refs):
    arrays, message = refs[:-1], refs[-1]

    def send(peer, carry):
        for k in range(CAP):
            value = fetch_row(arrays, each, vectors, jnp.maximum(asked[peer, k], 0))
            message[tile(peer * CAP + k, vectors), :] = value.astype(bf16)
        return carry

    lax.fori_loop(0, groups, send, 0)


def pack_rounded(asked, arrays, vectors):
    node = arrays[0].shape[1]
    each = arrays[0].shape[0] // vectors - 2
    groups = lax.axis_size("curve")
    return pl.pallas_call(
        functools.partial(pack_rounded_kernel, each, vectors, groups),
        out_shape=shaped((groups * CAP * vectors, node), bf16),
        in_specs=[smem()] + [vmem()] * (2 * CHUNKS),
        out_specs=vmem(),
        compiler_params=params(16),
        name="pack_rounded",
    )(asked, *arrays)


def finish_kernel(shares, scale, state_in, drive_in, image_in, out, one, two, mix, state, drive, image, sems):
    copies = [
        [pltpu.make_async_copy(source.at[v], place.at[v], sems.at[k, v]) for v in range(out.shape[0])]
        for k, (source, place) in enumerate(((state_in, state), (drive_in, drive), (image_in, image)))
    ]
    for column in copies:
        for copy in column:
            copy.start()
    shape = scale.shape
    vectors = shape[0]
    line = jnp.sum(shares[...], axis=0, keepdims=True)
    form, cross, energy = [as_column(line, shape, e * vectors) for e in range(3)]
    beta_zero = scale[...]
    unit = 1.0 - epsilon / (beta_zero * beta_zero)
    alpha_first = cross / beta_zero
    square = alpha_first * alpha_first
    beta_first = jnp.sqrt(jnp.maximum(energy - square * (2.0 - unit), 0.0) + epsilon)
    alpha_second = (form - 2.0 * alpha_first * energy + square * alpha_first) / (beta_first * beta_first)
    alpha_second = alpha_second - alpha_first * (1.0 - unit)
    term_one = jnp.ones(shape, f32)
    term_two = jnp.zeros(shape, f32)
    total_one, total_two = term_one, term_two
    for turn in range(1, TAYLOR):
        factor = time_step / (turn + 1.0)
        next_one = factor * (alpha_first * term_one + beta_first * term_two)
        next_two = factor * (beta_first * term_one + alpha_second * term_two)
        term_one, term_two = next_one, next_two
        total_one, total_two = total_one + next_one, total_two + next_two
    one[...] = time_step * total_one
    two[...] = time_step * beta_zero * total_two / beta_first
    mix[...] = alpha_first / beta_zero
    width = state.shape[0]
    for v in range(width):
        at = pl.ds(lax.axis_index("band") * width + v, 1)
        size = state.shape[1:]
        weight_one, weight_two, share = [jnp.broadcast_to(ref[at, :], size) for ref in (one, two, mix)]
        for column in copies:
            column[v].wait()
        out[v] = state[v] + (weight_one * drive[v] + weight_two * (image[v] - share * drive[v]))


def finish(shares, scale, state, drive, image):
    return pl.pallas_call(
        finish_kernel,
        out_shape=shaped(state.shape, f32),
        in_specs=[vmem()] * 2 + [anywhere()] * 3,
        out_specs=vmem(),
        scratch_shapes=[pltpu.VMEM(scale.shape, f32)] * 3
        + [pltpu.VMEM(state.shape, f32)] * 3
        + [pltpu.SemaphoreType.DMA((3, state.shape[0]))],
        compiler_params=params(16),
        name="finish",
    )(shares, scale, state, in_hbm(drive), in_hbm(image))


def swap(array, bit):
    size = lax.axis_size("band")
    return lax.ppermute(array, "band", [(k, k ^ bit) for k in range(size)])


def exchange(array):
    return lax.all_to_all(array, "curve", split_axis=0, concat_axis=0, tiled=True)


def band_sum(keep, give, vectors, drive=None):
    each = keep[0].shape[0] // vectors
    came = [swap(array, 1) for array in give]
    codes = [encode(one, two, vectors) for one, two in zip(keep, came)]
    across = []
    for code in codes:
        across.append(swap(code, 2))
    mine = [
        decode(code, other, vectors, each, None if drive is None else drive[c])
        for c, (code, other) in enumerate(zip(codes, across))
    ]
    return mine + [swap(array, 1) for array in mine]


def body(state, blocks, diag_blocks, block_cols):
    groups = lax.axis_size("curve")
    devices = groups * lax.axis_size("band")
    width, rows = state.shape[:2]
    vectors = width * lax.axis_size("band")
    blocks = in_hbm(blocks)
    diag_blocks = in_hbm(diag_blocks)
    rounded = state.astype(bf16)
    state = in_hbm(state)
    across = swap(rounded, 2)
    beside = swap(rounded, 1)
    pick, target, wanted, origin = plan(block_cols.reshape(1, rows))
    asked = exchange(wanted)
    corner = swap(across, 1)
    parts = [rounded, beside, across, corner]
    field, own, split = spread(parts, origin, blocks)
    message = reply(asked, field, split, vectors)
    halo = exchange(message)
    local = operate_local(pick, target, field, state, blocks, diag_blocks)
    keep, give = settle(wanted, origin, asked, local, halo, own, rows)
    drive = band_sum(keep, give, vectors)
    arrived = exchange(own)
    halo = exchange(pack(asked, origin, drive, vectors))
    keep, give, scale = operate_second(pick, target, asked, drive, halo, arrived, blocks, diag_blocks)
    image = band_sum(keep, give, vectors, drive)
    halo = exchange(pack_rounded(asked, image, vectors))
    form, left, drive_own, image_own = operate_third(
        pick, wanted, origin, drive, image, own, blocks, diag_blocks, width, vectors
    )
    share = tail(form, left, halo, image[:CHUNKS], devices)
    shares = lax.all_to_all(share, ("curve", "band"), split_axis=0, concat_axis=0, tiled=True)
    return finish(shares, scale, state, drive_own, image_own)


def solution(mesh):
    return jax.shard_map(
        body,
        mesh=mesh,
        in_specs=(
            P("band", "curve", None),
            P("curve", "band", None, None),
            P(("curve", "band"), None, None),
            P("curve", "band"),
        ),
        out_specs=P("band", "curve", None),
        check_vma=False,
    )
```

```python
import functools

import jax
import jax.numpy as jnp
from jax import lax
from jax.experimental import pallas as pl
from jax.experimental.pallas import tpu as pltpu
from jax.sharding import PartitionSpec as P


CAP = 2
TAYLOR = 16
UNROLL = 32
CHUNKS = 2

epsilon = 1e-06
time_step = 0.5
quadratic = 1.0
STEP = 256.0
FULL = 32767.0

f32 = jnp.float32
bf16 = jnp.bfloat16
i32 = jnp.int32


def nonlinear(field):
    return quadratic * field * field - field * field * field


def tile(index, rows):
    return pl.ds(pl.multiple_of(index * rows, rows), rows)


def smem():
    return pl.BlockSpec(memory_space=pltpu.SMEM)


def vmem():
    return pl.BlockSpec(memory_space=pltpu.VMEM)


def anywhere():
    return pl.BlockSpec(memory_space=pltpu.HBM)


def params(mebibytes):
    return pltpu.CompilerParams(vmem_limit_bytes=mebibytes * 1024 * 1024)


def in_hbm(array):
    return pltpu.with_memory_space_constraint(array, pltpu.HBM)


def shaped(shape, dtype):
    return jax.ShapeDtypeStruct(shape, dtype)


def times(field, block):
    return lax.dot_general(field, block, (((1,), (0,)), ((), ())), preferred_element_type=f32)


def two(one, other):
    nothing = jnp.zeros_like(one)
    upper = jnp.concatenate([one, nothing], axis=1)
    return jnp.concatenate([upper, jnp.concatenate([nothing, other], axis=1)], axis=0)


def times_two(one, other, blocks):
    value = times(two(one, other), blocks.reshape(-1, blocks.shape[-1]))
    return value[: one.shape[0]], value[one.shape[0] :]


def times_two_transposed(one, other, first, second):
    value = times(two(one, other), jnp.concatenate([first.T, second.T], axis=0))
    return value[: one.shape[0]], value[one.shape[0] :]


def row_sum(part):
    return jnp.sum(part, axis=1, keepdims=True)


def as_column(line, shape, offset=0):
    across = lax.broadcasted_iota(i32, shape, 1)
    down = lax.broadcasted_iota(i32, shape, 0)
    picked = jnp.where(across == down + offset, jnp.broadcast_to(line, shape), 0.0)
    return jnp.broadcast_to(row_sum(picked), shape)


def core_of(band):
    return jnp.bitwise_and(band, 1)


def plan_kernel(cols, state, rounded, pick, target, wanted, origin):
    rounded[...] = state[...].astype(bf16)
    groups, lanes = wanted.shape
    rows = cols.shape[1]
    here = lax.axis_index("curve")
    column = cols[...]
    owner = column // rows
    inner = column - owner * rows
    shape = (groups, rows)
    peer = lax.broadcasted_iota(i32, shape, 0)
    place = lax.broadcasted_iota(i32, shape, 1).astype(f32)
    inside = jnp.broadcast_to(inner.astype(f32), shape)
    left = (jnp.broadcast_to(owner, shape) == peer) & (peer != here)
    number = jnp.zeros((1, rows), f32)
    lane = lax.broadcasted_iota(i32, (groups, lanes), 1)
    want = jnp.full((groups, lanes), -1.0, f32)
    source = jnp.zeros((groups, lanes), f32)
    none = float(rows)
    for k in range(CAP):
        least = jnp.min(jnp.where(left, place, none), axis=1, keepdims=True)
        hit = left & (place == least)
        left = left & (place != least)
        aim = row_sum(jnp.where(hit, inside, 0.0))
        want = jnp.where((lane == k) & (least < none), aim, want)
        source = jnp.where((lane == k) & (least < none), least, source)
        slot = (peer * (2 * CAP) + k).astype(f32)
        number = number + jnp.sum(jnp.where(hit, slot, 0.0), axis=0, keepdims=True)
    wanted[...] = want.astype(i32)
    origin[...] = source.astype(i32)
    pick[...] = jnp.where(owner == here, inner, rows + number.astype(i32))
    target[...] = jnp.where(owner == here, inner, rows)


def plan(cols, state):
    rows = cols.shape[1]
    groups = lax.axis_size("curve")
    return pl.pallas_call(
        plan_kernel,
        out_shape=[shaped(state.shape, bf16)] + [shaped((1, rows), i32)] * 2 + [shaped((groups, 128), i32)] * 2,
        in_specs=[vmem()] * 2,
        out_specs=[vmem()] * 5,
        compiler_params=params(8),
        name="plan",
    )(in_hbm(cols), state)


def spread_kernel(rows, vectors, groups, width, origin, blocks, *refs):
    count = vectors // width
    parts, (field, own, split, wide, sems) = refs[:count], refs[count:]
    slots = groups * CAP

    def fetch(slot):
        peer = slot // CAP
        row = origin[peer, slot - peer * CAP]
        return pltpu.make_async_copy(blocks.at[row, 0], own.at[slot], sems.at[slot])

    def begin(slot, carry):
        fetch(slot).start()
        return carry

    lax.fori_loop(0, slots, begin, 0)
    band = lax.axis_index("band")
    for k, part in enumerate(parts):
        start = jnp.bitwise_xor(band, k) * width
        for v in range(width):
            wide[pl.ds(start + v, rows, stride=vectors), :] = part[v].astype(f32)
    field[0 : rows * vectors, :] = wide[...].astype(bf16)
    field[rows * vectors :, :] = jnp.zeros((vectors, field.shape[1]), bf16)

    def end(slot, carry):
        fetch(slot).wait()
        return carry

    lax.fori_loop(0, slots, end, 0)

    def product(peer, carry):
        fields = [field[tile(origin[peer, k], vectors), :] for k in range(CAP)]
        for k, value in enumerate(times_two(*fields, own[pl.ds(peer * CAP, CAP)])):
            high = value.astype(bf16)
            split[tile(peer * (2 * CAP) + k, vectors), :] = high
            split[tile(peer * (2 * CAP) + CAP + k, vectors), :] = (value - high.astype(f32)).astype(bf16)
        return carry

    lax.fori_loop(0, groups, product, 0, unroll=8)


def spread(parts, origin, blocks):
    width, rows, node = parts[0].shape
    groups = lax.axis_size("curve")
    slots = groups * CAP
    vectors = width * len(parts)
    return pl.pallas_call(
        functools.partial(spread_kernel, rows, vectors, groups, width),
        out_shape=[
            pltpu.HBM(((rows + 1) * vectors, node), bf16),
            shaped((slots, node, node), bf16),
            shaped((slots * 2 * vectors, node), bf16),
        ],
        in_specs=[smem(), anywhere()] + [vmem()] * len(parts),
        out_specs=[vmem()] * 3,
        scratch_shapes=[pltpu.VMEM((rows * vectors, node), f32), pltpu.SemaphoreType.DMA((slots,))],
        compiler_params=params(16),
        name="spread",
    )(origin, blocks, *parts)


def reply_kernel(vectors, groups, asked, field, split, message):
    def send(peer, carry):
        at = peer * (3 * CAP)
        for k in range(CAP):
            message[tile(at + k, vectors), :] = field[tile(jnp.maximum(asked[peer, k], 0), vectors), :]
        for k in range(2 * CAP):
            message[tile(at + CAP + k, vectors), :] = split[tile(peer * (2 * CAP) + k, vectors), :]
        return carry

    lax.fori_loop(0, groups, send, 0, unroll=8)


def reply(asked, field, split, vectors):
    groups = lax.axis_size("curve")
    return pl.pallas_call(
        functools.partial(reply_kernel, vectors, groups),
        out_shape=shaped((groups * 3 * CAP * vectors, field.shape[1]), bf16),
        in_specs=[smem()] + [vmem()] * 2,
        out_specs=vmem(),
        compiler_params=params(16),
        name="reply",
    )(asked, in_hbm(field), split)


class Stream:
    def __init__(self, blocks, diag, held, held_diag, sems):
        self.blocks, self.diag, self.held, self.held_diag, self.sems = blocks, diag, held, held_diag, sems
        self.pieces = blocks.shape[0] // UNROLL
        self.own = diag.shape[0] // self.pieces

    def copies(self, piece):
        rows = pl.ds(piece * UNROLL, UNROLL)
        own = pl.ds(piece * self.own, self.own)
        return (
            pltpu.make_async_copy(self.blocks.at[rows, 0], self.held.at[rows], self.sems.at[0, piece]),
            pltpu.make_async_copy(self.diag.at[own], self.held_diag.at[own], self.sems.at[1, piece]),
        )

    def start(self):
        for piece in range(self.pieces):
            for copy in self.copies(piece):
                copy.start()

    def wait(self, piece):
        for copy in self.copies(piece):
            copy.wait()


def stream_scratch(blocks, diag):
    rows, node = blocks.shape[0], blocks.shape[-1]
    return [
        pltpu.VMEM((rows, node, node), bf16),
        pltpu.VMEM(diag.shape, bf16),
        pltpu.SemaphoreType.DMA((2, rows // UNROLL)),
    ]


def products(vectors, limit, pick, target, field, stream, total):
    band = lax.axis_index("band")

    def at(row):
        return field[tile(row, vectors), :]

    def source(row):
        place = pick[0, row]
        return at(place if limit is None else jnp.minimum(place, limit))

    def some(piece, carry):
        stream.wait(piece)
        forward, mirrored = [], []
        base = piece * UNROLL
        for u in range(0, UNROLL, 2):
            row = base + u
            forward += times_two_transposed(source(row), source(row + 1), stream.held[row], stream.held[row + 1])
            mirrored += times_two(at(row), at(row + 1), stream.held[pl.ds(row, 2)])
        own = stream.own
        first = band * (own * stream.pieces) + piece * own
        values = []
        for d in range(0, own, 2):
            values += times_two(at(first + d), at(first + d + 1), stream.held_diag[pl.ds(piece * own + d, 2)])
        for u in range(UNROLL):
            total[tile(base + u, vectors), :] += forward[u]
            total[tile(target[0, base + u], vectors), :] += mirrored[u]
        for d, value in enumerate(values):
            total[tile(first + d, vectors), :] += value
        return carry

    lax.fori_loop(0, stream.pieces, some, 0)


def give_out(rows, vectors, total, outs):
    core = core_of(lax.axis_index("band"))
    half = rows // 2
    size = half // CHUNKS * vectors
    for side in range(2):
        start = jnp.where(core == side, 0, half) * vectors
        for c in range(CHUNKS):
            outs[side * CHUNKS + c][...] = total[pl.ds(pl.multiple_of(start + c * size, size), size), :]


def local_kernel(rows, vectors, pick, target, field, state, blocks, diag, total, *scratch):
    stream = Stream(blocks, diag, *scratch)
    stream.start()
    total[...] = jnp.zeros_like(total)
    width = state.shape[0]
    band = lax.axis_index("band")
    for v in range(width):
        total[pl.ds(band * width + v, rows, stride=vectors), :] = nonlinear(state[v])
    products(vectors, rows, pick, target, field, stream, total)


def operate_local(pick, target, field, state, blocks, diag):
    rows, node = blocks.shape[0], blocks.shape[-1]
    vectors = field.shape[0] // (rows + 1)
    return pl.pallas_call(
        functools.partial(local_kernel, rows, vectors),
        out_shape=shaped(((rows + 1) * vectors, node), f32),
        in_specs=[smem()] * 2 + [vmem()] * 2 + [anywhere()] * 2,
        out_specs=vmem(),
        scratch_shapes=stream_scratch(blocks, diag),
        compiler_params=params(20),
        name="operate_local",
    )(pick, target, in_hbm(field), state, blocks, diag)


def settle_kernel(rows, vectors, groups, wanted, origin, asked, local, halo, own, *refs):
    outs, total = refs[:-1], refs[-1]
    total[...] = local[...]

    def some(peer, carry):
        at = peer * (3 * CAP)
        values = []
        fields = [halo[tile(at + k, vectors), :] for k in range(CAP)]
        for k, value in enumerate(times_two_transposed(*fields, own[peer * CAP], own[peer * CAP + 1])):
            values.append((jnp.where(wanted[peer, k] < 0, rows, origin[peer, k]), value))
        for k in range(CAP):
            value = halo[tile(at + CAP + k, vectors), :].astype(f32)
            value = value + halo[tile(at + 2 * CAP + k, vectors), :].astype(f32)
            values.append((jnp.where(asked[peer, k] < 0, rows, asked[peer, k]), value))
        for aim, value in values:
            total[tile(aim, vectors), :] += value
        return carry

    lax.fori_loop(0, groups, some, 0, unroll=8)
    give_out(rows, vectors, total, outs)


def chunk_shapes(rows, vectors, node):
    return [shaped((rows // 2 // CHUNKS * vectors, node), f32)] * (2 * CHUNKS)


def settle(wanted, origin, asked, local, halo, own, rows):
    node = local.shape[1]
    vectors = local.shape[0] // (rows + 1)
    groups = lax.axis_size("curve")
    outs = pl.pallas_call(
        functools.partial(settle_kernel, rows, vectors, groups),
        out_shape=chunk_shapes(rows, vectors, node),
        in_specs=[smem()] * 3 + [vmem()] * 3,
        out_specs=[vmem()] * (2 * CHUNKS),
        scratch_shapes=[pltpu.VMEM(local.shape, f32)],
        compiler_params=params(20),
        name="settle",
    )(wanted, origin, asked, local, halo, own)
    return outs[:CHUNKS], outs[CHUNKS:]


def second_kernel(rows, vectors, groups, pick, target, asked, *refs):
    arrays, (halo, arrived, blocks, diag), refs = refs[: 2 * CHUNKS], refs[2 * CHUNKS : 2 * CHUNKS + 4], refs[2 * CHUNKS + 4 :]
    outs, (scale, field, total), scratch = refs[: 2 * CHUNKS], refs[2 * CHUNKS : 2 * CHUNKS + 3], refs[2 * CHUNKS + 3 :]
    stream = Stream(blocks, diag, *scratch)
    stream.start()
    half = rows // 2
    each = half // CHUNKS
    size = 2 * CAP + 1
    shape = scale.shape

    def gather(g, energy):
        last = from_code(halo[tile(g * size + 2 * CAP, vectors), :])
        digits = last[:, 2 * CAP + 1 : 2 * CAP + 2] + last[:, 2 * CAP + 2 : 2 * CAP + 3] * (1.0 / FULL)
        return energy + digits * scale_of(last)[:, 2 * CAP : 2 * CAP + 1]

    energy = lax.fori_loop(0, groups, gather, jnp.zeros((vectors, 1), f32), unroll=8)
    energy = jnp.broadcast_to(energy * (1.0 / FULL), shape)
    beta = jnp.sqrt(energy + epsilon)
    scale[...] = beta
    inverse = 1.0 / beta
    core = core_of(lax.axis_index("band"))
    for side in range(2):
        start = jnp.where(core == side, 0, half)
        for c in range(CHUNKS):
            array = arrays[side * CHUNKS + c]

            def one(p, carry, start=start, c=c, array=array):
                field[tile(start + c * each + p, vectors), :] = (array[tile(p, vectors), :] * inverse).astype(bf16)
                return carry

            lax.fori_loop(0, each, one, 0, unroll=16)

    def row(g, carry):
        gains = scale_of(from_code(halo[tile(g * size + 2 * CAP, vectors), :])) * (1.0 / FULL)
        for k in range(2 * CAP):
            value = from_code(halo[tile(g * size + k, vectors), :]) * gains[:, k : k + 1] * inverse
            field[tile(rows + g * (2 * CAP) + k, vectors), :] = value.astype(bf16)
        return carry

    lax.fori_loop(0, groups, row, 0, unroll=4)
    total[...] = jnp.zeros_like(total)
    products(vectors, None, pick, target, field, stream, total)

    def some(peer, carry):
        place = rows + peer * (2 * CAP) + CAP
        fields = [field[tile(place + k, vectors), :] for k in range(CAP)]
        for k, value in enumerate(times_two(*fields, arrived[pl.ds(peer * CAP, CAP)])):
            aim = asked[peer, k]
            total[tile(jnp.where(aim < 0, rows, aim), vectors), :] += value
        return carry

    lax.fori_loop(0, groups, some, 0, unroll=8)
    give_out(rows, vectors, total, outs)


def operate_second(pick, target, asked, arrays, halo, arrived, blocks, diag):
    rows, node = blocks.shape[0], blocks.shape[-1]
    groups = lax.axis_size("curve")
    vectors = halo.shape[0] // (groups * (2 * CAP + 1))
    outs = pl.pallas_call(
        functools.partial(second_kernel, rows, vectors, groups),
        out_shape=chunk_shapes(rows, vectors, node) + [shaped((vectors, node), f32)],
        in_specs=[smem()] * 3 + [vmem()] * (2 * CHUNKS + 2) + [anywhere()] * 2,
        out_specs=[vmem()] * (2 * CHUNKS + 1),
        scratch_shapes=[
            pltpu.VMEM(((rows + groups * 2 * CAP) * vectors, node), bf16),
            pltpu.VMEM(((rows + 1) * vectors, node), f32),
        ]
        + stream_scratch(blocks, diag),
        compiler_params=params(22),
        name="operate_second",
    )(pick, target, asked, *arrays, halo, arrived, blocks, diag)
    return outs[:CHUNKS], outs[CHUNKS : 2 * CHUNKS], outs[-1]


def third_kernel(rows, vectors, groups, width, pick, wanted, origin, *refs):
    count = 2 * CHUNKS
    drive, image, (own, blocks, diag), refs = refs[:count], refs[count : 2 * count], refs[2 * count : 2 * count + 3], refs[2 * count + 3 :]
    form, left, drive_own, image_own, field = refs[:5]
    stream = Stream(blocks, diag, *refs[5:])
    stream.start()
    half = rows // 2
    each = half // CHUNKS
    shape = form.shape
    band = lax.axis_index("band")
    core = core_of(band)
    for side in range(2):
        start = jnp.where(core == side, 0, half)
        for c in range(CHUNKS):
            array = image[side * CHUNKS + c]

            def one(p, carry, start=start, c=c, array=array):
                field[tile(start + c * each + p, vectors), :] = array[tile(p, vectors), :].astype(bf16)
                return carry

            lax.fori_loop(0, each, one, 0, unroll=16)
            for v in range(width):
                inside = pl.ds(pl.multiple_of(start + c * each, each), each)
                source = pl.ds(band * width + v, each, stride=vectors)
                drive_own[v, inside, :] = drive[side * CHUNKS + c][source, :]
                image_own[v, inside, :] = array[source, :]
    field[rows * vectors :, :] = jnp.zeros((vectors, shape[1]), bf16)

    def at(row):
        return field[tile(row, vectors), :]

    def some(piece, parts):
        stream.wait(piece)
        twice, once = parts
        base = piece * UNROLL
        for u in range(0, UNROLL, 2):
            row = base + u
            values = times_two(at(row), at(row + 1), stream.held[pl.ds(row, 2)])
            for k, value in enumerate(values):
                source = jnp.minimum(pick[0, row + k], rows)
                twice = twice + value * at(source).astype(f32)
        for d in range(0, stream.own, 2):
            row = (band * stream.pieces + piece) * stream.own + d
            here, there = at(row), at(row + 1)
            one, other = times_two(here, there, stream.held_diag[pl.ds(piece * stream.own + d, 2)])
            once = once + one * here.astype(f32) + other * there.astype(f32)
        return twice, once

    nothing = jnp.zeros(shape, f32)
    twice, once = lax.fori_loop(0, stream.pieces, some, (nothing, nothing))
    form[...] = 2.0 * twice + once

    def remote(peer, carry):
        fields = [at(origin[peer, k]) for k in range(CAP)]
        for k, value in enumerate(times_two(*fields, own[pl.ds(peer * CAP, CAP)])):
            left[tile(peer * CAP + k, vectors), :] = jnp.where(wanted[peer, k] < 0, 0.0, 2.0) * value
        return carry

    lax.fori_loop(0, groups, remote, 0, unroll=8)


def operate_third(pick, wanted, origin, drive, image, own, blocks, diag, width, vectors):
    rows, node = blocks.shape[0], blocks.shape[-1]
    groups = lax.axis_size("curve")
    mine = pltpu.HBM((width, rows, node), f32)
    return pl.pallas_call(
        functools.partial(third_kernel, rows, vectors, groups, width),
        out_shape=[shaped((vectors, node), f32), shaped((groups * CAP * vectors, node), f32), mine, mine],
        in_specs=[smem()] * 3 + [vmem()] * (4 * CHUNKS + 1) + [anywhere()] * 2,
        out_specs=[vmem()] * 4,
        scratch_shapes=[pltpu.VMEM(((rows + 1) * vectors, node), bf16)] + stream_scratch(blocks, diag),
        compiler_params=params(22),
        name="operate_third",
    )(pick, wanted, origin, *drive, *image[:CHUNKS], *map(in_hbm, image[CHUNKS:]), own, blocks, diag)


def tail_kernel(each, vectors, form, left, halo, image, share):
    shape = form.shape
    total = form[...]
    for slot in range(left.shape[0] // vectors):
        at = slot * vectors
        total = total + left[at : at + vectors, :] * halo[at : at + vectors, :].astype(f32)
    values = [total]
    for e in range(2):
        at = (each + e) * vectors
        values.append(0.5 * image[at : at + vectors, :])
    line = jnp.zeros((1, shape[1]), f32)
    across = lax.broadcasted_iota(i32, shape, 1)
    down = lax.broadcasted_iota(i32, shape, 0)
    for e, value in enumerate(values):
        column = jnp.broadcast_to(row_sum(value), shape)
        line = line + jnp.sum(jnp.where(across == down + e * vectors, column, 0.0), axis=0, keepdims=True)
    share[...] = jnp.broadcast_to(line, share.shape)


def tail(form, left, halo, image, devices):
    vectors, node = form.shape
    each = image.shape[0] // vectors - 2
    return pl.pallas_call(
        functools.partial(tail_kernel, each, vectors),
        out_shape=shaped((devices, node), f32),
        in_specs=[vmem()] * 4,
        out_specs=vmem(),
        compiler_params=params(16),
        name="tail",
    )(form, left, halo, image)


def code_tiles(each, node):
    return -(-each // node)


def encode_kernel(each, vectors, keep, came, code, wide):
    node = keep.shape[1]
    lanes = lax.broadcasted_iota(i32, (vectors, node), 1)
    for group in range(code_tiles(each, node)):
        inside = range(group * node, min(each, (group + 1) * node))
        peak = jnp.zeros((vectors, node), f32)
        for p in inside:
            at = p * vectors
            value = keep[at : at + vectors, :] + came[at : at + vectors, :]
            wide[at : at + vectors, :] = value
            peak = jnp.where(lanes == p - group * node, jnp.max(jnp.abs(value), axis=1, keepdims=True), peak)
        power = scale_power(peak)
        start = (each + group) * vectors
        code[start : start + vectors, :] = as_code(power)
        gain = FULL * scale_of(-power)
        for p in inside:
            at = p * vectors
            lane = p - group * node
            scaled = wide[at : at + vectors, :] * gain[:, lane : lane + 1]
            code[at : at + vectors, :] = as_code(jnp.round(scaled))


def encode(keep, came, vectors):
    size, node = keep.shape
    each = size // vectors
    return pl.pallas_call(
        functools.partial(encode_kernel, each, vectors),
        out_shape=shaped(((each + code_tiles(each, node)) * vectors, node), jnp.int16),
        in_specs=[vmem()] * 2,
        out_specs=vmem(),
        scratch_shapes=[pltpu.VMEM((size, node), f32)],
        compiler_params=params(12),
        name="encode",
    )(keep, came)


def decode_kernel(each, vectors, weighted, chained, *refs):
    code, came, out = refs[0], refs[1], refs[-1]
    drive = refs[2] if weighted else None
    node = code.shape[1]
    shape = (vectors, node)
    energy = jnp.zeros(shape, f32)
    cross = jnp.zeros(shape, f32)
    if chained:
        before = refs[-2]
        at = each * vectors
        if weighted:
            cross = before[at : at + vectors, :]
            at = at + vectors
        energy = before[at : at + vectors, :]
    for group in range(code_tiles(each, node)):
        start = (each + group) * vectors
        gains = [
            scale_of(from_code(ref[start : start + vectors, :])) * (1.0 / FULL)
            for ref in (code, came)
        ]
        for p in range(group * node, min(each, (group + 1) * node)):
            at = p * vectors
            lane = p - group * node
            one, two = [
                from_code(ref[at : at + vectors, :]) * gain[:, lane : lane + 1]
                for ref, gain in zip((code, came), gains)
            ]
            value = one + two
            out[at : at + vectors, :] = value
            energy = energy + value * value
            if weighted:
                cross = cross + value * drive[at : at + vectors, :]
    at = each * vectors
    if weighted:
        out[at : at + vectors, :] = cross
        at = at + vectors
    out[at : at + vectors, :] = energy


def decode(code, came, vectors, each, drive=None, before=None):
    node = code.shape[1]
    extra = 1 if drive is None else 2
    inputs = [array for array in (code, came, drive, before) if array is not None]
    return pl.pallas_call(
        functools.partial(decode_kernel, each, vectors, drive is not None, before is not None),
        out_shape=shaped(((each + extra) * vectors, node), f32),
        in_specs=[vmem()] * len(inputs),
        out_specs=vmem(),
        compiler_params=params(12),
        name="decode",
    )(*inputs)


def fetch_row(arrays, each, vectors, row):
    core = core_of(lax.axis_index("band"))
    half = each * CHUNKS
    side = row // half
    inside = row - side * half
    chunk = inside // each
    place = tile(inside - chunk * each, vectors)
    value = arrays[0][place, :]
    number = jnp.where(side == core, chunk, CHUNKS + chunk)
    for k in range(1, 2 * CHUNKS):
        value = jnp.where(number == k, arrays[k][place, :], value)
    return value


def scale_power(peak):
    return jnp.ceil(jnp.log2(jnp.maximum(peak, 1e-30)) * STEP) + 1.0


def scale_of(power):
    return jnp.exp2(power * (1.0 / STEP))


def as_code(value):
    return value.astype(i32).astype(jnp.int16)


def from_code(code):
    return code.astype(i32).astype(f32)


def pack_kernel(each, vectors, groups, asked, origin, *refs):
    arrays, message = refs[:-1], refs[-1]
    shape = (vectors, message.shape[1])
    lanes = lax.broadcasted_iota(i32, shape, 1)
    sums = arrays[CHUNKS - 1][each * vectors :, :] + arrays[2 * CHUNKS - 1][each * vectors :, :]
    energy = jnp.broadcast_to(row_sum(sums), shape)
    power = scale_power(energy)
    digits = energy * (FULL * scale_of(-power))
    high = jnp.floor(digits)
    low = jnp.round((digits - high) * FULL)
    extra = jnp.where(lanes == 2 * CAP, power, jnp.where(lanes == 2 * CAP + 1, high, low))
    size = 2 * CAP + 1

    def send(peer, carry):
        last = extra
        for k in range(2 * CAP):
            row = jnp.maximum(asked[peer, k], 0) if k < CAP else origin[peer, k - CAP]
            value = fetch_row(arrays, each, vectors, row)
            power = scale_power(jnp.broadcast_to(jnp.max(jnp.abs(value), axis=1, keepdims=True), shape))
            message[tile(peer * size + k, vectors), :] = as_code(jnp.round(value * (FULL * scale_of(-power))))
            last = jnp.where(lanes == k, power, last)
        message[tile(peer * size + 2 * CAP, vectors), :] = as_code(last)
        return carry

    lax.fori_loop(0, groups, send, 0, unroll=4)


def pack(asked, origin, arrays, vectors):
    node = arrays[0].shape[1]
    each = arrays[0].shape[0] // vectors - 1
    groups = lax.axis_size("curve")
    return pl.pallas_call(
        functools.partial(pack_kernel, each, vectors, groups),
        out_shape=shaped((groups * (2 * CAP + 1) * vectors, node), jnp.int16),
        in_specs=[smem()] * 2 + [vmem()] * (2 * CHUNKS),
        out_specs=vmem(),
        compiler_params=params(16),
        name="pack",
    )(asked, origin, *arrays)


def pack_rounded_kernel(each, vectors, groups, asked, *refs):
    arrays, message, left, sems = refs[: 2 * CHUNKS], refs[2 * CHUNKS], refs[2 * CHUNKS + 1 : -1], refs[-1]
    copies = [
        pltpu.make_async_copy(array, place, sems.at[c]) for c, (array, place) in enumerate(zip(arrays[CHUNKS:], left))
    ]
    for copy in copies:
        copy.start()

    def send(peer, carry):
        for k in range(CAP):
            value = fetch_row(arrays, each, vectors, jnp.maximum(asked[peer, k], 0))
            message[tile(peer * CAP + k, vectors), :] = value.astype(bf16)
        return carry

    lax.fori_loop(0, groups, send, 0, unroll=8)
    for copy in copies:
        copy.wait()


def pack_rounded(asked, arrays, vectors):
    node = arrays[0].shape[1]
    each = arrays[0].shape[0] // vectors - 2
    groups = lax.axis_size("curve")
    return pl.pallas_call(
        functools.partial(pack_rounded_kernel, each, vectors, groups),
        out_shape=[shaped((groups * CAP * vectors, node), bf16)] + [pltpu.HBM(arrays[0].shape, f32)] * CHUNKS,
        in_specs=[smem()] + [vmem()] * (2 * CHUNKS),
        out_specs=[vmem()] + [anywhere()] * CHUNKS,
        scratch_shapes=[pltpu.SemaphoreType.DMA((CHUNKS,))],
        compiler_params=params(16),
        name="pack_rounded",
    )(asked, *arrays)


def finish_kernel(shares, scale, state_in, drive_in, image_in, out, one, two, mix, state, drive, image, ready, sems):
    places = ((state_in, state), (drive_in, drive), (image_in, image), (ready, out))
    copies = [
        [pltpu.make_async_copy(source.at[v], place.at[v], sems.at[k, v]) for v in range(out.shape[0])]
        for k, (source, place) in enumerate(places)
    ]
    leaving = copies.pop()
    for v in range(out.shape[0]):
        for column in copies:
            column[v].start()
    shape = scale.shape
    vectors = shape[0]
    line = jnp.sum(shares[...], axis=0, keepdims=True)
    form, cross, energy = [as_column(line, shape, e * vectors) for e in range(3)]
    beta_zero = scale[...]
    unit = 1.0 - epsilon / (beta_zero * beta_zero)
    alpha_first = cross / beta_zero
    square = alpha_first * alpha_first
    beta_first = jnp.sqrt(jnp.maximum(energy - square * (2.0 - unit), 0.0) + epsilon)
    alpha_second = (form - 2.0 * alpha_first * energy + square * alpha_first) / (beta_first * beta_first)
    alpha_second = alpha_second - alpha_first * (1.0 - unit)
    term_one = jnp.ones(shape, f32)
    term_two = jnp.zeros(shape, f32)
    total_one, total_two = term_one, term_two
    for turn in range(1, TAYLOR):
        factor = time_step / (turn + 1.0)
        next_one = factor * (alpha_first * term_one + beta_first * term_two)
        next_two = factor * (beta_first * term_one + alpha_second * term_two)
        term_one, term_two = next_one, next_two
        total_one, total_two = total_one + next_one, total_two + next_two
    one[...] = time_step * total_one
    two[...] = time_step * beta_zero * total_two / beta_first
    mix[...] = alpha_first / beta_zero
    width = state.shape[0]
    for v in range(width):
        at = pl.ds(lax.axis_index("band") * width + v, 1)
        size = state.shape[1:]
        weight_one, weight_two, share = [jnp.broadcast_to(ref[at, :], size) for ref in (one, two, mix)]
        for column in copies:
            column[v].wait()
        ready[v] = state[v] + (weight_one * drive[v] + weight_two * (image[v] - share * drive[v]))
        leaving[v].start()
    for copy in leaving:
        copy.wait()


def finish(shares, scale, state, drive, image):
    return pl.pallas_call(
        finish_kernel,
        out_shape=shaped(state.shape, f32),
        in_specs=[vmem()] * 2 + [anywhere()] * 3,
        out_specs=anywhere(),
        scratch_shapes=[pltpu.VMEM(scale.shape, f32)] * 3
        + [pltpu.VMEM(state.shape, f32)] * 4
        + [pltpu.SemaphoreType.DMA((4, state.shape[0]))],
        compiler_params=params(16),
        name="finish",
    )(shares, scale, state, in_hbm(drive), in_hbm(image))


def swap(array, bit):
    size = lax.axis_size("band")
    return lax.ppermute(array, "band", [(k, k ^ bit) for k in range(size)])


def exchange(array):
    return lax.all_to_all(array, "curve", split_axis=0, concat_axis=0, tiled=True)


def band_sum(keep, give, vectors, drive=None):
    each = keep[0].shape[0] // vectors
    came = [swap(array, 1) for array in give]
    codes = [encode(one, two, vectors) for one, two in zip(keep, came)]
    across = []
    for code in codes:
        across.append(swap(code, 2))
    mine, others = [], []
    for c, (code, other) in enumerate(zip(codes, across)):
        mine.append(decode(code, other, vectors, each, drive and drive[c], mine[-1] if c else None))
        others.append(swap(mine[c], 1))
    return mine + others


def body(state, blocks, diag_blocks, block_cols):
    groups = lax.axis_size("curve")
    devices = groups * lax.axis_size("band")
    width, rows = state.shape[:2]
    vectors = width * lax.axis_size("band")
    blocks = in_hbm(blocks)
    diag_blocks = in_hbm(diag_blocks)
    state = in_hbm(state)
    rounded, pick, target, wanted, origin = plan(block_cols.reshape(1, rows), state)
    across = swap(rounded, 2)
    beside = swap(rounded, 1)
    asked = exchange(wanted)
    corner = swap(across, 1)
    parts = [rounded, beside, across, corner]
    field, own, split = spread(parts, origin, blocks)
    message = reply(asked, field, split, vectors)
    halo = exchange(message)
    local = operate_local(pick, target, field, state, blocks, diag_blocks)
    keep, give = settle(wanted, origin, asked, local, halo, own, rows)
    drive = band_sum(keep, give, vectors)
    arrived = exchange(own)
    halo = exchange(pack(asked, origin, drive, vectors))
    keep, give, scale = operate_second(pick, target, asked, drive, halo, arrived, blocks, diag_blocks)
    image = band_sum(keep, give, vectors, drive)
    message, *left = pack_rounded(asked, image, vectors)
    halo = exchange(message)
    image = image[:CHUNKS] + left
    form, left, drive_own, image_own = operate_third(
        pick, wanted, origin, drive, image, own, blocks, diag_blocks, width, vectors
    )
    share = tail(form, left, halo, image[CHUNKS - 1], devices)
    shares = lax.all_to_all(share, ("curve", "band"), split_axis=0, concat_axis=0, tiled=True)
    return finish(shares, scale, state, drive_own, image_own)


def solution(mesh):
    return jax.shard_map(
        body,
        mesh=mesh,
        in_specs=(
            P("band", "curve", None),
            P("curve", "band", None, None),
            P(("curve", "band"), None, None),
            P("curve", "band"),
        ),
        out_specs=P("band", "curve", None),
        check_vma=False,
    )
```

```python
import functools

import jax
import jax.numpy as jnp
from jax import lax
from jax.experimental import pallas as pl
from jax.experimental.pallas import tpu as pltpu
from jax.sharding import PartitionSpec as P


CAP = 2
TAYLOR = 16
UNROLL = 32
CHUNKS = 2

epsilon = 1e-06
time_step = 0.5
quadratic = 1.0
STEP = 256.0
FULL = 32767.0

f32 = jnp.float32
bf16 = jnp.bfloat16
i32 = jnp.int32


def nonlinear(field):
    return quadratic * field * field - field * field * field


def tile(index, rows):
    return pl.ds(pl.multiple_of(index * rows, rows), rows)


def smem():
    return pl.BlockSpec(memory_space=pltpu.SMEM)


def vmem():
    return pl.BlockSpec(memory_space=pltpu.VMEM)


def anywhere():
    return pl.BlockSpec(memory_space=pltpu.HBM)


def params(mebibytes):
    return pltpu.CompilerParams(vmem_limit_bytes=mebibytes * 1024 * 1024)


def in_hbm(array):
    return pltpu.with_memory_space_constraint(array, pltpu.HBM)


def shaped(shape, dtype):
    return jax.ShapeDtypeStruct(shape, dtype)


def times(field, block):
    return lax.dot_general(field, block, (((1,), (0,)), ((), ())), preferred_element_type=f32)


def two(one, other):
    nothing = jnp.zeros_like(one)
    upper = jnp.concatenate([one, nothing], axis=1)
    return jnp.concatenate([upper, jnp.concatenate([nothing, other], axis=1)], axis=0)


def times_two(one, other, blocks):
    value = times(two(one, other), blocks.reshape(-1, blocks.shape[-1]))
    return value[: one.shape[0]], value[one.shape[0] :]


def times_two_transposed(one, other, first, second):
    value = times(two(one, other), jnp.concatenate([first.T, second.T], axis=0))
    return value[: one.shape[0]], value[one.shape[0] :]


def row_sum(part):
    return jnp.sum(part, axis=1, keepdims=True)


def as_column(line, shape, offset=0):
    across = lax.broadcasted_iota(i32, shape, 1)
    down = lax.broadcasted_iota(i32, shape, 0)
    picked = jnp.where(across == down + offset, jnp.broadcast_to(line, shape), 0.0)
    return jnp.broadcast_to(row_sum(picked), shape)


def core_of(band):
    return jnp.bitwise_and(band, 1)


def plan_kernel(cols, state, rounded, pick, target, wanted, origin):
    rounded[...] = state[...].astype(bf16)
    groups, lanes = wanted.shape
    rows = cols.shape[1]
    here = lax.axis_index("curve")
    column = cols[...]
    owner = column // rows
    inner = column - owner * rows
    shape = (groups, rows)
    peer = lax.broadcasted_iota(i32, shape, 0)
    place = lax.broadcasted_iota(i32, shape, 1).astype(f32)
    inside = jnp.broadcast_to(inner.astype(f32), shape)
    left = (jnp.broadcast_to(owner, shape) == peer) & (peer != here)
    number = jnp.zeros((1, rows), f32)
    lane = lax.broadcasted_iota(i32, (groups, lanes), 1)
    want = jnp.full((groups, lanes), -1.0, f32)
    source = jnp.zeros((groups, lanes), f32)
    none = float(rows)
    for k in range(CAP):
        least = jnp.min(jnp.where(left, place, none), axis=1, keepdims=True)
        hit = left & (place == least)
        left = left & (place != least)
        aim = row_sum(jnp.where(hit, inside, 0.0))
        want = jnp.where((lane == k) & (least < none), aim, want)
        source = jnp.where((lane == k) & (least < none), least, source)
        slot = (peer * (2 * CAP) + k).astype(f32)
        number = number + jnp.sum(jnp.where(hit, slot, 0.0), axis=0, keepdims=True)
    wanted[...] = want.astype(i32)
    origin[...] = source.astype(i32)
    pick[...] = jnp.where(owner == here, inner, rows + number.astype(i32))
    target[...] = jnp.where(owner == here, inner, rows)


def plan(cols, state):
    rows = cols.shape[1]
    groups = lax.axis_size("curve")
    return pl.pallas_call(
        plan_kernel,
        out_shape=[shaped(state.shape, bf16)] + [shaped((1, rows), i32)] * 2 + [shaped((groups, 128), i32)] * 2,
        in_specs=[vmem()] * 2,
        out_specs=[vmem()] * 5,
        compiler_params=params(8),
        name="plan",
    )(in_hbm(cols), state)


def spread_kernel(rows, vectors, groups, width, origin, blocks, *refs):
    count = vectors // width
    parts, (field, own, split, wide, sems) = refs[:count], refs[count:]
    slots = groups * CAP

    def fetch(slot):
        peer = slot // CAP
        row = origin[peer, slot - peer * CAP]
        return pltpu.make_async_copy(blocks.at[row, 0], own.at[slot], sems.at[slot])

    def begin(slot, carry):
        fetch(slot).start()
        return carry

    lax.fori_loop(0, slots, begin, 0)
    band = lax.axis_index("band")
    for k, part in enumerate(parts):
        start = jnp.bitwise_xor(band, k) * width
        for v in range(width):
            wide[pl.ds(start + v, rows, stride=vectors), :] = part[v].astype(f32)
    field[0 : rows * vectors, :] = wide[...].astype(bf16)
    field[rows * vectors :, :] = jnp.zeros((vectors, field.shape[1]), bf16)

    def end(slot, carry):
        fetch(slot).wait()
        return carry

    lax.fori_loop(0, slots, end, 0)

    def product(peer, carry):
        fields = [field[tile(origin[peer, k], vectors), :] for k in range(CAP)]
        for k, value in enumerate(times_two(*fields, own[pl.ds(peer * CAP, CAP)])):
            high = value.astype(bf16)
            split[tile(peer * (2 * CAP) + k, vectors), :] = high
            split[tile(peer * (2 * CAP) + CAP + k, vectors), :] = (value - high.astype(f32)).astype(bf16)
        return carry

    lax.fori_loop(0, groups, product, 0, unroll=8)


def spread(parts, origin, blocks):
    width, rows, node = parts[0].shape
    groups = lax.axis_size("curve")
    slots = groups * CAP
    vectors = width * len(parts)
    return pl.pallas_call(
        functools.partial(spread_kernel, rows, vectors, groups, width),
        out_shape=[
            shaped(((rows + 1) * vectors, node), bf16),
            shaped((slots, node, node), bf16),
            shaped((slots * 2 * vectors, node), bf16),
        ],
        in_specs=[smem(), anywhere()] + [vmem()] * len(parts),
        out_specs=[vmem()] * 3,
        scratch_shapes=[pltpu.VMEM((rows * vectors, node), f32), pltpu.SemaphoreType.DMA((slots,))],
        compiler_params=params(10),
        name="spread",
    )(origin, blocks, *parts)


def reply_kernel(vectors, groups, asked, field, split, message):
    def send(peer, carry):
        at = peer * (3 * CAP)
        for k in range(CAP):
            message[tile(at + k, vectors), :] = field[tile(jnp.maximum(asked[peer, k], 0), vectors), :]
        for k in range(2 * CAP):
            message[tile(at + CAP + k, vectors), :] = split[tile(peer * (2 * CAP) + k, vectors), :]
        return carry

    lax.fori_loop(0, groups, send, 0, unroll=8)


def reply(asked, field, split, vectors):
    groups = lax.axis_size("curve")
    return pl.pallas_call(
        functools.partial(reply_kernel, vectors, groups),
        out_shape=shaped((groups * 3 * CAP * vectors, field.shape[1]), bf16),
        in_specs=[smem()] + [vmem()] * 2,
        out_specs=vmem(),
        compiler_params=params(10),
        name="reply",
    )(asked, field, split)


class Stream:
    def __init__(self, blocks, diag, held, held_diag, sems):
        self.blocks, self.diag, self.held, self.held_diag, self.sems = blocks, diag, held, held_diag, sems
        self.pieces = blocks.shape[0] // UNROLL
        self.own = diag.shape[0] // self.pieces

    def copies(self, piece):
        rows = pl.ds(piece * UNROLL, UNROLL)
        own = pl.ds(piece * self.own, self.own)
        return (
            pltpu.make_async_copy(self.blocks.at[rows, 0], self.held.at[rows], self.sems.at[0, piece]),
            pltpu.make_async_copy(self.diag.at[own], self.held_diag.at[own], self.sems.at[1, piece]),
        )

    def start(self):
        for piece in range(self.pieces):
            for copy in self.copies(piece):
                copy.start()

    def wait(self, piece):
        for copy in self.copies(piece):
            copy.wait()


def stream_scratch(blocks, diag):
    rows, node = blocks.shape[0], blocks.shape[-1]
    return [
        pltpu.VMEM((rows, node, node), bf16),
        pltpu.VMEM(diag.shape, bf16),
        pltpu.SemaphoreType.DMA((2, rows // UNROLL)),
    ]


def products(vectors, limit, pick, target, field, stream, total):
    band = lax.axis_index("band")

    def at(row):
        return field[tile(row, vectors), :]

    def source(row):
        place = pick[0, row]
        return at(place if limit is None else jnp.minimum(place, limit))

    def some(piece, carry):
        stream.wait(piece)
        forward, mirrored = [], []
        base = piece * UNROLL
        for u in range(0, UNROLL, 2):
            row = base + u
            forward += times_two_transposed(source(row), source(row + 1), stream.held[row], stream.held[row + 1])
            mirrored += times_two(at(row), at(row + 1), stream.held[pl.ds(row, 2)])
        own = stream.own
        first = band * (own * stream.pieces) + piece * own
        values = []
        for d in range(0, own, 2):
            values += times_two(at(first + d), at(first + d + 1), stream.held_diag[pl.ds(piece * own + d, 2)])
        for u in range(UNROLL):
            total[tile(base + u, vectors), :] += forward[u]
            total[tile(target[0, base + u], vectors), :] += mirrored[u]
        for d, value in enumerate(values):
            total[tile(first + d, vectors), :] += value
        return carry

    lax.fori_loop(0, stream.pieces, some, 0)


def give_out(rows, vectors, total, outs):
    core = core_of(lax.axis_index("band"))
    half = rows // 2
    size = half // CHUNKS * vectors
    for side in range(2):
        start = jnp.where(core == side, 0, half) * vectors
        for c in range(CHUNKS):
            outs[side * CHUNKS + c][...] = total[pl.ds(pl.multiple_of(start + c * size, size), size), :]


def local_kernel(rows, vectors, pick, target, field, state, blocks, diag, total, *scratch):
    stream = Stream(blocks, diag, *scratch)
    stream.start()
    total[...] = jnp.zeros_like(total)
    width = state.shape[0]
    band = lax.axis_index("band")
    for v in range(width):
        total[pl.ds(band * width + v, rows, stride=vectors), :] = nonlinear(state[v])
    products(vectors, rows, pick, target, field, stream, total)


def operate_local(pick, target, field, state, blocks, diag):
    rows, node = blocks.shape[0], blocks.shape[-1]
    vectors = field.shape[0] // (rows + 1)
    return pl.pallas_call(
        functools.partial(local_kernel, rows, vectors),
        out_shape=shaped(((rows + 1) * vectors, node), f32),
        in_specs=[smem()] * 2 + [vmem()] * 2 + [anywhere()] * 2,
        out_specs=vmem(),
        scratch_shapes=stream_scratch(blocks, diag),
        compiler_params=params(17),
        name="operate_local",
    )(pick, target, field, state, blocks, diag)


def settle_kernel(rows, vectors, groups, wanted, origin, asked, local, halo, own, *refs):
    outs, total = refs[:-1], refs[-1]
    total[...] = local[...]

    def some(peer, carry):
        at = peer * (3 * CAP)
        values = []
        fields = [halo[tile(at + k, vectors), :] for k in range(CAP)]
        for k, value in enumerate(times_two_transposed(*fields, own[peer * CAP], own[peer * CAP + 1])):
            values.append((jnp.where(wanted[peer, k] < 0, rows, origin[peer, k]), value))
        for k in range(CAP):
            value = halo[tile(at + CAP + k, vectors), :].astype(f32)
            value = value + halo[tile(at + 2 * CAP + k, vectors), :].astype(f32)
            values.append((jnp.where(asked[peer, k] < 0, rows, asked[peer, k]), value))
        for aim, value in values:
            total[tile(aim, vectors), :] += value
        return carry

    lax.fori_loop(0, groups, some, 0, unroll=8)
    give_out(rows, vectors, total, outs)


def chunk_shapes(rows, vectors, node):
    return [shaped((rows // 2 // CHUNKS * vectors, node), f32)] * (2 * CHUNKS)


def settle(wanted, origin, asked, local, halo, own, rows):
    node = local.shape[1]
    vectors = local.shape[0] // (rows + 1)
    groups = lax.axis_size("curve")
    outs = pl.pallas_call(
        functools.partial(settle_kernel, rows, vectors, groups),
        out_shape=chunk_shapes(rows, vectors, node),
        in_specs=[smem()] * 3 + [vmem()] * 3,
        out_specs=[vmem()] * (2 * CHUNKS),
        scratch_shapes=[pltpu.VMEM(local.shape, f32)],
        compiler_params=params(17),
        name="settle",
    )(wanted, origin, asked, local, halo, own)
    return outs[:CHUNKS], outs[CHUNKS:]


def second_kernel(rows, vectors, groups, pick, target, asked, *refs):
    arrays, (halo, arrived, blocks, diag), refs = refs[: 2 * CHUNKS], refs[2 * CHUNKS : 2 * CHUNKS + 4], refs[2 * CHUNKS + 4 :]
    outs, (scale, field, total), scratch = refs[: 2 * CHUNKS], refs[2 * CHUNKS : 2 * CHUNKS + 3], refs[2 * CHUNKS + 3 :]
    stream = Stream(blocks, diag, *scratch)
    stream.start()
    half = rows // 2
    each = half // CHUNKS
    size = 2 * CAP + 1
    shape = scale.shape

    def gather(g, energy):
        last = from_code(halo[tile(g * size + 2 * CAP, vectors), :])
        digits = last[:, 2 * CAP + 1 : 2 * CAP + 2] + last[:, 2 * CAP + 2 : 2 * CAP + 3] * (1.0 / FULL)
        return energy + digits * scale_of(last)[:, 2 * CAP : 2 * CAP + 1]

    energy = lax.fori_loop(0, groups, gather, jnp.zeros((vectors, 1), f32), unroll=8)
    energy = jnp.broadcast_to(energy * (1.0 / FULL), shape)
    beta = jnp.sqrt(energy + epsilon)
    scale[...] = beta
    inverse = 1.0 / beta
    core = core_of(lax.axis_index("band"))
    for side in range(2):
        start = jnp.where(core == side, 0, half)
        for c in range(CHUNKS):
            array = arrays[side * CHUNKS + c]

            def one(p, carry, start=start, c=c, array=array):
                field[tile(start + c * each + p, vectors), :] = (array[tile(p, vectors), :] * inverse).astype(bf16)
                return carry

            lax.fori_loop(0, each, one, 0, unroll=16)

    def row(g, carry):
        gains = scale_of(from_code(halo[tile(g * size + 2 * CAP, vectors), :])) * (1.0 / FULL)
        for k in range(2 * CAP):
            value = from_code(halo[tile(g * size + k, vectors), :]) * gains[:, k : k + 1] * inverse
            field[tile(rows + g * (2 * CAP) + k, vectors), :] = value.astype(bf16)
        return carry

    lax.fori_loop(0, groups, row, 0, unroll=4)
    total[...] = jnp.zeros_like(total)
    products(vectors, None, pick, target, field, stream, total)

    def some(peer, carry):
        place = rows + peer * (2 * CAP) + CAP
        fields = [field[tile(place + k, vectors), :] for k in range(CAP)]
        for k, value in enumerate(times_two(*fields, arrived[pl.ds(peer * CAP, CAP)])):
            aim = asked[peer, k]
            total[tile(jnp.where(aim < 0, rows, aim), vectors), :] += value
        return carry

    lax.fori_loop(0, groups, some, 0, unroll=8)
    give_out(rows, vectors, total, outs)


def operate_second(pick, target, asked, arrays, halo, arrived, blocks, diag):
    rows, node = blocks.shape[0], blocks.shape[-1]
    groups = lax.axis_size("curve")
    vectors = halo.shape[0] // (groups * (2 * CAP + 1))
    outs = pl.pallas_call(
        functools.partial(second_kernel, rows, vectors, groups),
        out_shape=chunk_shapes(rows, vectors, node) + [shaped((vectors, node), f32)],
        in_specs=[smem()] * 3 + [vmem()] * (2 * CHUNKS + 2) + [anywhere()] * 2,
        out_specs=[vmem()] * (2 * CHUNKS + 1),
        scratch_shapes=[
            pltpu.VMEM(((rows + groups * 2 * CAP) * vectors, node), bf16),
            pltpu.VMEM(((rows + 1) * vectors, node), f32),
        ]
        + stream_scratch(blocks, diag),
        compiler_params=params(18),
        name="operate_second",
    )(pick, target, asked, *arrays, halo, arrived, blocks, diag)
    return outs[:CHUNKS], outs[CHUNKS : 2 * CHUNKS], outs[-1]


def third_kernel(rows, vectors, groups, width, pick, wanted, origin, *refs):
    count = 2 * CHUNKS
    drive, image, (own, blocks, diag), refs = refs[:count], refs[count : 2 * count], refs[2 * count : 2 * count + 3], refs[2 * count + 3 :]
    form, left, drive_own, image_own, field = refs[:5]
    stream = Stream(blocks, diag, *refs[5:])
    stream.start()
    half = rows // 2
    each = half // CHUNKS
    shape = form.shape
    band = lax.axis_index("band")
    core = core_of(band)
    for side in range(2):
        start = jnp.where(core == side, 0, half)
        for c in range(CHUNKS):
            array = image[side * CHUNKS + c]

            def one(p, carry, start=start, c=c, array=array):
                field[tile(start + c * each + p, vectors), :] = array[tile(p, vectors), :].astype(bf16)
                return carry

            lax.fori_loop(0, each, one, 0, unroll=16)
            for v in range(width):
                inside = pl.ds(pl.multiple_of(start + c * each, each), each)
                source = pl.ds(band * width + v, each, stride=vectors)
                drive_own[v, inside, :] = drive[side * CHUNKS + c][source, :]
                image_own[v, inside, :] = array[source, :]
    field[rows * vectors :, :] = jnp.zeros((vectors, shape[1]), bf16)

    def at(row):
        return field[tile(row, vectors), :]

    def some(piece, parts):
        stream.wait(piece)
        twice, once = parts
        base = piece * UNROLL
        for u in range(0, UNROLL, 2):
            row = base + u
            values = times_two(at(row), at(row + 1), stream.held[pl.ds(row, 2)])
            for k, value in enumerate(values):
                source = jnp.minimum(pick[0, row + k], rows)
                twice = twice + value * at(source).astype(f32)
        for d in range(0, stream.own, 2):
            row = (band * stream.pieces + piece) * stream.own + d
            here, there = at(row), at(row + 1)
            one, other = times_two(here, there, stream.held_diag[pl.ds(piece * stream.own + d, 2)])
            once = once + one * here.astype(f32) + other * there.astype(f32)
        return twice, once

    nothing = jnp.zeros(shape, f32)
    twice, once = lax.fori_loop(0, stream.pieces, some, (nothing, nothing))
    form[...] = 2.0 * twice + once

    def remote(peer, carry):
        fields = [at(origin[peer, k]) for k in range(CAP)]
        for k, value in enumerate(times_two(*fields, own[pl.ds(peer * CAP, CAP)])):
            left[tile(peer * CAP + k, vectors), :] = jnp.where(wanted[peer, k] < 0, 0.0, 2.0) * value
        return carry

    lax.fori_loop(0, groups, remote, 0, unroll=8)


def operate_third(pick, wanted, origin, drive, image, own, blocks, diag, width, vectors):
    rows, node = blocks.shape[0], blocks.shape[-1]
    groups = lax.axis_size("curve")
    mine = pltpu.HBM((width, rows, node), f32)
    return pl.pallas_call(
        functools.partial(third_kernel, rows, vectors, groups, width),
        out_shape=[shaped((vectors, node), f32), shaped((groups * CAP * vectors, node), f32), mine, mine],
        in_specs=[smem()] * 3 + [vmem()] * (4 * CHUNKS + 1) + [anywhere()] * 2,
        out_specs=[vmem()] * 4,
        scratch_shapes=[pltpu.VMEM(((rows + 1) * vectors, node), bf16)] + stream_scratch(blocks, diag),
        compiler_params=params(18),
        name="operate_third",
    )(pick, wanted, origin, *drive, *image[:CHUNKS], *map(in_hbm, image[CHUNKS:]), own, blocks, diag)


def tail_kernel(each, vectors, form, left, halo, image, share):
    shape = form.shape
    total = form[...]
    for slot in range(left.shape[0] // vectors):
        at = slot * vectors
        total = total + left[at : at + vectors, :] * halo[at : at + vectors, :].astype(f32)
    values = [total]
    for e in range(2):
        at = (each + e) * vectors
        values.append(0.5 * image[at : at + vectors, :])
    line = jnp.zeros((1, shape[1]), f32)
    across = lax.broadcasted_iota(i32, shape, 1)
    down = lax.broadcasted_iota(i32, shape, 0)
    for e, value in enumerate(values):
        column = jnp.broadcast_to(row_sum(value), shape)
        line = line + jnp.sum(jnp.where(across == down + e * vectors, column, 0.0), axis=0, keepdims=True)
    share[...] = jnp.broadcast_to(line, share.shape)


def tail(form, left, halo, image, devices):
    vectors, node = form.shape
    each = image.shape[0] // vectors - 2
    return pl.pallas_call(
        functools.partial(tail_kernel, each, vectors),
        out_shape=shaped((devices, node), f32),
        in_specs=[vmem()] * 4,
        out_specs=vmem(),
        compiler_params=params(10),
        name="tail",
    )(form, left, halo, image)


def code_tiles(each, node):
    return -(-each // node)


def encode_kernel(each, vectors, keep, came, code, wide):
    node = keep.shape[1]
    lanes = lax.broadcasted_iota(i32, (vectors, node), 1)
    for group in range(code_tiles(each, node)):
        inside = range(group * node, min(each, (group + 1) * node))
        peak = jnp.zeros((vectors, node), f32)
        for p in inside:
            at = p * vectors
            value = keep[at : at + vectors, :] + came[at : at + vectors, :]
            wide[at : at + vectors, :] = value
            peak = jnp.where(lanes == p - group * node, jnp.max(jnp.abs(value), axis=1, keepdims=True), peak)
        power = scale_power(peak)
        start = (each + group) * vectors
        code[start : start + vectors, :] = as_code(power)
        gain = FULL * scale_of(-power)
        for p in inside:
            at = p * vectors
            lane = p - group * node
            scaled = wide[at : at + vectors, :] * gain[:, lane : lane + 1]
            code[at : at + vectors, :] = as_code(jnp.round(scaled))


def encode(keep, came, vectors):
    size, node = keep.shape
    each = size // vectors
    return pl.pallas_call(
        functools.partial(encode_kernel, each, vectors),
        out_shape=shaped(((each + code_tiles(each, node)) * vectors, node), jnp.int16),
        in_specs=[vmem()] * 2,
        out_specs=vmem(),
        scratch_shapes=[pltpu.VMEM((size, node), f32)],
        compiler_params=params(6),
        name="encode",
    )(keep, came)


def decode_kernel(each, vectors, weighted, chained, *refs):
    code, came, out = refs[0], refs[1], refs[-1]
    drive = refs[2] if weighted else None
    node = code.shape[1]
    shape = (vectors, node)
    energy = jnp.zeros(shape, f32)
    cross = jnp.zeros(shape, f32)
    if chained:
        before = refs[-2]
        at = each * vectors
        if weighted:
            cross = before[at : at + vectors, :]
            at = at + vectors
        energy = before[at : at + vectors, :]
    for group in range(code_tiles(each, node)):
        start = (each + group) * vectors
        gains = [
            scale_of(from_code(ref[start : start + vectors, :])) * (1.0 / FULL)
            for ref in (code, came)
        ]
        for p in range(group * node, min(each, (group + 1) * node)):
            at = p * vectors
            lane = p - group * node
            one, two = [
                from_code(ref[at : at + vectors, :]) * gain[:, lane : lane + 1]
                for ref, gain in zip((code, came), gains)
            ]
            value = one + two
            out[at : at + vectors, :] = value
            energy = energy + value * value
            if weighted:
                cross = cross + value * drive[at : at + vectors, :]
    at = each * vectors
    if weighted:
        out[at : at + vectors, :] = cross
        at = at + vectors
    out[at : at + vectors, :] = energy


def decode(code, came, vectors, each, drive=None, before=None):
    node = code.shape[1]
    extra = 1 if drive is None else 2
    inputs = [array for array in (code, came, drive, before) if array is not None]
    return pl.pallas_call(
        functools.partial(decode_kernel, each, vectors, drive is not None, before is not None),
        out_shape=shaped(((each + extra) * vectors, node), f32),
        in_specs=[vmem()] * len(inputs),
        out_specs=vmem(),
        compiler_params=params(6),
        name="decode",
    )(*inputs)


def fetch_row(arrays, each, vectors, row):
    core = core_of(lax.axis_index("band"))
    half = each * CHUNKS
    side = row // half
    inside = row - side * half
    chunk = inside // each
    place = tile(inside - chunk * each, vectors)
    value = arrays[0][place, :]
    number = jnp.where(side == core, chunk, CHUNKS + chunk)
    for k in range(1, 2 * CHUNKS):
        value = jnp.where(number == k, arrays[k][place, :], value)
    return value


def scale_power(peak):
    return jnp.ceil(jnp.log2(jnp.maximum(peak, 1e-30)) * STEP) + 1.0


def scale_of(power):
    return jnp.exp2(power * (1.0 / STEP))


def as_code(value):
    return value.astype(i32).astype(jnp.int16)


def from_code(code):
    return code.astype(i32).astype(f32)


def pack_kernel(each, vectors, groups, asked, origin, *refs):
    arrays, message = refs[:-1], refs[-1]
    shape = (vectors, message.shape[1])
    lanes = lax.broadcasted_iota(i32, shape, 1)
    sums = arrays[CHUNKS - 1][each * vectors :, :] + arrays[2 * CHUNKS - 1][each * vectors :, :]
    energy = jnp.broadcast_to(row_sum(sums), shape)
    power = scale_power(energy)
    digits = energy * (FULL * scale_of(-power))
    high = jnp.floor(digits)
    low = jnp.round((digits - high) * FULL)
    extra = jnp.where(lanes == 2 * CAP, power, jnp.where(lanes == 2 * CAP + 1, high, low))
    size = 2 * CAP + 1

    def send(peer, carry):
        last = extra
        for k in range(2 * CAP):
            row = jnp.maximum(asked[peer, k], 0) if k < CAP else origin[peer, k - CAP]
            value = fetch_row(arrays, each, vectors, row)
            power = scale_power(jnp.broadcast_to(jnp.max(jnp.abs(value), axis=1, keepdims=True), shape))
            message[tile(peer * size + k, vectors), :] = as_code(jnp.round(value * (FULL * scale_of(-power))))
            last = jnp.where(lanes == k, power, last)
        message[tile(peer * size + 2 * CAP, vectors), :] = as_code(last)
        return carry

    lax.fori_loop(0, groups, send, 0, unroll=4)


def pack(asked, origin, arrays, vectors):
    node = arrays[0].shape[1]
    each = arrays[0].shape[0] // vectors - 1
    groups = lax.axis_size("curve")
    return pl.pallas_call(
        functools.partial(pack_kernel, each, vectors, groups),
        out_shape=shaped((groups * (2 * CAP + 1) * vectors, node), jnp.int16),
        in_specs=[smem()] * 2 + [vmem()] * (2 * CHUNKS),
        out_specs=vmem(),
        compiler_params=params(10),
        name="pack",
    )(asked, origin, *arrays)


def pack_rounded_kernel(each, vectors, groups, asked, *refs):
    arrays, message, left, sems = refs[: 2 * CHUNKS], refs[2 * CHUNKS], refs[2 * CHUNKS + 1 : -1], refs[-1]
    copies = [
        pltpu.make_async_copy(array, place, sems.at[c]) for c, (array, place) in enumerate(zip(arrays[CHUNKS:], left))
    ]
    for copy in copies:
        copy.start()

    def send(peer, carry):
        for k in range(CAP):
            value = fetch_row(arrays, each, vectors, jnp.maximum(asked[peer, k], 0))
            message[tile(peer * CAP + k, vectors), :] = value.astype(bf16)
        return carry

    lax.fori_loop(0, groups, send, 0, unroll=8)
    for copy in copies:
        copy.wait()


def pack_rounded(asked, arrays, vectors):
    node = arrays[0].shape[1]
    each = arrays[0].shape[0] // vectors - 2
    groups = lax.axis_size("curve")
    return pl.pallas_call(
        functools.partial(pack_rounded_kernel, each, vectors, groups),
        out_shape=[shaped((groups * CAP * vectors, node), bf16)] + [pltpu.HBM(arrays[0].shape, f32)] * CHUNKS,
        in_specs=[smem()] + [vmem()] * (2 * CHUNKS),
        out_specs=[vmem()] + [anywhere()] * CHUNKS,
        scratch_shapes=[pltpu.SemaphoreType.DMA((CHUNKS,))],
        compiler_params=params(10),
        name="pack_rounded",
    )(asked, *arrays)


def finish_kernel(shares, scale, state_in, drive_in, image_in, out, one, two, mix, state, drive, image, ready, sems):
    places = ((state_in, state), (drive_in, drive), (image_in, image), (ready, out))
    copies = [
        [pltpu.make_async_copy(source.at[v], place.at[v], sems.at[k, v]) for v in range(out.shape[0])]
        for k, (source, place) in enumerate(places)
    ]
    leaving = copies.pop()
    for v in range(out.shape[0]):
        for column in copies:
            column[v].start()
    shape = scale.shape
    vectors = shape[0]
    line = jnp.sum(shares[...], axis=0, keepdims=True)
    form, cross, energy = [as_column(line, shape, e * vectors) for e in range(3)]
    beta_zero = scale[...]
    unit = 1.0 - epsilon / (beta_zero * beta_zero)
    alpha_first = cross / beta_zero
    square = alpha_first * alpha_first
    beta_first = jnp.sqrt(jnp.maximum(energy - square * (2.0 - unit), 0.0) + epsilon)
    alpha_second = (form - 2.0 * alpha_first * energy + square * alpha_first) / (beta_first * beta_first)
    alpha_second = alpha_second - alpha_first * (1.0 - unit)
    term_one = jnp.ones(shape, f32)
    term_two = jnp.zeros(shape, f32)
    total_one, total_two = term_one, term_two
    for turn in range(1, TAYLOR):
        factor = time_step / (turn + 1.0)
        next_one = factor * (alpha_first * term_one + beta_first * term_two)
        next_two = factor * (beta_first * term_one + alpha_second * term_two)
        term_one, term_two = next_one, next_two
        total_one, total_two = total_one + next_one, total_two + next_two
    one[...] = time_step * total_one
    two[...] = time_step * beta_zero * total_two / beta_first
    mix[...] = alpha_first / beta_zero
    width = state.shape[0]
    for v in range(width):
        at = pl.ds(lax.axis_index("band") * width + v, 1)
        size = state.shape[1:]
        weight_one, weight_two, share = [jnp.broadcast_to(ref[at, :], size) for ref in (one, two, mix)]
        for column in copies:
            column[v].wait()
        ready[v] = state[v] + (weight_one * drive[v] + weight_two * (image[v] - share * drive[v]))
        leaving[v].start()
    for copy in leaving:
        copy.wait()


def finish(shares, scale, state, drive, image):
    return pl.pallas_call(
        finish_kernel,
        out_shape=shaped(state.shape, f32),
        in_specs=[vmem()] * 2 + [anywhere()] * 3,
        out_specs=anywhere(),
        scratch_shapes=[pltpu.VMEM(scale.shape, f32)] * 3
        + [pltpu.VMEM(state.shape, f32)] * 4
        + [pltpu.SemaphoreType.DMA((4, state.shape[0]))],
        compiler_params=params(10),
        name="finish",
    )(shares, scale, state, in_hbm(drive), in_hbm(image))


def swap(array, bit):
    size = lax.axis_size("band")
    return lax.ppermute(array, "band", [(k, k ^ bit) for k in range(size)])


def exchange(array):
    return lax.all_to_all(array, "curve", split_axis=0, concat_axis=0, tiled=True)


def band_sum(keep, give, vectors, drive=None):
    each = keep[0].shape[0] // vectors
    came = [swap(array, 1) for array in give]
    codes = [encode(one, two, vectors) for one, two in zip(keep, came)]
    across = []
    for code in codes:
        across.append(swap(code, 2))
    mine, others = [], []
    for c, (code, other) in enumerate(zip(codes, across)):
        mine.append(decode(code, other, vectors, each, drive and drive[c], mine[-1] if c else None))
        others.append(swap(mine[c], 1))
    return mine + others


def body(state, blocks, diag_blocks, block_cols):
    groups = lax.axis_size("curve")
    devices = groups * lax.axis_size("band")
    width, rows = state.shape[:2]
    vectors = width * lax.axis_size("band")
    blocks = in_hbm(blocks)
    diag_blocks = in_hbm(diag_blocks)
    state = in_hbm(state)
    rounded, pick, target, wanted, origin = plan(block_cols.reshape(1, rows), state)
    across = swap(rounded, 2)
    beside = swap(rounded, 1)
    asked = exchange(wanted)
    corner = swap(across, 1)
    parts = [rounded, beside, across, corner]
    field, own, split = spread(parts, origin, blocks)
    message = reply(asked, field, split, vectors)
    halo = exchange(message)
    local = operate_local(pick, target, field, state, blocks, diag_blocks)
    keep, give = settle(wanted, origin, asked, local, halo, own, rows)
    drive = band_sum(keep, give, vectors)
    arrived = exchange(own)
    halo = exchange(pack(asked, origin, drive, vectors))
    keep, give, scale = operate_second(pick, target, asked, drive, halo, arrived, blocks, diag_blocks)
    image = band_sum(keep, give, vectors, drive)
    message, *left = pack_rounded(asked, image, vectors)
    halo = exchange(message)
    image = image[:CHUNKS] + left
    form, left, drive_own, image_own = operate_third(
        pick, wanted, origin, drive, image, own, blocks, diag_blocks, width, vectors
    )
    share = tail(form, left, halo, image[CHUNKS - 1], devices)
    shares = lax.all_to_all(share, ("curve", "band"), split_axis=0, concat_axis=0, tiled=True)
    return finish(shares, scale, state, drive_own, image_own)


def solution(mesh):
    return jax.shard_map(
        body,
        mesh=mesh,
        in_specs=(
            P("band", "curve", None),
            P("curve", "band", None, None),
            P(("curve", "band"), None, None),
            P("curve", "band"),
        ),
        out_specs=P("band", "curve", None),
        check_vma=False,
    )
```

```python
import functools

import jax
import jax.numpy as jnp
from jax import lax
from jax.experimental import pallas as pl
from jax.experimental.pallas import tpu as pltpu
from jax.sharding import PartitionSpec as P


CAP = 2
TAYLOR = 16
UNROLL = 32
CHUNKS = 2

epsilon = 1e-06
time_step = 0.5
quadratic = 1.0
STEP = 256.0
FULL = 32767.0

f32 = jnp.float32
bf16 = jnp.bfloat16
i32 = jnp.int32


def nonlinear(field):
    return quadratic * field * field - field * field * field


def tile(index, rows):
    return pl.ds(pl.multiple_of(index * rows, rows), rows)


def smem():
    return pl.BlockSpec(memory_space=pltpu.SMEM)


def vmem():
    return pl.BlockSpec(memory_space=pltpu.VMEM)


def anywhere():
    return pl.BlockSpec(memory_space=pltpu.HBM)


def params(mebibytes):
    return pltpu.CompilerParams(vmem_limit_bytes=mebibytes * 1024 * 1024)


def in_hbm(array):
    return pltpu.with_memory_space_constraint(array, pltpu.HBM)


def shaped(shape, dtype):
    return jax.ShapeDtypeStruct(shape, dtype)


def times(field, block):
    return lax.dot_general(field, block, (((1,), (0,)), ((), ())), preferred_element_type=f32)


def two(one, other):
    nothing = jnp.zeros_like(one)
    upper = jnp.concatenate([one, nothing], axis=1)
    return jnp.concatenate([upper, jnp.concatenate([nothing, other], axis=1)], axis=0)


def times_two(one, other, blocks):
    value = times(two(one, other), blocks.reshape(-1, blocks.shape[-1]))
    return value[: one.shape[0]], value[one.shape[0] :]


def times_two_transposed(one, other, first, second):
    value = times(two(one, other), jnp.concatenate([first.T, second.T], axis=0))
    return value[: one.shape[0]], value[one.shape[0] :]


def row_sum(part):
    return jnp.sum(part, axis=1, keepdims=True)


def as_column(line, shape, offset=0):
    across = lax.broadcasted_iota(i32, shape, 1)
    down = lax.broadcasted_iota(i32, shape, 0)
    picked = jnp.where(across == down + offset, jnp.broadcast_to(line, shape), 0.0)
    return jnp.broadcast_to(row_sum(picked), shape)


def core_of(band):
    return jnp.bitwise_and(band, 1)


def plan_kernel(cols, state, rounded, pick, target, wanted, origin):
    rounded[...] = state[...].astype(bf16)
    groups, lanes = wanted.shape
    rows = cols.shape[1]
    here = lax.axis_index("curve")
    column = cols[...]
    owner = column // rows
    inner = column - owner * rows
    shape = (groups, rows)
    peer = lax.broadcasted_iota(i32, shape, 0)
    place = lax.broadcasted_iota(i32, shape, 1).astype(f32)
    inside = jnp.broadcast_to(inner.astype(f32), shape)
    left = (jnp.broadcast_to(owner, shape) == peer) & (peer != here)
    number = jnp.zeros((1, rows), f32)
    lane = lax.broadcasted_iota(i32, (groups, lanes), 1)
    want = jnp.full((groups, lanes), -1.0, f32)
    source = jnp.zeros((groups, lanes), f32)
    none = float(rows)
    for k in range(CAP):
        least = jnp.min(jnp.where(left, place, none), axis=1, keepdims=True)
        hit = left & (place == least)
        left = left & (place != least)
        aim = row_sum(jnp.where(hit, inside, 0.0))
        want = jnp.where((lane == k) & (least < none), aim, want)
        source = jnp.where((lane == k) & (least < none), least, source)
        slot = (peer * (2 * CAP) + k).astype(f32)
        number = number + jnp.sum(jnp.where(hit, slot, 0.0), axis=0, keepdims=True)
    wanted[...] = want.astype(i32)
    origin[...] = source.astype(i32)
    pick[...] = jnp.where(owner == here, inner, rows + number.astype(i32))
    target[...] = jnp.where(owner == here, inner, rows)


def plan(cols, state):
    rows = cols.shape[1]
    groups = lax.axis_size("curve")
    return pl.pallas_call(
        plan_kernel,
        out_shape=[shaped(state.shape, bf16)] + [shaped((1, rows), i32)] * 2 + [shaped((groups, 128), i32)] * 2,
        in_specs=[vmem()] * 2,
        out_specs=[vmem()] * 5,
        compiler_params=params(8),
        name="plan",
    )(in_hbm(cols), state)


def spread_kernel(rows, vectors, groups, width, origin, blocks, *refs):
    count = vectors // width
    parts, (field, own, split, wide, sems) = refs[:count], refs[count:]
    slots = groups * CAP

    def fetch(slot):
        peer = slot // CAP
        row = origin[peer, slot - peer * CAP]
        return pltpu.make_async_copy(blocks.at[row, 0], own.at[slot], sems.at[slot])

    def begin(slot, carry):
        fetch(slot).start()
        return carry

    lax.fori_loop(0, slots, begin, 0)
    band = lax.axis_index("band")
    for k, part in enumerate(parts):
        start = jnp.bitwise_xor(band, k) * width
        for v in range(width):
            wide[pl.ds(start + v, rows, stride=vectors), :] = part[v].astype(f32)
    field[0 : rows * vectors, :] = wide[...].astype(bf16)
    field[rows * vectors :, :] = jnp.zeros((vectors, field.shape[1]), bf16)

    def end(slot, carry):
        fetch(slot).wait()
        return carry

    lax.fori_loop(0, slots, end, 0)

    def product(peer, carry):
        fields = [field[tile(origin[peer, k], vectors), :] for k in range(CAP)]
        for k, value in enumerate(times_two(*fields, own[pl.ds(peer * CAP, CAP)])):
            high = value.astype(bf16)
            split[tile(peer * (2 * CAP) + k, vectors), :] = high
            split[tile(peer * (2 * CAP) + CAP + k, vectors), :] = (value - high.astype(f32)).astype(bf16)
        return carry

    lax.fori_loop(0, groups, product, 0, unroll=8)


def spread(parts, origin, blocks):
    width, rows, node = parts[0].shape
    groups = lax.axis_size("curve")
    slots = groups * CAP
    vectors = width * len(parts)
    return pl.pallas_call(
        functools.partial(spread_kernel, rows, vectors, groups, width),
        out_shape=[
            shaped(((rows + 1) * vectors, node), bf16),
            shaped((slots, node, node), bf16),
            shaped((slots * 2 * vectors, node), bf16),
        ],
        in_specs=[smem(), anywhere()] + [vmem()] * len(parts),
        out_specs=[vmem()] * 3,
        scratch_shapes=[pltpu.VMEM((rows * vectors, node), f32), pltpu.SemaphoreType.DMA((slots,))],
        compiler_params=params(10),
        name="spread",
    )(origin, blocks, *parts)


def reply_kernel(vectors, groups, asked, field, split, message):
    def send(peer, carry):
        at = peer * (3 * CAP)
        for k in range(CAP):
            message[tile(at + k, vectors), :] = field[tile(jnp.maximum(asked[peer, k], 0), vectors), :]
        for k in range(2 * CAP):
            message[tile(at + CAP + k, vectors), :] = split[tile(peer * (2 * CAP) + k, vectors), :]
        return carry

    lax.fori_loop(0, groups, send, 0, unroll=8)


def reply(asked, field, split, vectors):
    groups = lax.axis_size("curve")
    return pl.pallas_call(
        functools.partial(reply_kernel, vectors, groups),
        out_shape=shaped((groups * 3 * CAP * vectors, field.shape[1]), bf16),
        in_specs=[smem()] + [vmem()] * 2,
        out_specs=vmem(),
        compiler_params=params(10),
        name="reply",
    )(asked, field, split)


class Stream:
    def __init__(self, blocks, diag, held, held_diag, sems):
        self.blocks, self.diag, self.held, self.held_diag, self.sems = blocks, diag, held, held_diag, sems
        self.pieces = blocks.shape[0] // UNROLL
        self.own = diag.shape[0] // self.pieces

    def copies(self, piece):
        rows = pl.ds(piece * UNROLL, UNROLL)
        own = pl.ds(piece * self.own, self.own)
        return (
            pltpu.make_async_copy(self.blocks.at[rows, 0], self.held.at[rows], self.sems.at[0, piece]),
            pltpu.make_async_copy(self.diag.at[own], self.held_diag.at[own], self.sems.at[1, piece]),
        )

    def start(self):
        for piece in range(self.pieces):
            for copy in self.copies(piece):
                copy.start()

    def wait(self, piece):
        for copy in self.copies(piece):
            copy.wait()


def stream_scratch(blocks, diag):
    rows, node = blocks.shape[0], blocks.shape[-1]
    return [
        pltpu.VMEM((rows, node, node), bf16),
        pltpu.VMEM(diag.shape, bf16),
        pltpu.SemaphoreType.DMA((2, rows // UNROLL)),
    ]


def products(vectors, limit, pick, target, field, stream, total):
    band = lax.axis_index("band")

    def at(row):
        return field[tile(row, vectors), :]

    def source(row):
        place = pick[0, row]
        return at(place if limit is None else jnp.minimum(place, limit))

    def some(piece, carry):
        stream.wait(piece)
        forward, mirrored = [], []
        base = piece * UNROLL
        for u in range(0, UNROLL, 2):
            row = base + u
            forward += times_two_transposed(source(row), source(row + 1), stream.held[row], stream.held[row + 1])
            mirrored += times_two(at(row), at(row + 1), stream.held[pl.ds(row, 2)])
        own = stream.own
        first = band * (own * stream.pieces) + piece * own
        values = []
        for d in range(0, own, 2):
            values += times_two(at(first + d), at(first + d + 1), stream.held_diag[pl.ds(piece * own + d, 2)])
        for u in range(UNROLL):
            total[tile(base + u, vectors), :] += forward[u]
            total[tile(target[0, base + u], vectors), :] += mirrored[u]
        for d, value in enumerate(values):
            total[tile(first + d, vectors), :] += value
        return carry

    lax.fori_loop(0, stream.pieces, some, 0)


def give_out(rows, vectors, total, outs):
    core = core_of(lax.axis_index("band"))
    half = rows // 2
    size = half // CHUNKS * vectors
    for side in range(2):
        start = jnp.where(core == side, 0, half) * vectors
        for c in range(CHUNKS):
            outs[side * CHUNKS + c][...] = total[pl.ds(pl.multiple_of(start + c * size, size), size), :]


def local_kernel(rows, vectors, pick, target, field, state, blocks, diag, total, *scratch):
    stream = Stream(blocks, diag, *scratch)
    stream.start()
    total[...] = jnp.zeros_like(total)
    width = state.shape[0]
    band = lax.axis_index("band")
    for v in range(width):
        total[pl.ds(band * width + v, rows, stride=vectors), :] = nonlinear(state[v])
    products(vectors, rows, pick, target, field, stream, total)


def operate_local(pick, target, field, state, blocks, diag):
    rows, node = blocks.shape[0], blocks.shape[-1]
    vectors = field.shape[0] // (rows + 1)
    return pl.pallas_call(
        functools.partial(local_kernel, rows, vectors),
        out_shape=shaped(((rows + 1) * vectors, node), f32),
        in_specs=[smem()] * 2 + [vmem()] * 2 + [anywhere()] * 2,
        out_specs=vmem(),
        scratch_shapes=stream_scratch(blocks, diag),
        compiler_params=params(17),
        name="operate_local",
    )(pick, target, field, state, blocks, diag)


def settle_kernel(rows, vectors, groups, wanted, origin, asked, local, halo, own, *refs):
    outs, total = refs[:-1], refs[-1]
    total[...] = local[...]

    def some(peer, carry):
        at = peer * (3 * CAP)
        values = []
        fields = [halo[tile(at + k, vectors), :] for k in range(CAP)]
        for k, value in enumerate(times_two_transposed(*fields, own[peer * CAP], own[peer * CAP + 1])):
            values.append((jnp.where(wanted[peer, k] < 0, rows, origin[peer, k]), value))
        for k in range(CAP):
            value = halo[tile(at + CAP + k, vectors), :].astype(f32)
            value = value + halo[tile(at + 2 * CAP + k, vectors), :].astype(f32)
            values.append((jnp.where(asked[peer, k] < 0, rows, asked[peer, k]), value))
        for aim, value in values:
            total[tile(aim, vectors), :] += value
        return carry

    lax.fori_loop(0, groups, some, 0, unroll=8)
    give_out(rows, vectors, total, outs)


def chunk_shapes(rows, vectors, node):
    return [shaped((rows // 2 // CHUNKS * vectors, node), f32)] * (2 * CHUNKS)


def settle(wanted, origin, asked, local, halo, own, rows):
    node = local.shape[1]
    vectors = local.shape[0] // (rows + 1)
    groups = lax.axis_size("curve")
    shapes = chunk_shapes(rows, vectors, node)
    shapes[CHUNKS - 1] = pltpu.HBM(shapes[0].shape, f32)
    outs = pl.pallas_call(
        functools.partial(settle_kernel, rows, vectors, groups),
        out_shape=shapes,
        in_specs=[smem()] * 3 + [vmem()] * 3,
        out_specs=[vmem()] * (2 * CHUNKS),
        scratch_shapes=[pltpu.VMEM(local.shape, f32)],
        compiler_params=params(17),
        name="settle",
    )(wanted, origin, asked, local, halo, own)
    return outs[:CHUNKS], outs[CHUNKS:]


def second_kernel(rows, vectors, groups, pick, target, asked, *refs):
    arrays, (halo, arrived, blocks, diag), refs = refs[: 2 * CHUNKS], refs[2 * CHUNKS : 2 * CHUNKS + 4], refs[2 * CHUNKS + 4 :]
    outs, (scale, field, total), scratch = refs[: 2 * CHUNKS], refs[2 * CHUNKS : 2 * CHUNKS + 3], refs[2 * CHUNKS + 3 :]
    stream = Stream(blocks, diag, *scratch)
    stream.start()
    half = rows // 2
    each = half // CHUNKS
    size = 2 * CAP + 1
    shape = scale.shape

    def gather(g, energy):
        last = from_code(halo[tile(g * size + 2 * CAP, vectors), :])
        digits = last[:, 2 * CAP + 1 : 2 * CAP + 2] + last[:, 2 * CAP + 2 : 2 * CAP + 3] * (1.0 / FULL)
        return energy + digits * scale_of(last)[:, 2 * CAP : 2 * CAP + 1]

    energy = lax.fori_loop(0, groups, gather, jnp.zeros((vectors, 1), f32), unroll=8)
    energy = jnp.broadcast_to(energy * (1.0 / FULL), shape)
    beta = jnp.sqrt(energy + epsilon)
    scale[...] = beta
    inverse = 1.0 / beta
    core = core_of(lax.axis_index("band"))
    for side in range(2):
        start = jnp.where(core == side, 0, half)
        for c in range(CHUNKS):
            array = arrays[side * CHUNKS + c]

            def one(p, carry, start=start, c=c, array=array):
                field[tile(start + c * each + p, vectors), :] = (array[tile(p, vectors), :] * inverse).astype(bf16)
                return carry

            lax.fori_loop(0, each, one, 0, unroll=16)

    def row(g, carry):
        gains = scale_of(from_code(halo[tile(g * size + 2 * CAP, vectors), :])) * (1.0 / FULL)
        for k in range(2 * CAP):
            value = from_code(halo[tile(g * size + k, vectors), :]) * gains[:, k : k + 1] * inverse
            field[tile(rows + g * (2 * CAP) + k, vectors), :] = value.astype(bf16)
        return carry

    lax.fori_loop(0, groups, row, 0, unroll=4)
    total[...] = jnp.zeros_like(total)
    products(vectors, None, pick, target, field, stream, total)

    def some(peer, carry):
        place = rows + peer * (2 * CAP) + CAP
        fields = [field[tile(place + k, vectors), :] for k in range(CAP)]
        for k, value in enumerate(times_two(*fields, arrived[pl.ds(peer * CAP, CAP)])):
            aim = asked[peer, k]
            total[tile(jnp.where(aim < 0, rows, aim), vectors), :] += value
        return carry

    lax.fori_loop(0, groups, some, 0, unroll=8)
    give_out(rows, vectors, total, outs)


def operate_second(pick, target, asked, arrays, halo, arrived, blocks, diag):
    rows, node = blocks.shape[0], blocks.shape[-1]
    groups = lax.axis_size("curve")
    vectors = halo.shape[0] // (groups * (2 * CAP + 1))
    outs = pl.pallas_call(
        functools.partial(second_kernel, rows, vectors, groups),
        out_shape=chunk_shapes(rows, vectors, node) + [shaped((vectors, node), f32)],
        in_specs=[smem()] * 3 + [vmem()] * (2 * CHUNKS + 2) + [anywhere()] * 2,
        out_specs=[vmem()] * (2 * CHUNKS + 1),
        scratch_shapes=[
            pltpu.VMEM(((rows + groups * 2 * CAP) * vectors, node), bf16),
            pltpu.VMEM(((rows + 1) * vectors, node), f32),
        ]
        + stream_scratch(blocks, diag),
        compiler_params=params(18),
        name="operate_second",
    )(pick, target, asked, *arrays, halo, arrived, blocks, diag)
    return outs[:CHUNKS], outs[CHUNKS : 2 * CHUNKS], outs[-1]


def third_kernel(rows, vectors, groups, width, pick, wanted, origin, *refs):
    count = 2 * CHUNKS
    image, (own, blocks, diag), refs = refs[:count], refs[count : count + 3], refs[count + 3 :]
    form, left, image_out, field, image_own, sem = refs[:6]
    stream = Stream(blocks, diag, *refs[6:])
    stream.start()
    leaving = pltpu.make_async_copy(image_own, image_out, sem)
    half = rows // 2
    each = half // CHUNKS
    shape = form.shape
    band = lax.axis_index("band")
    core = core_of(band)
    for side in range(2):
        start = jnp.where(core == side, 0, half)
        for c in range(CHUNKS):
            array = image[side * CHUNKS + c]

            def one(p, carry, start=start, c=c, array=array):
                field[tile(start + c * each + p, vectors), :] = array[tile(p, vectors), :].astype(bf16)
                return carry

            lax.fori_loop(0, each, one, 0, unroll=16)
            for v in range(width):
                inside = pl.ds(pl.multiple_of(start + c * each, each), each)
                source = pl.ds(band * width + v, each, stride=vectors)
                image_own[v, inside, :] = array[source, :]
    leaving.start()
    field[rows * vectors :, :] = jnp.zeros((vectors, shape[1]), bf16)

    def at(row):
        return field[tile(row, vectors), :]

    def some(piece, parts):
        stream.wait(piece)
        twice, once = parts
        base = piece * UNROLL
        for u in range(0, UNROLL, 2):
            row = base + u
            values = times_two(at(row), at(row + 1), stream.held[pl.ds(row, 2)])
            for k, value in enumerate(values):
                source = jnp.minimum(pick[0, row + k], rows)
                twice = twice + value * at(source).astype(f32)
        for d in range(0, stream.own, 2):
            row = (band * stream.pieces + piece) * stream.own + d
            here, there = at(row), at(row + 1)
            one, other = times_two(here, there, stream.held_diag[pl.ds(piece * stream.own + d, 2)])
            once = once + one * here.astype(f32) + other * there.astype(f32)
        return twice, once

    nothing = jnp.zeros(shape, f32)
    twice, once = lax.fori_loop(0, stream.pieces, some, (nothing, nothing))
    form[...] = 2.0 * twice + once

    def remote(peer, carry):
        fields = [at(origin[peer, k]) for k in range(CAP)]
        for k, value in enumerate(times_two(*fields, own[pl.ds(peer * CAP, CAP)])):
            left[tile(peer * CAP + k, vectors), :] = jnp.where(wanted[peer, k] < 0, 0.0, 2.0) * value
        return carry

    lax.fori_loop(0, groups, remote, 0, unroll=8)
    leaving.wait()


def operate_third(pick, wanted, origin, image, own, blocks, diag, width, vectors):
    rows, node = blocks.shape[0], blocks.shape[-1]
    groups = lax.axis_size("curve")
    mine = pltpu.HBM((width, rows, node), f32)
    return pl.pallas_call(
        functools.partial(third_kernel, rows, vectors, groups, width),
        out_shape=[shaped((vectors, node), f32), shaped((groups * CAP * vectors, node), f32), mine],
        in_specs=[smem()] * 3 + [vmem()] * (2 * CHUNKS + 1) + [anywhere()] * 2,
        out_specs=[vmem()] * 2 + [anywhere()],
        scratch_shapes=[
            pltpu.VMEM(((rows + 1) * vectors, node), bf16),
            pltpu.VMEM((width, rows, node), f32),
            pltpu.SemaphoreType.DMA(()),
        ]
        + stream_scratch(blocks, diag),
        compiler_params=params(18),
        name="operate_third",
    )(pick, wanted, origin, *image[:CHUNKS], *map(in_hbm, image[CHUNKS:]), own, blocks, diag)


def select_kernel(each, vectors, *refs):
    arrays, out = refs[:-1], refs[-1]
    width = out.shape[0]
    band = lax.axis_index("band")
    core = core_of(band)
    for side in range(2):
        start = jnp.where(core == side, 0, each * CHUNKS)
        for c in range(CHUNKS):
            inside = pl.ds(pl.multiple_of(start + c * each, each), each)
            for v in range(width):
                source = pl.ds(band * width + v, each, stride=vectors)
                out[v, inside, :] = arrays[side * CHUNKS + c][source, :]


def select_own(arrays, width, rows, vectors):
    node = arrays[0].shape[1]
    return pl.pallas_call(
        functools.partial(select_kernel, rows // 2 // CHUNKS, vectors),
        out_shape=pltpu.HBM((width, rows, node), f32),
        in_specs=[vmem()] * (2 * CHUNKS),
        out_specs=vmem(),
        compiler_params=params(10),
        name="select_own",
    )(*arrays)


def tail_kernel(each, vectors, form, left, halo, image, share):
    shape = form.shape
    total = form[...]
    for slot in range(left.shape[0] // vectors):
        at = slot * vectors
        total = total + left[at : at + vectors, :] * halo[at : at + vectors, :].astype(f32)
    values = [total]
    for e in range(2):
        at = (each + e) * vectors
        values.append(0.5 * image[at : at + vectors, :])
    line = jnp.zeros((1, shape[1]), f32)
    across = lax.broadcasted_iota(i32, shape, 1)
    down = lax.broadcasted_iota(i32, shape, 0)
    for e, value in enumerate(values):
        column = jnp.broadcast_to(row_sum(value), shape)
        line = line + jnp.sum(jnp.where(across == down + e * vectors, column, 0.0), axis=0, keepdims=True)
    share[...] = jnp.broadcast_to(line, share.shape)


def tail(form, left, halo, image, devices):
    vectors, node = form.shape
    each = image.shape[0] // vectors - 2
    return pl.pallas_call(
        functools.partial(tail_kernel, each, vectors),
        out_shape=shaped((devices, node), f32),
        in_specs=[vmem()] * 4,
        out_specs=vmem(),
        compiler_params=params(10),
        name="tail",
    )(form, left, halo, image)


def code_tiles(each, node):
    return -(-each // node)


def encode_kernel(each, vectors, keep, came, code, wide):
    node = keep.shape[1]
    lanes = lax.broadcasted_iota(i32, (vectors, node), 1)
    for group in range(code_tiles(each, node)):
        inside = range(group * node, min(each, (group + 1) * node))
        peak = jnp.zeros((vectors, node), f32)
        for p in inside:
            at = p * vectors
            value = keep[at : at + vectors, :] + came[at : at + vectors, :]
            wide[at : at + vectors, :] = value
            peak = jnp.where(lanes == p - group * node, jnp.max(jnp.abs(value), axis=1, keepdims=True), peak)
        power = scale_power(peak)
        start = (each + group) * vectors
        code[start : start + vectors, :] = as_code(power)
        gain = FULL * scale_of(-power)
        for p in inside:
            at = p * vectors
            lane = p - group * node
            scaled = wide[at : at + vectors, :] * gain[:, lane : lane + 1]
            code[at : at + vectors, :] = as_code(jnp.round(scaled))


def encode(keep, came, vectors):
    size, node = keep.shape
    each = size // vectors
    return pl.pallas_call(
        functools.partial(encode_kernel, each, vectors),
        out_shape=shaped(((each + code_tiles(each, node)) * vectors, node), jnp.int16),
        in_specs=[vmem()] * 2,
        out_specs=vmem(),
        scratch_shapes=[pltpu.VMEM((size, node), f32)],
        compiler_params=params(6),
        name="encode",
    )(keep, came)


def decode_kernel(each, vectors, weighted, chained, *refs):
    code, came, out = refs[0], refs[1], refs[-1]
    drive = refs[2] if weighted else None
    node = code.shape[1]
    shape = (vectors, node)
    energy = jnp.zeros(shape, f32)
    cross = jnp.zeros(shape, f32)
    if chained:
        before = refs[-2]
        at = each * vectors
        if weighted:
            cross = before[at : at + vectors, :]
            at = at + vectors
        energy = before[at : at + vectors, :]
    for group in range(code_tiles(each, node)):
        start = (each + group) * vectors
        gains = [
            scale_of(from_code(ref[start : start + vectors, :])) * (1.0 / FULL)
            for ref in (code, came)
        ]
        for p in range(group * node, min(each, (group + 1) * node)):
            at = p * vectors
            lane = p - group * node
            one, two = [
                from_code(ref[at : at + vectors, :]) * gain[:, lane : lane + 1]
                for ref, gain in zip((code, came), gains)
            ]
            value = one + two
            out[at : at + vectors, :] = value
            energy = energy + value * value
            if weighted:
                cross = cross + value * drive[at : at + vectors, :]
    at = each * vectors
    if weighted:
        out[at : at + vectors, :] = cross
        at = at + vectors
    out[at : at + vectors, :] = energy


def decode(code, came, vectors, each, drive=None, before=None):
    node = code.shape[1]
    extra = 1 if drive is None else 2
    inputs = [array for array in (code, came, drive, before) if array is not None]
    return pl.pallas_call(
        functools.partial(decode_kernel, each, vectors, drive is not None, before is not None),
        out_shape=shaped(((each + extra) * vectors, node), f32),
        in_specs=[vmem()] * len(inputs),
        out_specs=vmem(),
        compiler_params=params(6),
        name="decode",
    )(*inputs)


def fetch_row(arrays, each, vectors, row):
    core = core_of(lax.axis_index("band"))
    half = each * CHUNKS
    side = row // half
    inside = row - side * half
    chunk = inside // each
    place = tile(inside - chunk * each, vectors)
    value = arrays[0][place, :]
    number = jnp.where(side == core, chunk, CHUNKS + chunk)
    for k in range(1, 2 * CHUNKS):
        value = jnp.where(number == k, arrays[k][place, :], value)
    return value


def scale_power(peak):
    return jnp.ceil(jnp.log2(jnp.maximum(peak, 1e-30)) * STEP) + 1.0


def scale_of(power):
    return jnp.exp2(power * (1.0 / STEP))


def as_code(value):
    return value.astype(i32).astype(jnp.int16)


def from_code(code):
    return code.astype(i32).astype(f32)


def pack_kernel(each, vectors, groups, asked, origin, *refs):
    arrays, message = refs[:-1], refs[-1]
    shape = (vectors, message.shape[1])
    lanes = lax.broadcasted_iota(i32, shape, 1)
    sums = arrays[CHUNKS - 1][each * vectors :, :] + arrays[2 * CHUNKS - 1][each * vectors :, :]
    energy = jnp.broadcast_to(row_sum(sums), shape)
    power = scale_power(energy)
    digits = energy * (FULL * scale_of(-power))
    high = jnp.floor(digits)
    low = jnp.round((digits - high) * FULL)
    extra = jnp.where(lanes == 2 * CAP, power, jnp.where(lanes == 2 * CAP + 1, high, low))
    size = 2 * CAP + 1

    def send(peer, carry):
        last = extra
        for k in range(2 * CAP):
            row = jnp.maximum(asked[peer, k], 0) if k < CAP else origin[peer, k - CAP]
            value = fetch_row(arrays, each, vectors, row)
            power = scale_power(jnp.broadcast_to(jnp.max(jnp.abs(value), axis=1, keepdims=True), shape))
            message[tile(peer * size + k, vectors), :] = as_code(jnp.round(value * (FULL * scale_of(-power))))
            last = jnp.where(lanes == k, power, last)
        message[tile(peer * size + 2 * CAP, vectors), :] = as_code(last)
        return carry

    lax.fori_loop(0, groups, send, 0, unroll=4)


def pack(asked, origin, arrays, vectors):
    node = arrays[0].shape[1]
    each = arrays[0].shape[0] // vectors - 1
    groups = lax.axis_size("curve")
    return pl.pallas_call(
        functools.partial(pack_kernel, each, vectors, groups),
        out_shape=shaped((groups * (2 * CAP + 1) * vectors, node), jnp.int16),
        in_specs=[smem()] * 2 + [vmem()] * (2 * CHUNKS),
        out_specs=vmem(),
        compiler_params=params(10),
        name="pack",
    )(asked, origin, *arrays)


def pack_rounded_kernel(each, vectors, groups, asked, *refs):
    arrays, message, left, sems = refs[: 2 * CHUNKS], refs[2 * CHUNKS], refs[2 * CHUNKS + 1 : -1], refs[-1]
    copies = [
        pltpu.make_async_copy(array, place, sems.at[c]) for c, (array, place) in enumerate(zip(arrays[CHUNKS:], left))
    ]
    for copy in copies:
        copy.start()

    def send(peer, carry):
        for k in range(CAP):
            value = fetch_row(arrays, each, vectors, jnp.maximum(asked[peer, k], 0))
            message[tile(peer * CAP + k, vectors), :] = value.astype(bf16)
        return carry

    lax.fori_loop(0, groups, send, 0, unroll=8)
    for copy in copies:
        copy.wait()


def pack_rounded(asked, arrays, vectors):
    node = arrays[0].shape[1]
    each = arrays[0].shape[0] // vectors - 2
    groups = lax.axis_size("curve")
    return pl.pallas_call(
        functools.partial(pack_rounded_kernel, each, vectors, groups),
        out_shape=[shaped((groups * CAP * vectors, node), bf16)] + [pltpu.HBM(arrays[0].shape, f32)] * CHUNKS,
        in_specs=[smem()] + [vmem()] * (2 * CHUNKS),
        out_specs=[vmem()] + [anywhere()] * CHUNKS,
        scratch_shapes=[pltpu.SemaphoreType.DMA((CHUNKS,))],
        compiler_params=params(10),
        name="pack_rounded",
    )(asked, *arrays)


def finish_kernel(shares, scale, state_in, drive_in, image_in, out, one, two, mix, state, drive, image, ready, sems):
    places = ((state_in, state), (drive_in, drive), (image_in, image), (ready, out))
    copies = [
        [pltpu.make_async_copy(source.at[v], place.at[v], sems.at[k, v]) for v in range(out.shape[0])]
        for k, (source, place) in enumerate(places)
    ]
    leaving = copies.pop()
    for v in range(out.shape[0]):
        for column in copies:
            column[v].start()
    shape = scale.shape
    vectors = shape[0]
    line = jnp.sum(shares[...], axis=0, keepdims=True)
    form, cross, energy = [as_column(line, shape, e * vectors) for e in range(3)]
    beta_zero = scale[...]
    unit = 1.0 - epsilon / (beta_zero * beta_zero)
    alpha_first = cross / beta_zero
    square = alpha_first * alpha_first
    beta_first = jnp.sqrt(jnp.maximum(energy - square * (2.0 - unit), 0.0) + epsilon)
    alpha_second = (form - 2.0 * alpha_first * energy + square * alpha_first) / (beta_first * beta_first)
    alpha_second = alpha_second - alpha_first * (1.0 - unit)
    term_one = jnp.ones(shape, f32)
    term_two = jnp.zeros(shape, f32)
    total_one, total_two = term_one, term_two
    for turn in range(1, TAYLOR):
        factor = time_step / (turn + 1.0)
        next_one = factor * (alpha_first * term_one + beta_first * term_two)
        next_two = factor * (beta_first * term_one + alpha_second * term_two)
        term_one, term_two = next_one, next_two
        total_one, total_two = total_one + next_one, total_two + next_two
    one[...] = time_step * total_one
    two[...] = time_step * beta_zero * total_two / beta_first
    mix[...] = alpha_first / beta_zero
    width = state.shape[0]
    for v in range(width):
        at = pl.ds(lax.axis_index("band") * width + v, 1)
        size = state.shape[1:]
        weight_one, weight_two, share = [jnp.broadcast_to(ref[at, :], size) for ref in (one, two, mix)]
        for column in copies:
            column[v].wait()
        ready[v] = state[v] + (weight_one * drive[v] + weight_two * (image[v] - share * drive[v]))
        leaving[v].start()
    for copy in leaving:
        copy.wait()


def finish(shares, scale, state, drive, image):
    return pl.pallas_call(
        finish_kernel,
        out_shape=shaped(state.shape, f32),
        in_specs=[vmem()] * 2 + [anywhere()] * 3,
        out_specs=anywhere(),
        scratch_shapes=[pltpu.VMEM(scale.shape, f32)] * 3
        + [pltpu.VMEM(state.shape, f32)] * 4
        + [pltpu.SemaphoreType.DMA((4, state.shape[0]))],
        compiler_params=params(10),
        name="finish",
    )(shares, scale, state, in_hbm(drive), in_hbm(image))


def swap(array, bit):
    size = lax.axis_size("band")
    return lax.ppermute(array, "band", [(k, k ^ bit) for k in range(size)])


def exchange(array):
    return lax.all_to_all(array, "curve", split_axis=0, concat_axis=0, tiled=True)


def band_sum(keep, give, vectors, drive=None):
    each = keep[0].shape[0] // vectors
    came = [swap(array, 1) for array in give]
    codes = [encode(one, two, vectors) for one, two in zip(keep, came)]
    across = []
    for code in codes:
        across.append(swap(code, 2))
    mine, others = [], []
    for c, (code, other) in enumerate(zip(codes, across)):
        mine.append(decode(code, other, vectors, each, drive and drive[c], mine[-1] if c else None))
        others.append(swap(mine[c], 1))
    return mine + others


def body(state, blocks, diag_blocks, block_cols):
    groups = lax.axis_size("curve")
    devices = groups * lax.axis_size("band")
    width, rows = state.shape[:2]
    vectors = width * lax.axis_size("band")
    blocks = in_hbm(blocks)
    diag_blocks = in_hbm(diag_blocks)
    state = in_hbm(state)
    rounded, pick, target, wanted, origin = plan(block_cols.reshape(1, rows), state)
    across = swap(rounded, 2)
    beside = swap(rounded, 1)
    asked = exchange(wanted)
    corner = swap(across, 1)
    parts = [rounded, beside, across, corner]
    field, own, split = spread(parts, origin, blocks)
    message = reply(asked, field, split, vectors)
    halo = exchange(message)
    local = operate_local(pick, target, field, state, blocks, diag_blocks)
    keep, give = settle(wanted, origin, asked, local, halo, own, rows)
    drive = band_sum(keep, give, vectors)
    arrived = exchange(own)
    halo = exchange(pack(asked, origin, drive, vectors))
    keep, give, scale = operate_second(pick, target, asked, drive, halo, arrived, blocks, diag_blocks)
    drive_own = select_own(drive, width, rows, vectors)
    image = band_sum(keep, give, vectors, drive)
    message, *left = pack_rounded(asked, image, vectors)
    halo = exchange(message)
    image = image[:CHUNKS] + left
    form, left, image_own = operate_third(
        pick, wanted, origin, image, own, blocks, diag_blocks, width, vectors
    )
    share = tail(form, left, halo, image[CHUNKS - 1], devices)
    shares = lax.all_to_all(share, ("curve", "band"), split_axis=0, concat_axis=0, tiled=True)
    return finish(shares, scale, state, drive_own, image_own)


def solution(mesh):
    return jax.shard_map(
        body,
        mesh=mesh,
        in_specs=(
            P("band", "curve", None),
            P("curve", "band", None, None),
            P(("curve", "band"), None, None),
            P("curve", "band"),
        ),
        out_specs=P("band", "curve", None),
        check_vma=False,
    )
```
